128 devices in a mesh: row: 8 (over y, core), col: 16 (over x, z).
Axes of the slice: x: 4, y: 4, z: 4, core: 2. Of those that a mesh axis runs over, the one named last changes fastest.
Arguments:
- tokens: bfloat16 [104, 320, 384], P('row', 'col')
- row_sizes: int32 [8], replicated, may hold values from 1 to 13, 88 in all
- col_sizes: int32 [16], replicated, may hold values from 1 to 20, 256 in all
- norm_gain: float32 [384], replicated, may hold values from 0.25 to 1.75
- query_weight: bfloat16 [384, 384], replicated
- key_weight: bfloat16 [384, 384], replicated
- value_weight: bfloat16 [384, 384], replicated, may hold values from -0.3125 to 0.3125
- out_weight: bfloat16 [384, 384], replicated, may hold values from -0.625 to 0.625
- cache_one: bfloat16 [2, 104, 320, 384], P(None, 'row', 'col'), may hold values from -6 to 6
- gain_one: float32 [384], replicated, may hold values from 0.25 to 1.75
- conv_one: bfloat16 [3, 3, 3, 384, 384], replicated, may hold values from -0.0625 to 0.0625
- cache_two: bfloat16 [2, 208, 640, 384], P(None, 'row', 'col'), may hold values from -6 to 6
- gain_two: float32 [384], replicated, may hold values from 0.25 to 1.75
- conv_two: bfloat16 [3, 3, 3, 384, 192], replicated, may hold values from -0.0625 to 0.0625
Outputs:
- decoded: bfloat16 [208, 640, 192], P('row', 'col')
The draws below stay inside these ranges and needn't reach their ends.
Inputs may be any that keep to these rules, and one draw needn't show every extreme that they name: `row_sizes`: positive tile heights that sum to 88; the tallest has exactly 13 rows. `col_sizes`: positive tile widths that sum to 256; the widest has exactly 20 columns.
All inputs are finite; a program needn't handle non-finite values.
Results may differ from the reference program's by a relative error of at most 0.0095.
Values may be sent and summed in bfloat16 or wider, within the bound.
No kernel may reach another device: no remote copies, remote signals or barrier semaphores. Data moves between devices by JAX's collectives and lax.ppermute only.
A program may use at most 320 MiB of HBM per device.

```python
import math
import jax
import jax.numpy as jnp
import numpy as np
from jax import lax

C = 384
C_OUT = 192
TILE_ROWS = 13
TILE_COLS = 20
LAT_ROWS = 88
LAT_COLS = 256
PAD_ROWS = 104
PAD_COLS = 320
N_ROW = 8
N_COL = 16


def draw_tokens(key, part):
    key_base, key_pix, key_chan = jax.random.split(key, 3)
    shape = (PAD_ROWS, PAD_COLS, C)
    base = jax.random.normal(key_base, shape, jnp.float32)
    pixel_scale = jnp.exp(jax.random.uniform(key_pix, (PAD_ROWS, PAD_COLS, 1), jnp.float32, -1.15, 1.15))
    chan_scale = jnp.exp(jax.random.uniform(key_chan, (C,), jnp.float32, -1.15, 1.15))
    field = base * pixel_scale * chan_scale
    return field.astype(jnp.bfloat16)


def drawn_matrix(key, factor):
    return jax.random.normal(key, (C, C), jnp.float32) * (factor / jnp.sqrt(float(C)))


def draw_query_weight(key, part):
    return drawn_matrix(jax.random.fold_in(key, 11), 4.0).astype(jnp.bfloat16)


def draw_key_weight(key, part):
    return drawn_matrix(jax.random.fold_in(key, 23), 1.0).astype(jnp.bfloat16)


def steps_of(rng, shape, cuts, low, high):
    def one(axis_at, parts):
        steps = jax.random.uniform(jax.random.fold_in(jax.random.fold_in(rng, 6), axis_at), (parts,), jnp.float32, low / len(cuts), high / len(cuts))
        return jnp.repeat(jnp.exp(steps), shape[axis_at] // parts).reshape((-1,) + (1,) * (len(shape) - axis_at - 1))

    loudness = one(*cuts[0])
    for cut in cuts[1:]:
        loudness = loudness * one(*cut)
    return loudness


def length_profile(number_of, total, reach, slope):
    portions = [(1 << 20) // math.isqrt(rank ** slope) + 1 for rank in range(2, number_of + 1)]
    spare, holding = total - reach - (number_of - 1), [1] * (number_of - 1)
    while spare > 0:
        candidates = [i for i in range(number_of - 1) if holding[i] < reach]
        pool, budget = sum([portions[i] for i in candidates]), spare
        for i in candidates:
            extra = min(reach - holding[i], max(1, budget * portions[i] // pool), spare)
            holding[i] = holding[i] + extra
            spare = spare - extra
    return np.array([reach] + holding)


def ragged(own_key, number_of, total, reach, slope):
    if number_of == 2:
        one = jax.random.randint(own_key, (), max(1, total - reach), min(reach, total - 1) + 1)
        return jnp.stack([one, total - one])
    tallies = jnp.asarray(length_profile(number_of, total, reach, slope), jnp.int32)
    pairs = (number_of - 1) // 2
    donor, sink = tallies[1:1 + 2 * pairs:2], tallies[2:2 + 2 * pairs:2]
    room = jnp.minimum(donor - 1, reach - sink)
    shifted = jax.random.randint(jax.random.fold_in(own_key, 1), (pairs,), 0, 1 << 20) % (room + 1)
    tallies = tallies.at[1:1 + 2 * pairs:2].set(donor - shifted).at[2:2 + 2 * pairs:2].set(sink + shifted)
    return tallies[jax.random.permutation(jax.random.fold_in(own_key, 2), number_of)]


def scatter_about(rng, extent, scale, most, shards=(), kind=jnp.bfloat16):
    level = steps_of(rng, extent, shards, -0.22, 0.18) if shards else 1.0
    drawn = jax.random.normal(rng, extent, jnp.float32) * scale * level
    return jnp.minimum(jnp.maximum(drawn, -most), most).astype(kind)


def setup_inputs(seed: int = 0) -> dict:
    splits = jax.random.split(jax.random.key(seed), 15)
    return {
        "tokens": draw_tokens(jax.random.fold_in(splits[14], 71), 0),
        "row_sizes": ragged(splits[1], N_ROW, LAT_ROWS, TILE_ROWS, 2).astype(jnp.int32),
        "col_sizes": ragged(splits[2], N_COL, LAT_COLS, TILE_COLS, 2).astype(jnp.int32),
        "norm_gain": jnp.clip(1.0 + 0.15 * jax.random.normal(splits[3], (C,), jnp.float32), 0.25, 1.75),
        "query_weight": draw_query_weight(jax.random.fold_in(splits[14], 71), 0),
        "key_weight": draw_key_weight(jax.random.fold_in(splits[14], 71), 0),
        "value_weight": scatter_about(splits[6], (C, C), C ** -0.5, 0.3125),
        "out_weight": scatter_about(splits[7], (C, C), (C // 4) ** -0.5, 0.625),
        "cache_one": scatter_about(splits[8], (2, PAD_ROWS, PAD_COLS, C), 1.0, 6.0, ((1, 8), (2, 16))),
        "gain_one": jnp.clip(1.0 + 0.15 * jax.random.normal(splits[9], (C,), jnp.float32), 0.25, 1.75),
        "conv_one": scatter_about(splits[10], (3, 3, 3, C, C), (27 * C) ** -0.5, 0.0625),
        "cache_two": scatter_about(splits[11], (2, 2 * PAD_ROWS, 2 * PAD_COLS, C), 1.0, 6.0, ((1, 8), (2, 16))),
        "gain_two": jnp.clip(1.0 + 0.15 * jax.random.normal(splits[12], (C,), jnp.float32), 0.25, 1.75),
        "conv_two": scatter_about(splits[13], (3, 3, 3, C, C_OUT), (27 * C) ** -0.5, 0.0625),
    }


epsilon = 1e-06

def lookup(size_table, positions):
    marks = positions[:, None] == jnp.arange(size_table.shape[0], dtype=jnp.int32)[None, :]
    return lax.optimization_barrier(jnp.sum(jnp.where(marks, size_table[None, :], 0), axis=1)).astype(jnp.int32)

def placement(extent_list, tile_len, extent_sum):
    ends = jnp.cumsum(extent_list).astype(jnp.int32)
    starts = (ends - extent_list).astype(jnp.int32)
    position = jnp.arange(extent_sum, dtype=jnp.int32)
    owner_tile = lax.optimization_barrier(jnp.sum((position[:, None] >= ends[None, :]).astype(jnp.int32), axis=1))
    first_pos = lookup(starts, owner_tile)
    return (owner_tile * tile_len + position - first_pos).astype(jnp.int32)

def spread_back(extent_list, tile_len, padded_len, extent_sum):
    ends = jnp.cumsum(extent_list).astype(jnp.int32)
    starts = (ends - extent_list).astype(jnp.int32)
    slot_index = jnp.arange(padded_len, dtype=jnp.int32)
    owner_tile = slot_index // tile_len
    local_slot = slot_index - owner_tile * tile_len
    usable = local_slot < lookup(extent_list, owner_tile)
    target = jnp.clip(lookup(starts, owner_tile) + local_slot, 0, extent_sum - 1).astype(jnp.int32)
    return (target, usable)

def rms_scale(values_in, gain_vec):
    wide = values_in.astype(jnp.float32)
    return wide * lax.rsqrt(lax.optimization_barrier(jnp.mean(wide * wide, axis=-1, keepdims=True)) + epsilon) * gain_vec

def causal_conv(frames, kernel):
    result = lax.conv_general_dilated(frames[None].astype(jnp.float32), kernel.astype(jnp.float32), (1, 1, 1), ((0, 0), (1, 1), (1, 1)), dimension_numbers=('NDHWC', 'DHWIO', 'NDHWC'), precision=lax.Precision.HIGHEST)
    return result[0, 0]

def reference(tokens, row_sizes, col_sizes, norm_gain, query_weight, key_weight, value_weight, out_weight, cache_one, gain_one, conv_one, cache_two, gain_two, conv_two):
    channels = tokens.shape[-1]
    row_map = placement(row_sizes, TILE_ROWS, LAT_ROWS)
    col_map = placement(col_sizes, TILE_COLS, LAT_COLS)
    row_fine = placement(2 * row_sizes, 2 * TILE_ROWS, 2 * LAT_ROWS)
    col_fine = placement(2 * col_sizes, 2 * TILE_COLS, 2 * LAT_COLS)
    frame = jnp.take(jnp.take(tokens, row_map, axis=0), col_map, axis=1)
    prior_one = jnp.take(jnp.take(cache_one, row_map, axis=1), col_map, axis=2)
    prior_two = jnp.take(jnp.take(cache_two, row_fine, axis=1), col_fine, axis=2)
    count = LAT_ROWS * LAT_COLS
    normed = rms_scale(frame, norm_gain).astype(jnp.bfloat16).reshape(count, channels)
    queries = jnp.dot(normed, query_weight, preferred_element_type=jnp.float32).astype(jnp.bfloat16)
    key_rows = jnp.dot(normed, key_weight, preferred_element_type=jnp.float32).astype(jnp.bfloat16)
    value_rows = jnp.dot(normed, value_weight, preferred_element_type=jnp.float32).astype(jnp.bfloat16)
    scale = 1.0 / math.sqrt(channels)
    block = math.gcd(count, 1024)

    def one_block(query_block):
        scores = jnp.dot(query_block, key_rows.T, preferred_element_type=jnp.float32) * scale
        highest = lax.optimization_barrier(jnp.max(scores, axis=1, keepdims=True))
        expos = jnp.exp(scores - highest)
        denominator = lax.optimization_barrier(jnp.sum(expos, axis=1, keepdims=True))
        probs = expos.astype(jnp.bfloat16)
        return (jnp.dot(probs, value_rows, preferred_element_type=jnp.float32) / denominator).astype(jnp.bfloat16)
    attention = lax.map(one_block, queries.reshape(count // block, block, channels)).reshape(count, channels)
    projected = jnp.dot(attention, out_weight, preferred_element_type=jnp.float32)
    mixed = (frame.astype(jnp.float32) + projected.reshape(LAT_ROWS, LAT_COLS, channels)).astype(jnp.bfloat16)
    act_one = jax.nn.silu(rms_scale(mixed, gain_one)).astype(jnp.bfloat16)
    frames_one = jnp.concatenate([prior_one, act_one[None]], axis=0)
    y_one = causal_conv(frames_one, conv_one).astype(jnp.bfloat16)
    act_small = jax.nn.silu(rms_scale(y_one, gain_two)).astype(jnp.bfloat16)
    act_two = jnp.repeat(jnp.repeat(act_small, 2, axis=0), 2, axis=1)
    frames_two = jnp.concatenate([prior_two, act_two[None]], axis=0)
    y_two = causal_conv(frames_two, conv_two).astype(jnp.bfloat16)
    row_target, row_usable = spread_back(2 * row_sizes, 2 * TILE_ROWS, 2 * PAD_ROWS, 2 * LAT_ROWS)
    col_target, col_usable = spread_back(2 * col_sizes, 2 * TILE_COLS, 2 * PAD_COLS, 2 * LAT_COLS)
    placed = jnp.take(jnp.take(y_two, row_target, axis=0), col_target, axis=1)
    usable = (row_usable[:, None] & col_usable[None, :])[:, :, None]
    return jnp.where(usable, placed, jnp.zeros_like(placed)).astype(jnp.bfloat16)
```

```python
import math

import jax
import jax.numpy as jnp
from jax import lax
from jax.experimental import pallas as pl
from jax.experimental.pallas import tpu as pltpu
from jax.sharding import Mesh
from jax.sharding import PartitionSpec as P

epsilon = 1e-06
masked_score = -1e30
ROWS = ("y", "core")
COLS = ("x", "z")
HALO = 2
KEY_TILE = 272
KEY_CHUNK = 512
MAX_CHUNKS = 14
KEY_ROWS = MAX_CHUNKS * KEY_CHUNK + KEY_CHUNK
QUERY_BLOCK = 352
BLOCK_ROWS = 384
VMEM_BYTES = 60 * 1024 * 1024


def rms_scale(values_in, gain_vec):
    wide = values_in.astype(jnp.float32)
    return wide * lax.rsqrt(jnp.mean(wide * wide, axis=-1, keepdims=True) + epsilon) * gain_vec


def silu(v):
    return v / (1.0 + jnp.exp(-v))


def hop(value, axes, count, step):
    pairs = [(i, i + step) for i in range(count) if 0 <= i + step < count]
    return lax.ppermute(value, axes, pairs)


def pick(values, index, axis):
    return lax.dynamic_index_in_dim(values, jnp.maximum(index, 0), axis, keepdims=False)


def place(values, part, index, axis):
    return lax.dynamic_update_slice_in_dim(values, part, index, axis)


def put_rows(ref, start, value):
    for g in range(ref.shape[0]):
        ref[g, pl.ds(start, value.shape[0]), :] = value[:, g * 128 : (g + 1) * 128]


def get_rows(ref, start, count):
    return jnp.concatenate([ref[g, pl.ds(start, count), :] for g in range(ref.shape[0])], axis=1)


def query_kernel(starts_ref, strip_ref, gain_ref, qw_ref, kw_ref, query_ref, frame_ref, wide_ref, *, half, lat_rows, scale):
    front = HALO * half
    wide_ref[...] = jnp.zeros_like(wide_ref)
    tiles, tall, _ = strip_ref.shape
    for t in range(tiles):
        put_rows(wide_ref, front + starts_ref[t] * half, strip_ref[t].astype(jnp.float32))
    count = lat_rows * half
    frame_ref[...] = get_rows(wide_ref, starts_ref[tiles] * half, BLOCK_ROWS).astype(jnp.bfloat16)
    for i in range(count // QUERY_BLOCK):
        raw = get_rows(wide_ref, front + i * QUERY_BLOCK, QUERY_BLOCK)
        normed = rms_scale(raw, gain_ref[...]).astype(jnp.bfloat16)
        query = jnp.dot(normed, qw_ref[...], preferred_element_type=jnp.float32).astype(jnp.bfloat16)
        turned = lax.dot_general(query, kw_ref[...], (((1,), (1,)), ((), ())), preferred_element_type=jnp.float32)
        query_ref[i * QUERY_BLOCK : (i + 1) * QUERY_BLOCK, :] = (turned * scale).astype(jnp.bfloat16)


def attention_kernel(
    offsets_ref, chunks_ref, starts_ref, query_ref, tile_ref, bias_ref, out_ref,
    key_ref, score_ref, top_ref, sum_ref, acc_ref, wide_ref, stat_ref, *, half
):
    tiles = tile_ref.shape[0]

    def gather(t, carry):
        offset = pl.multiple_of(offsets_ref[t], 16)
        key_ref[pl.ds(offset, KEY_TILE), :] = tile_ref[t]
        return carry

    lax.fori_loop(0, tiles, gather, 0)
    tail = pl.multiple_of(offsets_ref[tiles], 16)
    key_ref[pl.ds(tail, KEY_CHUNK), :] = jnp.zeros((KEY_CHUNK, key_ref.shape[1]), jnp.bfloat16)
    front = HALO * half
    total = wide_ref.shape[1]
    count = query_ref.shape[0]
    wide_ref[:, 0:front, :] = jnp.zeros((3, front, 128), jnp.float32)
    wide_ref[:, front + count : total, :] = jnp.zeros((3, total - front - count, 128), jnp.float32)
    stat_ref[0:front, :] = jnp.zeros((front, 128), jnp.float32)
    stat_ref[front + count : total, :] = jnp.zeros((total - front - count, 128), jnp.float32)
    chunk_count = chunks_ref[0]
    blocks = count // QUERY_BLOCK
    lane_groups = KEY_CHUNK // 128

    def keys_at(j):
        return key_ref[pl.ds(pl.multiple_of(j * KEY_CHUNK, KEY_CHUNK), KEY_CHUNK), :]

    def score_step(i, j):
        slot = i % 2
        query = query_ref[i * QUERY_BLOCK : (i + 1) * QUERY_BLOCK, :]
        s = lax.dot_general(query, keys_at(j), (((1,), (1,)), ((), ())), preferred_element_type=jnp.float32)
        s = s + bias_ref[j]
        score_ref[slot, j] = s
        best = s[:, 0:128]
        for g in range(1, lane_groups):
            best = jnp.maximum(best, s[:, g * 128 : (g + 1) * 128])
        top_ref[slot] = jnp.maximum(top_ref[slot], best)

    def value_step(i, j):
        slot = i % 2
        p = jnp.exp2(score_ref[slot, j] - jnp.max(top_ref[slot], axis=1, keepdims=True))
        part = p[:, 0:128]
        for g in range(1, lane_groups):
            part = part + p[:, g * 128 : (g + 1) * 128]
        sum_ref[...] = sum_ref[...] + part
        acc_ref[...] = acc_ref[...] + jnp.dot(p.astype(jnp.bfloat16), keys_at(j), preferred_element_type=jnp.float32)

    for i in range(blocks + 1):
        if i < blocks:
            top_ref[i % 2] = jnp.full((QUERY_BLOCK, 128), masked_score, jnp.float32)
        if i > 0:
            last = (i - 1) % 2
            best = jnp.max(top_ref[last], axis=1, keepdims=True)
            top_ref[last] = jnp.broadcast_to(best, (QUERY_BLOCK, 128))
            sum_ref[...] = jnp.zeros_like(sum_ref)
            acc_ref[...] = jnp.zeros_like(acc_ref)

        def step(j, carry):
            if i < blocks:
                score_step(i, j)
            if i > 0:
                value_step(i - 1, j)
            return carry

        lax.fori_loop(0, chunk_count, step, 0)
        if i > 0:
            denominator = jnp.sum(sum_ref[...], axis=1, keepdims=True)
            lo = front + (i - 1) * QUERY_BLOCK
            put_rows(wide_ref, lo, acc_ref[...] / denominator)
            level = top_ref[(i - 1) % 2] + jnp.log2(jnp.broadcast_to(denominator, (QUERY_BLOCK, 128)))
            high = level.astype(jnp.bfloat16).astype(jnp.float32)
            mid = (level - high).astype(jnp.bfloat16).astype(jnp.float32)
            low = level - high - mid
            lane = lax.broadcasted_iota(jnp.int32, (QUERY_BLOCK, 128), 1)
            packed = jnp.where(lane == 0, high, jnp.where(lane == 1, mid, jnp.where(lane == 2, low, 0.0)))
            stat_ref[lo : lo + QUERY_BLOCK, :] = packed
    select = (
        lax.broadcasted_iota(jnp.int32, (16, 128), 0) == lax.broadcasted_iota(jnp.int32, (16, 128), 1)
    ).astype(jnp.bfloat16)
    for b in range(out_ref.shape[0]):
        offset = starts_ref[b] * half
        out_ref[b, 0 : BLOCK_ROWS - 16, :] = get_rows(wide_ref, offset, BLOCK_ROWS - 16).astype(jnp.bfloat16)
        levels = stat_ref[pl.ds(offset, BLOCK_ROWS), :].astype(jnp.bfloat16)
        out_ref[b, BLOCK_ROWS - 16 : BLOCK_ROWS, :] = lax.dot_general(
            select, levels, (((1,), (1,)), ((), ())), preferred_element_type=jnp.float32
        ).astype(jnp.bfloat16)


def merge_kernel(part_ref, frame_ref, mask_ref, vw_ref, ow_ref, gain_ref, act_ref):
    groups = part_ref.shape[0]
    ones = (lax.broadcasted_iota(jnp.int32, (16, 128), 0) < 3).astype(jnp.bfloat16)
    levels = [
        lax.dot_general(
            part_ref[g, BLOCK_ROWS - 16 : BLOCK_ROWS, :], ones, (((0,), (0,)), ((), ())), preferred_element_type=jnp.float32
        )
        for g in range(groups)
    ]
    best = levels[0]
    for g in range(1, groups):
        best = jnp.maximum(best, levels[g])
    weights = [jnp.exp2(level - best) for level in levels]
    total = weights[0]
    for g in range(1, groups):
        total = total + weights[g]
    merged = None
    for g in range(groups):
        share = weights[g] / total
        term = part_ref[g].astype(jnp.float32) * jnp.concatenate([share] * 3, axis=1)
        merged = term if merged is None else merged + term
    merged = merged.astype(jnp.bfloat16)
    attention = jnp.dot(merged, vw_ref[...], preferred_element_type=jnp.float32).astype(jnp.bfloat16)
    projected = jnp.dot(attention, ow_ref[...], preferred_element_type=jnp.float32)
    mixed = (frame_ref[...].astype(jnp.float32) + projected).astype(jnp.bfloat16)
    act = silu(rms_scale(mixed, gain_ref[...]))
    usable = jnp.concatenate([mask_ref[...]] * 3, axis=1) > 0.0
    act_ref[...] = jnp.where(usable, act, 0.0).astype(jnp.bfloat16)


def conv(frames, kernel):
    depth = frames.shape[0]
    total = None
    for t in range(depth):
        part = lax.conv_general_dilated(
            frames[t][None], kernel[t], (1, 1), "VALID",
            dimension_numbers=("NHWC", "HWIO", "NHWC"), preferred_element_type=jnp.float32,
        )[0]
        total = part if total is None else total + part
    return total


def local(
    tokens, row_sizes, col_sizes, norm_gain, query_weight, key_weight, value_weight, out_weight,
    cache_one, gain_one, conv_one, cache_two, gain_two, conv_two,
):
    tile_rows, tile_cols, channels = tokens.shape
    n_row = row_sizes.shape[0]
    n_col = col_sizes.shape[0]
    n_y = lax.axis_size("y")
    lat_rows = 88
    ext_cols = tile_cols + 2 * HALO
    half = ext_cols // 2
    core = lax.axis_index("core")
    y_at = lax.axis_index("y")
    row_at = y_at * lax.axis_size("core") + core
    col_at = lax.axis_index("x") * lax.axis_size("z") + lax.axis_index("z")
    row_starts = jnp.cumsum(row_sizes) - row_sizes
    col_starts = jnp.cumsum(col_sizes) - col_sizes
    row_padded = jnp.pad(row_sizes, (1, 1))
    col_padded = jnp.pad(col_sizes, (1, 1))
    tall = row_padded[row_at + 1]
    wide = col_padded[col_at + 1]

    normed = rms_scale(tokens, norm_gain).astype(jnp.bfloat16).reshape(tile_rows * tile_cols, channels)
    slot = jnp.arange(tile_rows * tile_cols, dtype=jnp.int32)
    slot_row = slot // tile_cols
    slot_col = slot - slot_row * tile_cols
    target = jnp.where((slot_row < tall) & (slot_col < wide), slot_row * wide + slot_col, -1)
    chosen = (jnp.arange(KEY_TILE, dtype=jnp.int32)[:, None] == target[None, :]).astype(jnp.bfloat16)
    own_keys = jnp.dot(chosen, normed, preferred_element_type=jnp.float32).astype(jnp.bfloat16)
    tiles = lax.all_gather(own_keys, ("core", "x", "z"), axis=0, tiled=False)
    pair_sizes = lax.dynamic_slice_in_dim(row_sizes, 2 * y_at, 2)
    counts = (pair_sizes[:, None] * col_sizes[None, :]).reshape(-1)
    padded = (counts + 15) // 16 * 16
    ends = jnp.cumsum(padded)
    offsets = jnp.concatenate([jnp.zeros((1,), jnp.int32), ends]).astype(jnp.int32)
    chunk_count = ((ends[-1:] + KEY_CHUNK - 1) // KEY_CHUNK).astype(jnp.int32)
    key_slot = jnp.arange(MAX_CHUNKS * KEY_CHUNK, dtype=jnp.int32)
    key_ok = jnp.any((key_slot[:, None] >= offsets[None, :-1]) & (key_slot[:, None] < (offsets[:-1] + counts)[None, :]), axis=1)
    bias = jnp.where(key_ok, 0.0, masked_score).astype(jnp.float32).reshape(MAX_CHUNKS, 1, KEY_CHUNK)

    coarse = jnp.concatenate([cache_one, tokens[None]], axis=0)
    last_two = pick(coarse, wide - 2, 2)
    last_one = pick(coarse, wide - 1, 2)
    first_one = coarse[:, :, 0]
    first_two = coarse[:, :, 1]
    fine_last = pick(cache_two, 2 * wide - 1, 2)
    fine_first = cache_two[:, :, 0]
    flat = lambda *parts: jnp.concatenate([p.reshape(-1, channels) for p in parts], axis=0)
    near = 3 * tile_rows
    from_left = hop(flat(last_two, last_one, fine_last), COLS, n_col, 1)
    from_right = hop(flat(first_one, first_two, fine_first), COLS, n_col, -1)
    from_left_far = hop(flat(last_one), COLS, n_col, 2)
    from_right_far = hop(flat(first_one), COLS, n_col, -2)
    left_two = jnp.where(col_padded[col_at] >= 2, from_left[:near], from_left_far)
    right_two = jnp.where(col_padded[jnp.minimum(col_at + 2, n_col + 1)] >= 2, from_right[near : 2 * near], from_right_far)
    line = lambda v: v.reshape(3, tile_rows, 1, channels)
    coarse_ext = jnp.concatenate(
        [line(left_two), line(from_left[near : 2 * near]), coarse, jnp.zeros((3, tile_rows, 2, channels), coarse.dtype)], axis=2
    )
    coarse_ext = place(coarse_ext, jnp.concatenate([line(from_right[:near]), line(right_two)], axis=2), wide + HALO, 2)
    fine_line = lambda v: v.reshape(2, 2 * tile_rows, 1, channels)
    fine_ext = jnp.concatenate([fine_line(from_left[2 * near :]), cache_two, fine_line(jnp.zeros_like(from_left[2 * near :]))], axis=2)
    fine_ext = place(fine_ext, fine_line(from_right[2 * near :]), 2 * wide + 1, 2)

    strip = coarse_ext[2]
    own_half = jnp.where(core == 0, strip[:, :half], strip[:, half:])
    other_half = jnp.where(core == 0, strip[:, half:], strip[:, :half])
    swap = [(0, 1), (1, 0)]
    sibling_half = lax.ppermute(other_half, "core", swap)
    two = jnp.where(core == 0, jnp.stack([own_half, sibling_half]), jnp.stack([sibling_half, own_half]))
    two = two.reshape(2, tile_rows * half, channels)
    tall_tile = (tile_rows * half + 15) // 16 * 16
    two = jnp.pad(two, ((0, 0), (0, tall_tile - tile_rows * half), (0, 0)))
    column = lax.all_gather(two.reshape(2 * tall_tile, channels), "y", axis=0, tiled=True).reshape(n_row, tall_tile, channels)
    chip_starts = row_starts[::2]
    tables = jnp.concatenate([row_starts, pick(row_starts, 2 * y_at, 0)[None]]).astype(jnp.int32)
    smem = pl.BlockSpec(memory_space=pltpu.SMEM)
    wide_rows = lat_rows * half + BLOCK_ROWS
    params = pltpu.CompilerParams(vmem_limit_bytes=VMEM_BYTES)
    vmem = lambda: pl.BlockSpec(memory_space=pltpu.VMEM)
    scale = math.log2(math.e) / math.sqrt(channels)

    def query_body(*refs):
        query_kernel(*refs, half=half, lat_rows=lat_rows, scale=scale)

    queries, frame = pl.pallas_call(
        query_body,
        in_specs=[smem, vmem(), vmem(), vmem(), vmem()],
        out_specs=[vmem(), vmem()],
        out_shape=[
            jax.ShapeDtypeStruct((lat_rows * half, channels), jnp.bfloat16),
            jax.ShapeDtypeStruct((BLOCK_ROWS, channels), jnp.bfloat16),
        ],
        scratch_shapes=[pltpu.VMEM((3, wide_rows, 128), jnp.float32)],
        compiler_params=params,
    )(tables, column, norm_gain[None], query_weight, key_weight)

    prior = coarse_ext[:2]
    row_last_two = pick(prior, tall - 2, 1)
    row_last_one = pick(prior, tall - 1, 1)
    near = 2 * ext_cols
    from_up = hop(flat(row_last_two, row_last_one, pick(fine_ext, 2 * tall - 1, 1)), ROWS, n_row, 1)
    from_down = hop(flat(prior[:, 0], prior[:, 1], fine_ext[:, 0]), ROWS, n_row, -1)
    from_up_far = hop(flat(row_last_one), ROWS, n_row, 2)
    from_down_far = hop(flat(prior[:, 0]), ROWS, n_row, -2)
    up_two = jnp.where(row_padded[row_at] >= 2, from_up[:near], from_up_far)
    down_two = jnp.where(row_padded[jnp.minimum(row_at + 2, n_row + 1)] >= 2, from_down[near : 2 * near], from_down_far)
    line = lambda v: v.reshape(2, 1, ext_cols, channels)
    prior_ext = jnp.concatenate(
        [line(up_two), line(from_up[near : 2 * near]), prior, jnp.zeros((2, 2, ext_cols, channels), prior.dtype)], axis=1
    )
    prior_ext = place(prior_ext, jnp.concatenate([line(from_down[:near]), line(down_two)], axis=1), tall + HALO, 1)
    fine_line = lambda v: v.reshape(2, 1, 2 * tile_cols + 2, channels)
    fine_full = jnp.concatenate([fine_line(from_up[2 * near :]), fine_ext, fine_line(jnp.zeros_like(from_up[2 * near :]))], axis=1)
    fine_full = place(fine_full, fine_line(from_down[2 * near :]), 2 * tall + 1, 1)
    prior_sum_one = conv(prior_ext, conv_one)
    prior_sum_two = conv(fine_full, conv_two)

    def attention_body(*refs):
        attention_kernel(*refs, half=half)

    parts = pl.pallas_call(
        attention_body,
        in_specs=[smem, smem, smem, vmem(), vmem(), vmem()],
        out_specs=vmem(),
        out_shape=jax.ShapeDtypeStruct((n_y, BLOCK_ROWS, channels), jnp.bfloat16),
        scratch_shapes=[
            pltpu.VMEM((KEY_ROWS, channels), jnp.bfloat16),
            pltpu.VMEM((2, MAX_CHUNKS, QUERY_BLOCK, KEY_CHUNK), jnp.float32),
            pltpu.VMEM((2, QUERY_BLOCK, 128), jnp.float32),
            pltpu.VMEM((QUERY_BLOCK, 128), jnp.float32),
            pltpu.VMEM((QUERY_BLOCK, channels), jnp.float32),
            pltpu.VMEM((3, wide_rows, 128), jnp.float32),
            pltpu.VMEM((wide_rows, 128), jnp.float32),
        ],
        compiler_params=params,
    )(offsets, chunk_count, chip_starts.astype(jnp.int32), queries, tiles.reshape(2 * n_col, KEY_TILE, channels), bias)
    parts = lax.all_to_all(parts, "y", 0, 0)

    spot = jnp.arange(BLOCK_ROWS, dtype=jnp.int32)
    spot_row = pick(row_starts, 2 * y_at, 0) - HALO + spot // half
    spot_col = pick(col_starts, col_at, 0) - HALO + spot % half + half * core
    inside = (spot_row >= 0) & (spot_row < lat_rows) & (spot_col >= 0) & (spot_col < jnp.sum(col_sizes))
    mask = jnp.broadcast_to(inside.astype(jnp.float32)[:, None], (BLOCK_ROWS, 128))
    act = pl.pallas_call(
        merge_kernel,
        in_specs=[vmem()] * 6 + [],
        out_specs=vmem(),
        out_shape=jax.ShapeDtypeStruct((BLOCK_ROWS, channels), jnp.bfloat16),
        compiler_params=params,
    )(parts, frame, mask, value_weight, out_weight, gain_one[None])
    act = act.reshape(BLOCK_ROWS // half, half, channels)
    ext_rows = tile_rows + 2 * HALO
    upper = act[:ext_rows]
    lower = lax.dynamic_slice_in_dim(act, row_sizes[2 * y_at], ext_rows, 0)
    mine = jnp.where(core == 0, upper, lower)
    theirs = lax.ppermute(jnp.where(core == 0, lower, upper), "core", swap)
    act_one = jnp.where(
        core == 0, jnp.concatenate([mine, theirs], axis=1), jnp.concatenate([theirs, mine], axis=1)
    )

    y_one = (conv(act_one[None], conv_one[2:]) + prior_sum_one).astype(jnp.bfloat16)
    act_small = silu(rms_scale(y_one, gain_two)).astype(jnp.bfloat16)
    near_row = jnp.arange(tile_rows + 2, dtype=jnp.int32) + pick(row_starts, row_at, 0) - 1
    near_col = jnp.arange(tile_cols + 2, dtype=jnp.int32) + pick(col_starts, col_at, 0) - 1
    inside = ((near_row >= 0) & (near_row < lat_rows))[:, None] & ((near_col >= 0) & (near_col < jnp.sum(col_sizes)))[None, :]
    act_small = jnp.where(inside[:, :, None], act_small, jnp.zeros_like(act_small))
    act_two = jnp.repeat(jnp.repeat(act_small, 2, axis=0), 2, axis=1)[1:-1, 1:-1]
    y_two = conv(act_two[None], conv_two[2:]) + prior_sum_two
    row_usable = jnp.arange(2 * tile_rows, dtype=jnp.int32) < 2 * tall
    col_usable = jnp.arange(2 * tile_cols, dtype=jnp.int32) < 2 * wide
    usable = (row_usable[:, None] & col_usable[None, :])[:, :, None]
    return jnp.where(usable, y_two, 0.0).astype(jnp.bfloat16)


def solution(mesh):
    grid = Mesh(mesh.devices.reshape(4, 2, 4, 4), ("y", "core", "x", "z"))
    placed = (
        P(ROWS, COLS, None), P(), P(), P(), P(), P(), P(), P(),
        P(None, ROWS, COLS, None), P(), P(), P(None, ROWS, COLS, None), P(), P(),
    )
    return jax.shard_map(local, mesh=grid, in_specs=placed, out_specs=P(ROWS, COLS, None), check_vma=False)
```

```python
import math

import jax
import jax.numpy as jnp
from jax import lax
from jax.experimental import pallas as pl
from jax.experimental.pallas import tpu as pltpu
from jax.sharding import Mesh
from jax.sharding import PartitionSpec as P

epsilon = 1e-06
masked_score = -1e30
ROWS = ("y", "core")
COLS = ("x", "z")
LAT_ROWS = 88
LAT_COLS = 256
TILE_ROWS = 13
TILE_COLS = 20
HALO = 2
EXT_ROWS = TILE_ROWS + 2 * HALO
EXT_COLS = TILE_COLS + 2 * HALO
HALF = EXT_COLS // 2
FRONT = HALO * HALF
FINE_ROWS = 2 * TILE_ROWS
FINE_COLS = 2 * TILE_COLS
FINE_PITCH = 48
KEY_TILE = 272
KEY_CHUNK = 512
MAX_CHUNKS = 14
KEY_ROWS = MAX_CHUNKS * KEY_CHUNK + KEY_CHUNK
QUERY_BLOCK = 352
BLOCK_ROWS = 384
HALF_ROWS = 208
WIDE_ROWS = LAT_ROWS * HALF + BLOCK_ROWS
TALL_TILE = 160
VMEM_BYTES = 60 * 1024 * 1024
NEAR = 48


def rms_scale(values_in, gain_vec):
    wide = values_in.astype(jnp.float32)
    return wide * lax.rsqrt(jnp.mean(wide * wide, axis=-1, keepdims=True) + epsilon) * gain_vec


def silu(v):
    return v / (1.0 + jnp.exp(-v))


def hop(value, axes, count, step):
    pairs = [(i, i + step) for i in range(count) if 0 <= i + step < count]
    return lax.ppermute(value, axes, pairs)


def put_rows(ref, start, value):
    for g in range(ref.shape[0]):
        ref[g, pl.ds(start, value.shape[0]), :] = value[:, g * 128 : (g + 1) * 128].astype(ref.dtype)


def get_rows(ref, start, count, stride=None):
    return jnp.concatenate([ref[g, pl.ds(start, count, stride), :] for g in range(ref.shape[0])], axis=1)


def put_strided(ref, start, stride, value):
    for g in range(ref.shape[0]):
        ref[g, pl.ds(start, value.shape[0], stride), :] = value[:, g * 128 : (g + 1) * 128].astype(ref.dtype)


def before(size_ref, index):
    total = 0
    for t in range(size_ref.shape[0]):
        total = total + jnp.where(t < index, size_ref[t], 0)
    return total


def size_at(size_ref, index):
    count = size_ref.shape[0]
    inside = (index >= 0) & (index < count)
    return jnp.where(inside, size_ref[jnp.clip(index, 0, count - 1)], 0)


def prepare_kernel(
    place_ref, row_ref, col_ref, token_ref, one_ref, two_ref, gain_ref,
    key_ref, right_ref, left_ref, right_far_ref, left_far_ref, pack_ref, coarse_ref, fine_ref,
):
    wide = col_ref[place_ref[1]]
    pack_ref[...] = jnp.zeros_like(pack_ref)
    for i in range(TILE_ROWS):
        raw = token_ref[i].astype(jnp.float32)
        put_rows(coarse_ref, (2 * TILE_ROWS + i) * 24, raw)
        put_rows(pack_ref, i * wide, rms_scale(raw, gain_ref[...]))
    key_ref[...] = get_rows(pack_ref, 0, KEY_TILE).astype(jnp.bfloat16)
    for f in range(2):
        for i in range(TILE_ROWS):
            put_rows(coarse_ref, (f * TILE_ROWS + i) * 24, one_ref[f, i].astype(jnp.float32))

        def copy_fine(i, carry):
            put_rows(fine_ref, pl.multiple_of((f * FINE_ROWS + i) * FINE_COLS, 8), two_ref[f, i].astype(jnp.float32))
            return carry

        lax.fori_loop(0, FINE_ROWS, copy_fine, 0)
    near = 3 * TILE_ROWS
    fine = 2 * FINE_ROWS
    for ref in (right_ref, left_ref, right_far_ref, left_far_ref):
        ref[...] = jnp.zeros_like(ref)
    last = get_rows(coarse_ref, wide - 1, near, 24).astype(jnp.bfloat16)
    first = get_rows(coarse_ref, 0, near, 24).astype(jnp.bfloat16)
    right_ref[0:near, :] = last
    right_ref[NEAR : NEAR + near, :] = get_rows(coarse_ref, jnp.maximum(wide - 2, 0), near, 24).astype(jnp.bfloat16)
    right_ref[2 * NEAR : 2 * NEAR + fine, :] = get_rows(fine_ref, 2 * wide - 1, fine, FINE_COLS).astype(jnp.bfloat16)
    left_ref[0:near, :] = first
    left_ref[NEAR : NEAR + near, :] = get_rows(coarse_ref, 1, near, 24).astype(jnp.bfloat16)
    left_ref[2 * NEAR : 2 * NEAR + fine, :] = get_rows(fine_ref, 0, fine, FINE_COLS).astype(jnp.bfloat16)
    right_far_ref[0:near, :] = last
    left_far_ref[0:near, :] = first


def columns_kernel(
    place_ref, row_ref, col_ref, token_ref, one_ref, two_ref, from_left_ref, from_right_ref, from_left_far_ref, from_right_far_ref,
    mine_ref, other_ref, prior_ref, fine_out_ref, down_ref, up_ref, down_far_ref, up_far_ref, coarse_ref, fine_ref, half_ref,
):
    core = place_ref[2]
    tall = row_ref[place_ref[0]]
    wide = col_ref[place_ref[1]]
    left_wide = size_at(col_ref, place_ref[1] - 1)
    right_wide = size_at(col_ref, place_ref[1] + 1)
    near = 3 * TILE_ROWS
    fine = 2 * FINE_ROWS
    blank = jnp.zeros((near, 384), jnp.float32)
    put_strided(coarse_ref, EXT_COLS - 2, EXT_COLS, blank)
    put_strided(coarse_ref, EXT_COLS - 1, EXT_COLS, blank)
    for f in range(3):
        for i in range(TILE_ROWS):
            row = one_ref[f, i] if f < 2 else token_ref[i]
            put_rows(coarse_ref, (f * TILE_ROWS + i) * EXT_COLS + HALO, row.astype(jnp.float32))
    left_two = jnp.where(left_wide >= 2, from_left_ref[NEAR : NEAR + near, :], from_left_far_ref[0:near, :])
    right_two = jnp.where(right_wide >= 2, from_right_ref[NEAR : NEAR + near, :], from_right_far_ref[0:near, :])
    put_strided(coarse_ref, 0, EXT_COLS, left_two.astype(jnp.float32))
    put_strided(coarse_ref, 1, EXT_COLS, from_left_ref[0:near, :].astype(jnp.float32))
    put_strided(coarse_ref, wide + 2, EXT_COLS, from_right_ref[0:near, :].astype(jnp.float32))
    put_strided(coarse_ref, wide + 3, EXT_COLS, right_two.astype(jnp.float32))
    for side, ref in ((core, mine_ref), (1 - core, other_ref)):
        for i in range(TILE_ROWS):
            put_rows(half_ref, i * HALF, get_rows(coarse_ref, (2 * TILE_ROWS + i) * EXT_COLS + side * HALF, HALF))
        half_ref[:, TILE_ROWS * HALF : TALL_TILE, :] = jnp.zeros((3, TALL_TILE - TILE_ROWS * HALF, 128), jnp.float32)
        ref[...] = get_rows(half_ref, 0, TALL_TILE).astype(jnp.bfloat16)
    for i in range(2 * TILE_ROWS):
        prior_ref[i] = get_rows(coarse_ref, i * EXT_COLS, EXT_COLS).astype(jnp.bfloat16)
    for c in range(FINE_COLS + 1, FINE_PITCH):
        put_strided(fine_ref, c, FINE_PITCH, jnp.zeros((fine, 384), jnp.float32))
    for f in range(2):

        def copy_fine(i, carry):
            put_rows(fine_ref, (f * FINE_ROWS + i) * FINE_PITCH + 1, two_ref[f, i].astype(jnp.float32))
            return carry

        lax.fori_loop(0, FINE_ROWS, copy_fine, 0)
    put_strided(fine_ref, 0, FINE_PITCH, from_left_ref[2 * NEAR : 2 * NEAR + fine, :].astype(jnp.float32))
    put_strided(fine_ref, 2 * wide + 1, FINE_PITCH, from_right_ref[2 * NEAR : 2 * NEAR + fine, :].astype(jnp.float32))

    def write_fine(i, carry):
        fine_out_ref[i] = get_rows(fine_ref, pl.multiple_of(i * FINE_PITCH, 8), FINE_PITCH).astype(jnp.bfloat16)
        return carry

    lax.fori_loop(0, fine, write_fine, 0)
    for f in range(2):
        base = f * TILE_ROWS
        last = prior_ref[base + tall - 1]
        down_ref[f] = last
        down_ref[2 + f] = prior_ref[base + jnp.maximum(tall - 2, 0)]
        down_far_ref[f] = last
        up_ref[f] = prior_ref[base]
        up_ref[2 + f] = prior_ref[base + 1]
        up_far_ref[f] = prior_ref[base]
        bottom = fine_out_ref[f * FINE_ROWS + 2 * tall - 1]
        top = fine_out_ref[f * FINE_ROWS]
        for h in range(2):
            down_ref[4 + 2 * f + h] = bottom[h * 24 : (h + 1) * 24]
            up_ref[4 + 2 * f + h] = top[h * 24 : (h + 1) * 24]


def prior_kernel(
    place_ref, row_ref, prior_ref, fine_ref, from_up_ref, from_down_ref, from_up_far_ref, from_down_far_ref, one_ref, two_ref,
    sum_one_ref, sum_two_ref, coarse_ref, wide_ref, part_ref,
):
    tall = row_ref[place_ref[0]]
    up_tall = size_at(row_ref, place_ref[0] - 1)
    down_tall = size_at(row_ref, place_ref[0] + 1)
    for f in range(2):
        coarse_ref[f, 0] = jnp.where(up_tall >= 2, from_up_ref[2 + f], from_up_far_ref[f])
        coarse_ref[f, 1] = from_up_ref[f]
        for i in range(TILE_ROWS):
            coarse_ref[f, HALO + i] = prior_ref[f * TILE_ROWS + i]
        for i in (TILE_ROWS + 2, TILE_ROWS + 3):
            coarse_ref[f, i] = jnp.zeros((EXT_COLS, 384), jnp.bfloat16)
        coarse_ref[f, tall + 2] = from_down_ref[f]
        coarse_ref[f, tall + 3] = jnp.where(down_tall >= 2, from_down_ref[2 + f], from_down_far_ref[f])
        wide_ref[f, 0] = jnp.concatenate([from_up_ref[4 + 2 * f], from_up_ref[5 + 2 * f]], axis=0)

        def copy_fine(i, carry):
            wide_ref[f, 1 + i] = fine_ref[f * FINE_ROWS + i]
            return carry

        lax.fori_loop(0, FINE_ROWS, copy_fine, 0)
        wide_ref[f, FINE_ROWS + 1] = jnp.zeros((FINE_PITCH, 384), jnp.bfloat16)
        wide_ref[f, 2 * tall + 1] = jnp.concatenate([from_down_ref[4 + 2 * f], from_down_ref[5 + 2 * f]], axis=0)
    rows = TILE_ROWS + 2
    left = jnp.concatenate(
        [coarse_ref[f, a : a + rows].reshape(rows * EXT_COLS, 384) for f in range(2) for a in range(3)], axis=1
    )
    sum_one_ref[...] = shifted_sum(left, lambda b: jnp.concatenate([one_ref[f, a, b] for f in range(2) for a in range(3)], axis=0), part_ref, 3)
    step = 13
    for r in range(0, FINE_ROWS, step):
        left = jnp.concatenate(
            [wide_ref[f, r + a : r + a + step].reshape(step * FINE_PITCH, 384) for f in range(2) for a in range(3)], axis=1
        )
        sum_two_ref[r * FINE_PITCH : (r + step) * FINE_PITCH, :] = shifted_sum(
            left, lambda b: jnp.concatenate([two_ref[f, a, b] for f in range(2) for a in range(3)], axis=0), part_ref, 2
        )[:, 0:192]


def shifted_sum(left, weight_of, part_ref, groups):
    count = left.shape[0]
    total = jnp.dot(left, weight_of(0), preferred_element_type=jnp.float32)
    for b in (1, 2):
        product = jnp.dot(left, weight_of(b), preferred_element_type=jnp.float32)
        width = product.shape[1]
        for g in range(groups):
            hi = min((g + 1) * 128, width)
            part_ref[g, 0:count, 0 : hi - g * 128] = product[:, g * 128 : hi]
        moved = jnp.concatenate([part_ref[g, b : b + count, :] for g in range(groups)], axis=1)
        total = total + moved[:, 0:width]
    return total


def query_kernel(
    place_ref, row_ref, own_ref, one_ref, two_ref, three_ref, gain_ref, qw_ref, kw_ref, query_ref, frame_ref, wide_ref, *, scale
):
    y_at = place_ref[0] // 2
    wide_ref[...] = jnp.zeros_like(wide_ref)
    slot = lax.broadcasted_iota(jnp.int32, (TALL_TILE, 128), 0)
    for k, ref in enumerate((own_ref, one_ref, two_ref, three_ref)):
        source = jnp.bitwise_and(y_at - k, 3)
        for t in range(2):
            start = FRONT + before(row_ref, 2 * source + t) * HALF
            usable = slot < row_ref[2 * source + t] * HALF
            part = ref[t].astype(jnp.float32)
            for g in range(3):
                held = wide_ref[g, pl.ds(start, TALL_TILE), :]
                wide_ref[g, pl.ds(start, TALL_TILE), :] = jnp.where(usable, part[:, g * 128 : (g + 1) * 128], held)
    count = LAT_ROWS * HALF
    frame_ref[...] = get_rows(wide_ref, before(row_ref, 2 * y_at) * HALF, BLOCK_ROWS).astype(jnp.bfloat16)
    for i in range(count // QUERY_BLOCK):
        raw = get_rows(wide_ref, FRONT + i * QUERY_BLOCK, QUERY_BLOCK)
        normed = rms_scale(raw, gain_ref[...]).astype(jnp.bfloat16)
        query = jnp.dot(normed, qw_ref[...], preferred_element_type=jnp.float32).astype(jnp.bfloat16)
        turned = lax.dot_general(query, kw_ref[...], (((1,), (1,)), ((), ())), preferred_element_type=jnp.float32)
        query_ref[i * QUERY_BLOCK : (i + 1) * QUERY_BLOCK, :] = (turned * scale).astype(jnp.bfloat16)


def attention_kernel(
    place_ref, row_ref, col_ref, query_ref, tile_ref, out_ref,
    key_ref, bias_ref, score_ref, top_ref, sum_ref, acc_ref, wide_ref, stat_ref,
):
    tiles = tile_ref.shape[0]
    cols = col_ref.shape[0]
    y_at = place_ref[0] // 2
    spot = lax.broadcasted_iota(jnp.int32, (16, KEY_CHUNK), 0) * KEY_CHUNK + lax.broadcasted_iota(jnp.int32, (16, KEY_CHUNK), 1)

    def gather(t, carry):
        offset, bias = carry
        offset = pl.multiple_of(offset, 16)
        key_ref[pl.ds(offset, KEY_TILE), :] = tile_ref[t]
        count = row_ref[2 * y_at + t // cols] * col_ref[t % cols]
        bias = jnp.where((spot >= offset) & (spot < offset + count), 0.0, bias)
        return offset + (count + 15) // 16 * 16, bias

    tail, bias = lax.fori_loop(0, tiles, gather, (jnp.int32(0), jnp.full((16, KEY_CHUNK), masked_score, jnp.float32)))
    tail = pl.multiple_of(tail, 16)
    key_ref[pl.ds(tail, KEY_CHUNK), :] = jnp.zeros((KEY_CHUNK, key_ref.shape[1]), jnp.bfloat16)
    for j in range(MAX_CHUNKS):
        bias_ref[j] = bias[j : j + 1, :]
    chunk_count = (tail + KEY_CHUNK - 1) // KEY_CHUNK
    total = wide_ref.shape[1]
    count = query_ref.shape[0]
    wide_ref[:, 0:FRONT, :] = jnp.zeros((3, FRONT, 128), jnp.float32)
    wide_ref[:, FRONT + count : total, :] = jnp.zeros((3, total - FRONT - count, 128), jnp.float32)
    stat_ref[0:FRONT, :] = jnp.zeros((FRONT, 128), jnp.float32)
    stat_ref[FRONT + count : total, :] = jnp.zeros((total - FRONT - count, 128), jnp.float32)
    blocks = count // QUERY_BLOCK
    lane_groups = KEY_CHUNK // 128

    def keys_at(j):
        return key_ref[pl.ds(pl.multiple_of(j * KEY_CHUNK, KEY_CHUNK), KEY_CHUNK), :]

    def score_step(i, j):
        slot = i % 2
        query = query_ref[i * QUERY_BLOCK : (i + 1) * QUERY_BLOCK, :]
        s = lax.dot_general(query, keys_at(j), (((1,), (1,)), ((), ())), preferred_element_type=jnp.float32)
        s = s + bias_ref[j]
        score_ref[slot, j] = s
        best = s[:, 0:128]
        for g in range(1, lane_groups):
            best = jnp.maximum(best, s[:, g * 128 : (g + 1) * 128])
        top_ref[slot] = jnp.maximum(top_ref[slot], best)

    def value_step(i, j):
        slot = i % 2
        top = top_ref[slot]
        p = jnp.exp2(score_ref[slot, j] - jnp.concatenate([top] * lane_groups, axis=1))
        part = p[:, 0:128]
        for g in range(1, lane_groups):
            part = part + p[:, g * 128 : (g + 1) * 128]
        sum_ref[...] = sum_ref[...] + part
        acc_ref[...] = acc_ref[...] + jnp.dot(p.astype(jnp.bfloat16), keys_at(j), preferred_element_type=jnp.float32)

    for i in range(blocks + 1):
        if i < blocks:
            top_ref[i % 2] = jnp.full((QUERY_BLOCK, 128), masked_score, jnp.float32)
        if i > 0:
            last = (i - 1) % 2
            best = jnp.max(top_ref[last], axis=1, keepdims=True)
            top_ref[last] = jnp.broadcast_to(best, (QUERY_BLOCK, 128))
            sum_ref[...] = jnp.zeros_like(sum_ref)
            acc_ref[...] = jnp.zeros_like(acc_ref)

        def step(j, carry):
            if i < blocks:
                score_step(i, j)
            if i > 0:
                value_step(i - 1, j)
            return carry

        lax.fori_loop(0, chunk_count, step, 0)
        if i > 0:
            denominator = jnp.sum(sum_ref[...], axis=1, keepdims=True)
            lo = FRONT + (i - 1) * QUERY_BLOCK
            put_rows(wide_ref, lo, acc_ref[...] / denominator)
            level = top_ref[(i - 1) % 2] + jnp.log2(jnp.broadcast_to(denominator, (QUERY_BLOCK, 128)))
            high = level.astype(jnp.bfloat16).astype(jnp.float32)
            mid = (level - high).astype(jnp.bfloat16).astype(jnp.float32)
            low = level - high - mid
            lane = lax.broadcasted_iota(jnp.int32, (QUERY_BLOCK, 128), 1)
            packed = jnp.where(lane == 0, high, jnp.where(lane == 1, mid, jnp.where(lane == 2, low, 0.0)))
            stat_ref[lo : lo + QUERY_BLOCK, :] = packed
    select = (
        lax.broadcasted_iota(jnp.int32, (16, 128), 0) == lax.broadcasted_iota(jnp.int32, (16, 128), 1)
    ).astype(jnp.bfloat16)
    for b in range(out_ref.shape[0]):
        offset = before(row_ref, 2 * b) * HALF
        out_ref[b, 0 : BLOCK_ROWS - 16, :] = get_rows(wide_ref, offset, BLOCK_ROWS - 16).astype(jnp.bfloat16)
        levels = stat_ref[pl.ds(offset, BLOCK_ROWS), :].astype(jnp.bfloat16)
        out_ref[b, BLOCK_ROWS - 16 : BLOCK_ROWS, :] = lax.dot_general(
            select, levels, (((1,), (1,)), ((), ())), preferred_element_type=jnp.float32
        ).astype(jnp.bfloat16)


def merge_kernel(
    place_ref, row_ref, col_ref, part_ref, frame_ref, vw_ref, ow_ref, gain_ref, mine_ref, other_ref, wide_ref
):
    groups = part_ref.shape[0]
    core = place_ref[2]
    y_at = place_ref[0] // 2
    ones = (lax.broadcasted_iota(jnp.int32, (16, 128), 0) < 3).astype(jnp.bfloat16)
    levels = [
        lax.dot_general(
            part_ref[g, BLOCK_ROWS - 16 : BLOCK_ROWS, :], ones, (((0,), (0,)), ((), ())), preferred_element_type=jnp.float32
        )
        for g in range(groups)
    ]
    best = levels[0]
    for g in range(1, groups):
        best = jnp.maximum(best, levels[g])
    weights = [jnp.exp2(level - best) for level in levels]
    total = weights[0]
    for g in range(1, groups):
        total = total + weights[g]
    merged = None
    for g in range(groups):
        share = weights[g] / total
        term = part_ref[g].astype(jnp.float32) * jnp.concatenate([share] * 3, axis=1)
        merged = term if merged is None else merged + term
    merged = merged.astype(jnp.bfloat16)
    attention = jnp.dot(merged, vw_ref[...], preferred_element_type=jnp.float32).astype(jnp.bfloat16)
    projected = jnp.dot(attention, ow_ref[...], preferred_element_type=jnp.float32)
    mixed = (frame_ref[...].astype(jnp.float32) + projected).astype(jnp.bfloat16)
    act = silu(rms_scale(mixed, gain_ref[...]))
    slot = lax.broadcasted_iota(jnp.int32, (BLOCK_ROWS, 128), 0)
    row = jnp.right_shift(slot * 43691, 19)
    at_row = before(row_ref, 2 * y_at) - HALO + row
    at_col = before(col_ref, place_ref[1]) - HALO + slot - row * HALF + core * HALF
    inside = (at_row >= 0) & (at_row < LAT_ROWS) & (at_col >= 0) & (at_col < LAT_COLS)
    for g in range(3):
        wide_ref[g] = jnp.where(inside, act[:, g * 128 : (g + 1) * 128], 0.0)
    upper = row_ref[2 * y_at] * HALF
    mine_ref[...] = get_rows(wide_ref, core * upper, HALF_ROWS).astype(jnp.bfloat16)
    other_ref[...] = get_rows(wide_ref, (1 - core) * upper, HALF_ROWS).astype(jnp.bfloat16)


def tail_kernel(
    place_ref, row_ref, col_ref, mine_ref, other_ref, sum_one_ref, sum_two_ref, one_ref, two_ref, gain_ref, out_ref,
    half_ref, act_ref, first_ref, up_ref, fine_ref, part_ref,
):
    core = place_ref[2]
    tall = row_ref[place_ref[0]]
    wide = col_ref[place_ref[1]]
    for side, ref in ((core, mine_ref), (1 - core, other_ref)):
        put_rows(half_ref, 0, ref[...].astype(jnp.float32))
        for i in range(EXT_ROWS):
            put_rows(act_ref, i * EXT_COLS + side * HALF, get_rows(half_ref, i * HALF, HALF))
    for i in range(EXT_ROWS):
        first_ref[i] = get_rows(act_ref, i * EXT_COLS, EXT_COLS).astype(jnp.bfloat16)
    rows = TILE_ROWS + 2
    left = jnp.concatenate([first_ref[a : a + rows].reshape(rows * EXT_COLS, 384) for a in range(3)], axis=1)
    total = shifted_sum(left, lambda b: jnp.concatenate([one_ref[0, a, b] for a in range(3)], axis=0), part_ref, 3)
    y_one = (total + sum_one_ref[...]).astype(jnp.bfloat16)
    act = silu(rms_scale(y_one, gain_ref[...])).astype(jnp.bfloat16).astype(jnp.float32)
    slot = lax.broadcasted_iota(jnp.int32, (rows * EXT_COLS, 128), 0)
    row = jnp.right_shift(slot * 43691, 20)
    at_row = before(row_ref, place_ref[0]) - 1 + row
    at_col = before(col_ref, place_ref[1]) - 1 + slot - row * EXT_COLS
    inside = (at_row >= 0) & (at_row < LAT_ROWS) & (at_col >= 0) & (at_col < LAT_COLS)
    for g in range(3):
        act_ref[g, 0 : rows * EXT_COLS, :] = jnp.where(inside, act[:, g * 128 : (g + 1) * 128], 0.0)
    for i in range(rows):
        small = get_rows(act_ref, i * EXT_COLS, EXT_COLS)
        put_strided(up_ref, 7, 2, small)
        put_strided(up_ref, 8, 2, small)
        fine = get_rows(up_ref, 8, FINE_PITCH).astype(jnp.bfloat16)
        for f in (2 * i - 1, 2 * i):
            if 0 <= f < FINE_ROWS + 2:
                fine_ref[f] = fine
    step = 13
    col = lax.broadcasted_iota(jnp.int32, (FINE_COLS, 192), 0)
    for r in range(0, FINE_ROWS, step):
        left = jnp.concatenate([fine_ref[r + a : r + a + step].reshape(step * FINE_PITCH, 384) for a in range(3)], axis=1)
        y_two = shifted_sum(left, lambda b: jnp.concatenate([two_ref[0, a, b] for a in range(3)], axis=0), part_ref, 2)[:, 0:192]
        y_two = y_two + sum_two_ref[r * FINE_PITCH : (r + step) * FINE_PITCH, :]
        for i in range(step):
            line = y_two[i * FINE_PITCH : i * FINE_PITCH + FINE_COLS, :]
            usable = (col < 2 * wide) & (r + i < 2 * tall)
            out_ref[r + i] = jnp.where(usable, line, 0.0).astype(jnp.bfloat16)


def call(body, inputs, outs, scratch, smem_count, name, flops=0):
    smem = pl.BlockSpec(memory_space=pltpu.SMEM)
    vmem = pl.BlockSpec(memory_space=pltpu.VMEM)
    moved = sum(math.prod(v.shape) * v.dtype.itemsize for v in list(inputs) + list(outs))
    return pl.pallas_call(
        body,
        in_specs=[smem] * smem_count + [vmem] * (len(inputs) - smem_count),
        out_specs=[vmem] * len(outs),
        out_shape=outs,
        scratch_shapes=scratch,
        compiler_params=pltpu.CompilerParams(vmem_limit_bytes=VMEM_BYTES),
        cost_estimate=pl.CostEstimate(flops=int(flops), transcendentals=0, bytes_accessed=int(moved)),
        name=name,
    )(*inputs)


def local(
    tokens, row_sizes, col_sizes, norm_gain, query_weight, key_weight, value_weight, out_weight,
    cache_one, gain_one, conv_one, cache_two, gain_two, conv_two,
):
    channels = tokens.shape[2]
    n_row = row_sizes.shape[0]
    n_col = col_sizes.shape[0]
    n_y = lax.axis_size("y")
    core = lax.axis_index("core")
    row_at = lax.axis_index("y") * lax.axis_size("core") + core
    col_at = lax.axis_index("x") * lax.axis_size("z") + lax.axis_index("z")
    place = jnp.stack([row_at, col_at, core]).astype(jnp.int32)
    shape = lambda *dims: jax.ShapeDtypeStruct(dims, jnp.bfloat16)
    wide_shape = lambda *dims: jax.ShapeDtypeStruct(dims, jnp.float32)
    scratch = lambda *dims: pltpu.VMEM(dims, jnp.float32)
    narrow = lambda *dims: pltpu.VMEM(dims, jnp.bfloat16)
    message = 160
    own_keys, to_right, to_left, to_right_far, to_left_far = call(
        prepare_kernel,
        [place, row_sizes, col_sizes, tokens, cache_one, cache_two, norm_gain[None]],
        [shape(KEY_TILE, channels), shape(message, channels), shape(message, channels), shape(NEAR, channels), shape(NEAR, channels)],
        [scratch(3, 304, 128), scratch(3, 3 * TILE_ROWS * 24, 128), scratch(3, 2 * FINE_ROWS * FINE_COLS, 128)],
        3, "prepare",
    )
    tiles = lax.all_gather(own_keys, ("core", "x", "z"), axis=0, tiled=False)
    from_left = hop(to_right, COLS, n_col, 1)
    from_right = hop(to_left, COLS, n_col, -1)
    from_left_far = hop(to_right_far, COLS, n_col, 2)
    from_right_far = hop(to_left_far, COLS, n_col, -2)
    mine, other, prior, fine, down, up, down_far, up_far = call(
        columns_kernel,
        [place, row_sizes, col_sizes, tokens, cache_one, cache_two, from_left, from_right, from_left_far, from_right_far],
        [
            shape(TALL_TILE, channels), shape(TALL_TILE, channels), shape(2 * TILE_ROWS, EXT_COLS, channels),
            shape(2 * FINE_ROWS, FINE_PITCH, channels), shape(8, EXT_COLS, channels), shape(8, EXT_COLS, channels),
            shape(2, EXT_COLS, channels), shape(2, EXT_COLS, channels),
        ],
        [scratch(3, 3 * TILE_ROWS * EXT_COLS, 128), scratch(3, 2 * FINE_ROWS * FINE_PITCH, 128), scratch(3, TALL_TILE, 128)],
        3, "columns",
    )
    swap = [(0, 1), (1, 0)]
    sibling = lax.ppermute(other, "core", swap)
    pair = jnp.where(core == 0, jnp.stack([mine, sibling]), jnp.stack([sibling, mine]))
    strips = [pair] + [lax.ppermute(pair, "y", [(i, (i + k) % n_y) for i in range(n_y)]) for k in range(1, n_y)]
    scale = math.log2(math.e) / math.sqrt(channels)

    def query_body(*refs):
        query_kernel(*refs, scale=scale)

    queries, frame = call(
        query_body,
        [place, row_sizes, *strips, norm_gain[None], query_weight, key_weight],
        [shape(LAT_ROWS * HALF, channels), shape(BLOCK_ROWS, channels)],
        [scratch(3, WIDE_ROWS, 128)],
        2, "queries", 4 * LAT_ROWS * HALF * channels * channels,
    )
    from_up = hop(down, ROWS, n_row, 1)
    from_down = hop(up, ROWS, n_row, -1)
    from_up_far = hop(down_far, ROWS, n_row, 2)
    from_down_far = hop(up_far, ROWS, n_row, -2)
    (parts,) = call(
        attention_kernel,
        [place, row_sizes, col_sizes, queries, tiles.reshape(2 * n_col, KEY_TILE, channels)],
        [shape(n_y, BLOCK_ROWS, channels)],
        [
            narrow(KEY_ROWS, channels), scratch(MAX_CHUNKS, 1, KEY_CHUNK), scratch(2, MAX_CHUNKS, QUERY_BLOCK, KEY_CHUNK),
            scratch(2, QUERY_BLOCK, 128), scratch(QUERY_BLOCK, 128), scratch(QUERY_BLOCK, channels),
            scratch(3, WIDE_ROWS, 128), scratch(WIDE_ROWS, 128),
        ],
        3, "attention", 4 * LAT_ROWS * HALF * channels * KEY_ROWS,
    )
    parts = lax.all_to_all(parts, "y", 0, 0)
    sum_one, sum_two = call(
        prior_kernel,
        [place, row_sizes, prior, fine, from_up, from_down, from_up_far, from_down_far, conv_one[:2], conv_two[:2]],
        [wide_shape((TILE_ROWS + 2) * EXT_COLS, channels), wide_shape(FINE_ROWS * FINE_PITCH, conv_two.shape[-1])],
        [narrow(2, EXT_ROWS, EXT_COLS, channels), narrow(2, FINE_ROWS + 2, FINE_PITCH, channels), scratch(3, 640, 128)],
        2, "prior", 2 * 18 * channels * (360 * 384 + 1248 * 192),
    )
    half_mine, half_other = call(
        merge_kernel,
        [place, row_sizes, col_sizes, parts, frame, value_weight, out_weight, gain_one[None]],
        [shape(HALF_ROWS, channels), shape(HALF_ROWS, channels)],
        [scratch(3, BLOCK_ROWS, 128)],
        3, "merge",
    )
    half_other = lax.ppermute(half_other, "core", swap)
    (decoded,) = call(
        tail_kernel,
        [place, row_sizes, col_sizes, half_mine, half_other, sum_one, sum_two, conv_one[2:], conv_two[2:], gain_two[None]],
        [shape(FINE_ROWS, FINE_COLS, conv_two.shape[-1])],
        [
            scratch(3, HALF_ROWS, 128), scratch(3, EXT_ROWS * EXT_COLS, 128), narrow(EXT_ROWS, EXT_COLS, channels),
            scratch(3, 64, 128), narrow(FINE_ROWS + 2, FINE_PITCH, channels), scratch(3, 640, 128),
        ],
        3, "tail",
    )
    return decoded


def solution(mesh):
    grid = Mesh(mesh.devices.reshape(4, 2, 4, 4), ("y", "core", "x", "z"))
    placed = (
        P(ROWS, COLS, None), P(), P(), P(), P(), P(), P(), P(),
        P(None, ROWS, COLS, None), P(), P(), P(None, ROWS, COLS, None), P(), P(),
    )
    return jax.shard_map(local, mesh=grid, in_specs=placed, out_specs=P(ROWS, COLS, None), check_vma=False)
```

```python
import math

import jax
import jax.numpy as jnp
from jax import lax
from jax.experimental import pallas as pl
from jax.experimental.pallas import tpu as pltpu
from jax.sharding import Mesh
from jax.sharding import PartitionSpec as P

epsilon = 1e-06
masked_score = -1e30
ROWS = ("y", "core")
COLS = ("x", "z")
LAT_ROWS = 88
LAT_COLS = 256
TILE_ROWS = 13
TILE_COLS = 20
HALO = 2
EXT_ROWS = TILE_ROWS + 2 * HALO
EXT_COLS = TILE_COLS + 2 * HALO
HALF = EXT_COLS // 2
FRONT = HALO * HALF
FINE_ROWS = 2 * TILE_ROWS
FINE_COLS = 2 * TILE_COLS
FINE_PITCH = 48
KEY_TILE = 272
KEY_CHUNK = 1024
MAX_CHUNKS = 7
KEY_ROWS = MAX_CHUNKS * KEY_CHUNK + KEY_CHUNK
QUERY_BLOCK = 1056
HALF_ROWS = 208
BLOCK_ROWS = HALF_ROWS + 16
WIDE_ROWS = LAT_ROWS * HALF + 384
FINE_STEP = 13
TALL_TILE = 160
VMEM_BYTES = 60 * 1024 * 1024
NEAR = 48


def rms_scale(values_in, gain_vec):
    wide = values_in.astype(jnp.float32)
    return wide * lax.rsqrt(jnp.mean(wide * wide, axis=-1, keepdims=True) + epsilon) * gain_vec


def silu(v):
    return v / (1.0 + jnp.exp(-v))


def hop(value, axes, count, step):
    pairs = [(i, i + step) for i in range(count) if 0 <= i + step < count]
    return lax.ppermute(value, axes, pairs)


def put_rows(ref, start, value):
    for g in range(ref.shape[0]):
        ref[g, pl.ds(start, value.shape[0]), :] = value[:, g * 128 : (g + 1) * 128].astype(ref.dtype)


def get_rows(ref, start, count, stride=None):
    return jnp.concatenate([ref[g, pl.ds(start, count, stride), :] for g in range(ref.shape[0])], axis=1)


def put_strided(ref, start, stride, value):
    for g in range(ref.shape[0]):
        ref[g, pl.ds(start, value.shape[0], stride), :] = value[:, g * 128 : (g + 1) * 128].astype(ref.dtype)


def before(size_ref, index):
    total = 0
    for t in range(size_ref.shape[0]):
        total = total + jnp.where(t < index, size_ref[t], 0)
    return total


def size_at(size_ref, index):
    count = size_ref.shape[0]
    inside = (index >= 0) & (index < count)
    return jnp.where(inside, size_ref[jnp.clip(index, 0, count - 1)], 0)


def keys_kernel(place_ref, row_ref, col_ref, token_ref, gain_ref, key_ref, pack_ref):
    wide = col_ref[place_ref[1]]
    pack_ref[...] = jnp.zeros_like(pack_ref)
    gain = gain_ref[...][None]
    for i in range(TILE_ROWS):
        put_rows(pack_ref, i * wide, rms_scale(token_ref[i].astype(jnp.float32), gain))
    key_ref[...] = get_rows(pack_ref, 0, KEY_TILE).astype(jnp.bfloat16)


def edges_kernel(
    place_ref, row_ref, col_ref, token_ref, one_ref, two_ref, right_ref, left_ref, right_far_ref, left_far_ref, coarse_ref, fine_ref
):
    wide = col_ref[place_ref[1]]
    for f in range(3):
        for i in range(TILE_ROWS):
            row = one_ref[f, i] if f < 2 else token_ref[i]
            put_rows(coarse_ref, (f * TILE_ROWS + i) * 24, row.astype(jnp.float32))
    for f in range(2):

        def copy_fine(i, carry):
            put_rows(fine_ref, pl.multiple_of((f * FINE_ROWS + i) * FINE_COLS, 8), two_ref[f, i].astype(jnp.float32))
            return carry

        lax.fori_loop(0, FINE_ROWS, copy_fine, 0)
    near = 3 * TILE_ROWS
    fine = 2 * FINE_ROWS
    for ref in (right_ref, left_ref, right_far_ref, left_far_ref):
        ref[...] = jnp.zeros_like(ref)
    last = get_rows(coarse_ref, wide - 1, near, 24).astype(jnp.bfloat16)
    first = get_rows(coarse_ref, 0, near, 24).astype(jnp.bfloat16)
    right_ref[0:near, :] = last
    right_ref[NEAR : NEAR + near, :] = get_rows(coarse_ref, jnp.maximum(wide - 2, 0), near, 24).astype(jnp.bfloat16)
    right_ref[2 * NEAR : 2 * NEAR + fine, :] = get_rows(fine_ref, 2 * wide - 1, fine, FINE_COLS).astype(jnp.bfloat16)
    left_ref[0:near, :] = first
    left_ref[NEAR : NEAR + near, :] = get_rows(coarse_ref, 1, near, 24).astype(jnp.bfloat16)
    left_ref[2 * NEAR : 2 * NEAR + fine, :] = get_rows(fine_ref, 0, fine, FINE_COLS).astype(jnp.bfloat16)
    right_far_ref[0:near, :] = last
    left_far_ref[0:near, :] = first


def columns_kernel(
    place_ref, row_ref, col_ref, token_ref, one_ref, two_ref, from_left_ref, from_right_ref, from_left_far_ref, from_right_far_ref,
    mine_ref, other_ref, prior_ref, fine_out_ref, down_ref, up_ref, down_far_ref, up_far_ref, coarse_ref, fine_ref, half_ref,
):
    core = place_ref[2]
    tall = row_ref[place_ref[0]]
    wide = col_ref[place_ref[1]]
    left_wide = size_at(col_ref, place_ref[1] - 1)
    right_wide = size_at(col_ref, place_ref[1] + 1)
    near = 3 * TILE_ROWS
    fine = 2 * FINE_ROWS
    blank = jnp.zeros((near, 384), jnp.float32)
    put_strided(coarse_ref, EXT_COLS - 2, EXT_COLS, blank)
    put_strided(coarse_ref, EXT_COLS - 1, EXT_COLS, blank)
    for f in range(3):
        for i in range(TILE_ROWS):
            row = one_ref[f, i] if f < 2 else token_ref[i]
            put_rows(coarse_ref, (f * TILE_ROWS + i) * EXT_COLS + HALO, row.astype(jnp.float32))
    left_two = jnp.where(left_wide >= 2, from_left_ref[NEAR : NEAR + near, :], from_left_far_ref[0:near, :])
    right_two = jnp.where(right_wide >= 2, from_right_ref[NEAR : NEAR + near, :], from_right_far_ref[0:near, :])
    put_strided(coarse_ref, 0, EXT_COLS, left_two.astype(jnp.float32))
    put_strided(coarse_ref, 1, EXT_COLS, from_left_ref[0:near, :].astype(jnp.float32))
    put_strided(coarse_ref, wide + 2, EXT_COLS, from_right_ref[0:near, :].astype(jnp.float32))
    put_strided(coarse_ref, wide + 3, EXT_COLS, right_two.astype(jnp.float32))
    for side, ref in ((core, mine_ref), (1 - core, other_ref)):
        for i in range(TILE_ROWS):
            put_rows(half_ref, i * HALF, get_rows(coarse_ref, (2 * TILE_ROWS + i) * EXT_COLS + side * HALF, HALF))
        half_ref[:, TILE_ROWS * HALF : TALL_TILE, :] = jnp.zeros((3, TALL_TILE - TILE_ROWS * HALF, 128), jnp.float32)
        ref[...] = get_rows(half_ref, 0, TALL_TILE).astype(jnp.bfloat16)
    for i in range(2 * TILE_ROWS):
        prior_ref[i] = get_rows(coarse_ref, i * EXT_COLS, EXT_COLS).astype(jnp.bfloat16)
    for c in range(FINE_COLS + 1, FINE_PITCH):
        put_strided(fine_ref, c, FINE_PITCH, jnp.zeros((fine, 384), jnp.float32))
    for f in range(2):

        def copy_fine(i, carry):
            put_rows(fine_ref, (f * FINE_ROWS + i) * FINE_PITCH + 1, two_ref[f, i].astype(jnp.float32))
            return carry

        lax.fori_loop(0, FINE_ROWS, copy_fine, 0)
    put_strided(fine_ref, 0, FINE_PITCH, from_left_ref[2 * NEAR : 2 * NEAR + fine, :].astype(jnp.float32))
    put_strided(fine_ref, 2 * wide + 1, FINE_PITCH, from_right_ref[2 * NEAR : 2 * NEAR + fine, :].astype(jnp.float32))

    def write_fine(i, carry):
        fine_out_ref[i] = get_rows(fine_ref, pl.multiple_of(i * FINE_PITCH, 8), FINE_PITCH).astype(jnp.bfloat16)
        return carry

    lax.fori_loop(0, fine, write_fine, 0)
    for f in range(2):
        base = f * TILE_ROWS
        last = prior_ref[base + tall - 1]
        down_ref[f] = last
        down_ref[2 + f] = prior_ref[base + jnp.maximum(tall - 2, 0)]
        down_far_ref[f] = last
        up_ref[f] = prior_ref[base]
        up_ref[2 + f] = prior_ref[base + 1]
        up_far_ref[f] = prior_ref[base]
        bottom = fine_out_ref[f * FINE_ROWS + 2 * tall - 1]
        top = fine_out_ref[f * FINE_ROWS]
        for h in range(2):
            down_ref[4 + 2 * f + h] = bottom[h * 24 : (h + 1) * 24]
            up_ref[4 + 2 * f + h] = top[h * 24 : (h + 1) * 24]


def prior_kernel(
    place_ref, row_ref, prior_ref, fine_ref, from_up_ref, from_down_ref, from_up_far_ref, from_down_far_ref, one_ref, two_ref,
    sum_one_ref, sum_two_ref, coarse_ref, wide_ref, part_ref, weight_one_ref, weight_two_ref, sem_ref,
):
    fetch_one = pltpu.make_async_copy(one_ref.at[pl.ds(0, 2)], weight_one_ref, sem_ref.at[0])
    fetch_two = pltpu.make_async_copy(two_ref.at[pl.ds(0, 2)], weight_two_ref, sem_ref.at[1])
    fetch_one.start()
    fetch_two.start()
    tall = row_ref[place_ref[0]]
    up_tall = size_at(row_ref, place_ref[0] - 1)
    down_tall = size_at(row_ref, place_ref[0] + 1)
    for f in range(2):
        coarse_ref[f, 0] = jnp.where(up_tall >= 2, from_up_ref[2 + f], from_up_far_ref[f])
        coarse_ref[f, 1] = from_up_ref[f]
        for i in range(TILE_ROWS):
            coarse_ref[f, HALO + i] = prior_ref[f * TILE_ROWS + i]
        for i in (TILE_ROWS + 2, TILE_ROWS + 3):
            coarse_ref[f, i] = jnp.zeros((EXT_COLS, 384), jnp.bfloat16)
        coarse_ref[f, tall + 2] = from_down_ref[f]
        coarse_ref[f, tall + 3] = jnp.where(down_tall >= 2, from_down_ref[2 + f], from_down_far_ref[f])
        wide_ref[f, 0] = jnp.concatenate([from_up_ref[4 + 2 * f], from_up_ref[5 + 2 * f]], axis=0)

        def copy_fine(i, carry):
            wide_ref[f, 1 + i] = fine_ref[f * FINE_ROWS + i]
            return carry

        lax.fori_loop(0, FINE_ROWS, copy_fine, 0)
        wide_ref[f, FINE_ROWS + 1] = jnp.zeros((FINE_PITCH, 384), jnp.bfloat16)
        wide_ref[f, 2 * tall + 1] = jnp.concatenate([from_down_ref[4 + 2 * f], from_down_ref[5 + 2 * f]], axis=0)
    fetch_one.wait()
    sum_one_ref[...] = coarse_conv(lambda f, a, n: coarse_ref[f, a : a + n], weight_one_ref, part_ref, 2)
    fetch_two.wait()
    for r in range(0, FINE_ROWS, FINE_STEP):
        sum_two_ref[r * FINE_PITCH : (r + FINE_STEP) * FINE_PITCH, :] = fine_conv(
            lambda f, a, n: wide_ref[f, r + a : r + a + n], weight_two_ref, part_ref, 2
        )


def coarse_conv(rows_of, weight_ref, part_ref, depth):
    rows = TILE_ROWS + 2
    taps = [(f, a) for f in range(depth) for a in range(3)]
    left = jnp.concatenate([rows_of(f, a, rows).reshape(rows * EXT_COLS, 384) for f, a in taps], axis=1)
    right = jnp.concatenate([jnp.concatenate([weight_ref[f, a, b] for b in range(3)], axis=1) for f, a in taps], axis=0)
    product = jnp.dot(left, right, preferred_element_type=jnp.float32)
    return shifted_sum([product[:, b * 384 : (b + 1) * 384] for b in range(3)], part_ref)


def fine_conv(rows_of, weight_ref, part_ref, depth):
    taps = [(f, a) for f in range(depth) for a in range(3)]
    left = jnp.concatenate([rows_of(f, a, FINE_STEP).reshape(FINE_STEP * FINE_PITCH, 384) for f, a in taps], axis=1)
    products = [
        lax.dot_general(
            left, jnp.concatenate([weight_ref[f, a, b] for f, a in taps], axis=1), (((1,), (1,)), ((), ())),
            preferred_element_type=jnp.float32,
        )
        for b in range(3)
    ]
    return shifted_sum(products, part_ref)


def shifted_sum(products, part_ref):
    total = products[0]
    count, width = total.shape
    groups = -(-width // 128)
    for b in (1, 2):
        for g in range(groups):
            hi = min((g + 1) * 128, width)
            part_ref[g, 0:count, 0 : hi - g * 128] = products[b][:, g * 128 : hi]
        moved = jnp.concatenate([part_ref[g, b : b + count, :] for g in range(groups)], axis=1)
        total = total + moved[:, 0:width]
    return total


def query_kernel(
    place_ref, row_ref, own_ref, one_ref, two_ref, three_ref, gain_ref, qw_ref, kw_ref, query_ref, frame_ref, frame_other_ref, wide_ref, *, scale
):
    y_at = place_ref[0] // 2
    wide_ref[...] = jnp.zeros_like(wide_ref)
    slot = lax.broadcasted_iota(jnp.int32, (TALL_TILE, 128), 0)
    for k, ref in enumerate((own_ref, one_ref, two_ref, three_ref)):
        source = jnp.bitwise_and(y_at - k, 3)
        for t in range(2):
            start = FRONT + before(row_ref, 2 * source + t) * HALF
            usable = slot < row_ref[2 * source + t] * HALF
            part = ref[t].astype(jnp.float32)
            for g in range(3):
                held = wide_ref[g, pl.ds(start, TALL_TILE), :]
                wide_ref[g, pl.ds(start, TALL_TILE), :] = jnp.where(usable, part[:, g * 128 : (g + 1) * 128], held)
    count = LAT_ROWS * HALF
    frame_ref[...] = get_rows(wide_ref, before(row_ref, place_ref[0]) * HALF, HALF_ROWS).astype(jnp.bfloat16)
    sibling = place_ref[0] + 1 - 2 * place_ref[2]
    frame_other_ref[...] = get_rows(wide_ref, before(row_ref, sibling) * HALF, HALF_ROWS).astype(jnp.bfloat16)
    step = count // 3
    for i in range(3):
        raw = get_rows(wide_ref, FRONT + i * step, step)
        normed = rms_scale(raw, gain_ref[...][None]).astype(jnp.bfloat16)
        query = jnp.dot(normed, qw_ref[...], preferred_element_type=jnp.float32).astype(jnp.bfloat16)
        turned = lax.dot_general(query, kw_ref[...], (((1,), (1,)), ((), ())), preferred_element_type=jnp.float32)
        query_ref[i * step : (i + 1) * step, :] = (turned * scale).astype(jnp.bfloat16)


def attention_kernel(
    place_ref, row_ref, col_ref, query_ref, tile_ref, out_ref,
    key_ref, bias_ref, score_ref, top_ref, sum_ref, acc_ref, wide_ref, stat_ref,
):
    tiles = tile_ref.shape[0]
    cols = col_ref.shape[0]
    y_at = place_ref[0] // 2
    spot = lax.broadcasted_iota(jnp.int32, (16, KEY_CHUNK), 0) * KEY_CHUNK + lax.broadcasted_iota(jnp.int32, (16, KEY_CHUNK), 1)

    def gather(t, carry):
        offset, bias = carry
        offset = pl.multiple_of(offset, 16)
        key_ref[pl.ds(offset, KEY_TILE), :] = tile_ref[t]
        count = row_ref[2 * y_at + t // cols] * col_ref[t % cols]
        bias = jnp.where((spot >= offset) & (spot < offset + count), 0.0, bias)
        return offset + (count + 15) // 16 * 16, bias

    tail, bias = lax.fori_loop(0, tiles, gather, (jnp.int32(0), jnp.full((16, KEY_CHUNK), masked_score, jnp.float32)))
    tail = pl.multiple_of(tail, 16)
    key_ref[pl.ds(tail, KEY_CHUNK), :] = jnp.zeros((KEY_CHUNK, key_ref.shape[1]), jnp.bfloat16)
    for j in range(MAX_CHUNKS):
        bias_ref[j] = bias[j : j + 1, :]
    chunk_count = (tail + KEY_CHUNK - 1) // KEY_CHUNK
    total = wide_ref.shape[1]
    count = query_ref.shape[0]
    wide_ref[:, 0:FRONT, :] = jnp.zeros((3, FRONT, 128), jnp.float32)
    wide_ref[:, FRONT + count : total, :] = jnp.zeros((3, total - FRONT - count, 128), jnp.float32)
    stat_ref[0:FRONT, :] = jnp.zeros((FRONT, 128), jnp.float32)
    stat_ref[FRONT + count : total, :] = jnp.zeros((total - FRONT - count, 128), jnp.float32)
    blocks = count // QUERY_BLOCK
    lane_groups = KEY_CHUNK // 128

    def keys_at(j):
        return key_ref[pl.ds(pl.multiple_of(j * KEY_CHUNK, KEY_CHUNK), KEY_CHUNK), :]

    def score_step(i, j):
        slot = 0
        query = query_ref[i * QUERY_BLOCK : (i + 1) * QUERY_BLOCK, :]
        s = lax.dot_general(query, keys_at(j), (((1,), (1,)), ((), ())), preferred_element_type=jnp.float32)
        s = s + bias_ref[j]
        score_ref[slot, j] = s
        best = s[:, 0:128]
        for g in range(1, lane_groups):
            best = jnp.maximum(best, s[:, g * 128 : (g + 1) * 128])
        top_ref[slot] = jnp.maximum(top_ref[slot], best)

    def value_step(i, j):
        slot = 0
        top = top_ref[slot]
        p = jnp.exp2(score_ref[slot, j] - jnp.concatenate([top] * lane_groups, axis=1))
        part = p[:, 0:128]
        for g in range(1, lane_groups):
            part = part + p[:, g * 128 : (g + 1) * 128]
        sum_ref[...] = sum_ref[...] + part
        acc_ref[...] = acc_ref[...] + jnp.dot(p.astype(jnp.bfloat16), keys_at(j), preferred_element_type=jnp.float32)

    for i in range(blocks + 1):
        if i < blocks:
            top_ref[0] = jnp.full((QUERY_BLOCK, 128), masked_score, jnp.float32)
        if i > 0:
            last = 0
            best = jnp.max(top_ref[last], axis=1, keepdims=True)
            top_ref[last] = jnp.broadcast_to(best, (QUERY_BLOCK, 128))
            sum_ref[...] = jnp.zeros_like(sum_ref)
            acc_ref[...] = jnp.zeros_like(acc_ref)

        def step(j, carry):
            if i < blocks:
                score_step(i, j)
            if i > 0:
                value_step(i - 1, j)
            return carry

        lax.fori_loop(0, chunk_count, step, 0)
        if i > 0:
            denominator = jnp.sum(sum_ref[...], axis=1, keepdims=True)
            lo = FRONT + (i - 1) * QUERY_BLOCK
            put_rows(wide_ref, lo, acc_ref[...] / denominator)
            level = top_ref[0] + jnp.log2(jnp.broadcast_to(denominator, (QUERY_BLOCK, 128)))
            high = level.astype(jnp.bfloat16).astype(jnp.float32)
            mid = (level - high).astype(jnp.bfloat16).astype(jnp.float32)
            low = level - high - mid
            lane = lax.broadcasted_iota(jnp.int32, (QUERY_BLOCK, 128), 1)
            packed = jnp.where(lane == 0, high, jnp.where(lane == 1, mid, jnp.where(lane == 2, low, 0.0)))
            stat_ref[lo : lo + QUERY_BLOCK, :] = packed
    select = (
        lax.broadcasted_iota(jnp.int32, (16, 128), 0) == lax.broadcasted_iota(jnp.int32, (16, 128), 1)
    ).astype(jnp.bfloat16)
    for b in range(out_ref.shape[0]):
        offset = before(row_ref, b) * HALF
        out_ref[b, 0:HALF_ROWS, :] = get_rows(wide_ref, offset, HALF_ROWS).astype(jnp.bfloat16)
        levels = stat_ref[pl.ds(offset, 384), :].astype(jnp.bfloat16)
        out_ref[b, HALF_ROWS:BLOCK_ROWS, :] = lax.dot_general(
            select, levels, (((1,), (1,)), ((), ())), preferred_element_type=jnp.float32
        ).astype(jnp.bfloat16)


def finish_kernel(
    place_ref, row_ref, col_ref, part_ref, mine_ref, other_ref, vw_ref, ow_ref, gain_one_ref, sum_one_ref, sum_two_ref, one_ref, two_ref,
    gain_two_ref, out_ref, act_ref, first_ref, up_ref, fine_ref, shift_ref, weight_one_ref, weight_two_ref, sem_ref,
):
    fetch_one = pltpu.make_async_copy(one_ref.at[pl.ds(2, 1)], weight_one_ref, sem_ref.at[0])
    fetch_two = pltpu.make_async_copy(two_ref.at[pl.ds(2, 1)], weight_two_ref, sem_ref.at[1])
    fetch_one.start()
    fetch_two.start()
    core = place_ref[2]
    tall = row_ref[place_ref[0]]
    wide = col_ref[place_ref[1]]
    ones = (lax.broadcasted_iota(jnp.int32, (16, 128), 0) < 3).astype(jnp.bfloat16)
    halves = []
    for side in range(2):
        sources = range(side, part_ref.shape[0], 2)
        levels = [
            lax.dot_general(
                part_ref[g, HALF_ROWS:BLOCK_ROWS, 0:256], ones, (((0,), (0,)), ((), ())), preferred_element_type=jnp.float32
            )[0:HALF_ROWS]
            for g in sources
        ]
        best = jnp.maximum(jnp.maximum(levels[0], levels[1]), jnp.maximum(levels[2], levels[3]))
        weights = [jnp.exp2(level - best) for level in levels]
        total = (weights[0] + weights[1]) + (weights[2] + weights[3])
        merged = None
        for weight, g in zip(weights, sources):
            share = weight / total
            term = part_ref[g, 0:HALF_ROWS, :].astype(jnp.float32) * jnp.concatenate([share] * 3, axis=1)
            merged = term if merged is None else merged + term
        halves.append(merged.astype(jnp.bfloat16))
    merged = jnp.concatenate(halves, axis=0)
    attention = jnp.dot(merged, vw_ref[...], preferred_element_type=jnp.float32).astype(jnp.bfloat16)
    projected = jnp.dot(attention, ow_ref[...], preferred_element_type=jnp.float32)
    mine = mine_ref[...].astype(jnp.float32)
    other = other_ref[...].astype(jnp.float32)
    frame = jnp.concatenate([jnp.where(core == 0, mine, other), jnp.where(core == 0, other, mine)], axis=0)
    mixed = (frame + projected).astype(jnp.bfloat16)
    put_rows(shift_ref, 0, silu(rms_scale(mixed, gain_one_ref[...][None])))
    row_start = before(row_ref, place_ref[0])
    col_start = before(col_ref, place_ref[1])
    for side in range(2):
        for i in range(EXT_ROWS):
            put_rows(act_ref, i * EXT_COLS + side * HALF, get_rows(shift_ref, side * HALF_ROWS + i * HALF, HALF))
    at_col = col_start - HALO + lax.broadcasted_iota(jnp.int32, (EXT_COLS, 384), 0)
    col_inside = (at_col >= 0) & (at_col < LAT_COLS)
    for i in range(EXT_ROWS):
        at_row = row_start - HALO + i
        inside = col_inside & (at_row >= 0) & (at_row < LAT_ROWS)
        first_ref[i] = jnp.where(inside, get_rows(act_ref, i * EXT_COLS, EXT_COLS), 0.0).astype(jnp.bfloat16)
    rows = TILE_ROWS + 2
    fetch_one.wait()
    total = coarse_conv(lambda f, a, n: first_ref[a : a + n], weight_one_ref, shift_ref, 1)
    y_one = (total + sum_one_ref[...]).astype(jnp.bfloat16)
    act = silu(rms_scale(y_one, gain_two_ref[...][None])).astype(jnp.bfloat16).astype(jnp.float32)
    put_rows(act_ref, 0, act)
    at_col = col_start - 1 + lax.broadcasted_iota(jnp.int32, (EXT_COLS, 384), 0)
    col_inside = (at_col >= 0) & (at_col < LAT_COLS)
    for i in range(rows):
        at_row = row_start - 1 + i
        inside = col_inside & (at_row >= 0) & (at_row < LAT_ROWS)
        small = jnp.where(inside, get_rows(act_ref, i * EXT_COLS, EXT_COLS), 0.0)
        put_strided(up_ref, 7, 2, small)
        put_strided(up_ref, 8, 2, small)
        fine = get_rows(up_ref, 8, FINE_PITCH).astype(jnp.bfloat16)
        for f in (2 * i - 1, 2 * i):
            if 0 <= f < FINE_ROWS + 2:
                fine_ref[f] = fine
    col = lax.broadcasted_iota(jnp.int32, (FINE_COLS, 192), 0)
    fetch_two.wait()
    for r in range(0, FINE_ROWS, FINE_STEP):
        y_two = fine_conv(lambda f, a, n: fine_ref[r + a : r + a + n], weight_two_ref, shift_ref, 1)
        y_two = y_two + sum_two_ref[r * FINE_PITCH : (r + FINE_STEP) * FINE_PITCH, :]
        for i in range(FINE_STEP):
            line = y_two[i * FINE_PITCH : i * FINE_PITCH + FINE_COLS, :]
            usable = (col < 2 * wide) & (r + i < 2 * tall)
            out_ref[r + i] = jnp.where(usable, line, 0.0).astype(jnp.bfloat16)


def call(body, inputs, outs, scratch, smem_count, name, flops=0, far=()):
    smem = pl.BlockSpec(memory_space=pltpu.SMEM)
    vmem = pl.BlockSpec(memory_space=pltpu.VMEM)
    moved = sum(math.prod(v.shape) * v.dtype.itemsize for v in list(inputs) + list(outs))
    return pl.pallas_call(
        body,
        in_specs=[
            smem if i < smem_count else pl.BlockSpec(memory_space=pl.ANY) if i in far else vmem for i in range(len(inputs))
        ],
        out_specs=[vmem] * len(outs),
        out_shape=outs,
        scratch_shapes=scratch,
        compiler_params=pltpu.CompilerParams(vmem_limit_bytes=VMEM_BYTES),
        cost_estimate=pl.CostEstimate(flops=int(flops), transcendentals=0, bytes_accessed=int(moved)),
        name=name,
    )(*inputs)


def attend(place, row_sizes, col_sizes, queries, tiles):
    channels = queries.shape[1]
    scratch = lambda *dims: pltpu.VMEM(dims, jnp.float32)
    (parts,) = call(
        attention_kernel,
        [place, row_sizes, col_sizes, queries, tiles],
        [jax.ShapeDtypeStruct((8, BLOCK_ROWS, channels), jnp.bfloat16)],
        [
            pltpu.VMEM((KEY_ROWS, channels), jnp.bfloat16), scratch(MAX_CHUNKS, 1, KEY_CHUNK),
            scratch(1, MAX_CHUNKS, QUERY_BLOCK, KEY_CHUNK),
            scratch(1, QUERY_BLOCK, 128), scratch(QUERY_BLOCK, 128), scratch(QUERY_BLOCK, channels),
            scratch(3, WIDE_ROWS, 128), scratch(WIDE_ROWS, 128),
        ],
        3, "attention", 4 * LAT_ROWS * HALF * channels * KEY_ROWS,
    )
    return parts


def local(
    tokens, row_sizes, col_sizes, norm_gain, query_weight, key_weight, value_weight, out_weight,
    cache_one, gain_one, conv_one, cache_two, gain_two, conv_two,
):
    channels = tokens.shape[2]
    n_row = row_sizes.shape[0]
    n_col = col_sizes.shape[0]
    n_y = lax.axis_size("y")
    core = lax.axis_index("core")
    row_at = lax.axis_index("y") * lax.axis_size("core") + core
    col_at = lax.axis_index("x") * lax.axis_size("z") + lax.axis_index("z")
    place = jnp.stack([row_at, col_at, core]).astype(jnp.int32)
    shape = lambda *dims: jax.ShapeDtypeStruct(dims, jnp.bfloat16)
    wide_shape = lambda *dims: jax.ShapeDtypeStruct(dims, jnp.float32)
    scratch = lambda *dims: pltpu.VMEM(dims, jnp.float32)
    narrow = lambda *dims: pltpu.VMEM(dims, jnp.bfloat16)
    message = 160
    place_args = [place, row_sizes, col_sizes]
    (own_keys,) = call(
        keys_kernel, [*place_args, tokens, norm_gain], [shape(KEY_TILE, channels)], [scratch(3, 304, 128)], 3, "keys"
    )
    tiles = lax.all_gather(own_keys, ("core", "x", "z"), axis=0, tiled=False)
    to_right, to_left, to_right_far, to_left_far = call(
        edges_kernel,
        [*place_args, tokens, cache_one, cache_two],
        [shape(message, channels), shape(message, channels), shape(NEAR, channels), shape(NEAR, channels)],
        [scratch(3, 3 * TILE_ROWS * 24, 128), scratch(3, 2 * FINE_ROWS * FINE_COLS, 128)],
        3, "edges",
    )
    from_left = hop(to_right, COLS, n_col, 1)
    from_right = hop(to_left, COLS, n_col, -1)
    from_left_far = hop(to_right_far, COLS, n_col, 2)
    from_right_far = hop(to_left_far, COLS, n_col, -2)
    mine, other, prior, fine, down, up, down_far, up_far = call(
        columns_kernel,
        [*place_args, tokens, cache_one, cache_two, from_left, from_right, from_left_far, from_right_far],
        [
            shape(TALL_TILE, channels), shape(TALL_TILE, channels), shape(2 * TILE_ROWS, EXT_COLS, channels),
            shape(2 * FINE_ROWS, FINE_PITCH, channels), shape(8, EXT_COLS, channels), shape(8, EXT_COLS, channels),
            shape(2, EXT_COLS, channels), shape(2, EXT_COLS, channels),
        ],
        [scratch(3, 3 * TILE_ROWS * EXT_COLS, 128), scratch(3, 2 * FINE_ROWS * FINE_PITCH, 128), scratch(3, TALL_TILE, 128)],
        3, "columns",
    )
    swap = [(0, 1), (1, 0)]
    sibling = lax.ppermute(other, "core", swap)
    pair = jnp.where(core == 0, jnp.stack([mine, sibling]), jnp.stack([sibling, mine]))
    strips = [pair] + [lax.ppermute(pair, "y", [(i, (i + k) % n_y) for i in range(n_y)]) for k in range(1, n_y)]
    around = [hop(down, ROWS, n_row, 1), hop(up, ROWS, n_row, -1), hop(down_far, ROWS, n_row, 2), hop(up_far, ROWS, n_row, -2)]
    strips, around = lax.optimization_barrier((strips, around))
    scale = math.log2(math.e) / math.sqrt(channels)

    def query_body(*refs):
        query_kernel(*refs, scale=scale)

    queries, frame, frame_other = call(
        query_body,
        [place, row_sizes, *strips, norm_gain, query_weight, key_weight],
        [shape(LAT_ROWS * HALF, channels), shape(HALF_ROWS, channels), shape(HALF_ROWS, channels)],
        [scratch(3, WIDE_ROWS, 128)],
        2, "queries", 4 * LAT_ROWS * HALF * channels * channels,
    )
    frame_other = lax.ppermute(frame_other, "core", swap)
    parts = attend(place, row_sizes, col_sizes, queries, tiles.reshape(2 * n_col, KEY_TILE, channels))
    parts = lax.all_to_all(parts, ROWS, 0, 0)
    conv_two = jnp.swapaxes(conv_two, 3, 4)
    channels_out = conv_two.shape[3]
    sum_one, sum_two = call(
        prior_kernel,
        [place, row_sizes, prior, fine, *around, conv_one, conv_two],
        [wide_shape((TILE_ROWS + 2) * EXT_COLS, channels), wide_shape(FINE_ROWS * FINE_PITCH, channels_out)],
        [
            narrow(2, EXT_ROWS, EXT_COLS, channels), narrow(2, FINE_ROWS + 2, FINE_PITCH, channels), scratch(3, 640, 128),
            narrow(2, 3, 3, channels, channels), narrow(2, 3, 3, channels_out, channels), pltpu.SemaphoreType.DMA((2,)),
        ],
        2, "prior", 2 * 18 * channels * (360 * 384 + 1248 * 192), (8, 9),
    )
    (decoded,) = call(
        finish_kernel,
        [
            *place_args, parts, frame, frame_other, value_weight, out_weight, gain_one, sum_one, sum_two, conv_one, conv_two, gain_two,
        ],
        [shape(FINE_ROWS, FINE_COLS, channels_out)],
        [
            scratch(3, EXT_ROWS * EXT_COLS, 128), narrow(EXT_ROWS, EXT_COLS, channels),
            scratch(3, 64, 128), narrow(FINE_ROWS + 2, FINE_PITCH, channels), scratch(3, 640, 128),
            narrow(1, 3, 3, channels, channels), narrow(1, 3, 3, channels_out, channels), pltpu.SemaphoreType.DMA((2,)),
        ],
        3, "finish", 0, (11, 12),
    )
    return decoded


def solution(mesh):
    grid = Mesh(mesh.devices.reshape(4, 2, 4, 4), ("y", "core", "x", "z"))
    placed = (
        P(ROWS, COLS, None), P(), P(), P(), P(), P(), P(), P(),
        P(None, ROWS, COLS, None), P(), P(), P(None, ROWS, COLS, None), P(), P(),
    )
    return jax.shard_map(local, mesh=grid, in_specs=placed, out_specs=P(ROWS, COLS, None), check_vma=False)
```

```python
import math

import jax
import jax.numpy as jnp
from jax import lax
from jax.experimental import pallas as pl
from jax.experimental.pallas import tpu as pltpu
from jax.sharding import Mesh
from jax.sharding import PartitionSpec as P

epsilon = 1e-06
masked_score = -1e30
ROWS = ("y", "core")
COLS = ("x", "z")
LAT_ROWS = 88
LAT_COLS = 256
TILE_ROWS = 13
TILE_COLS = 20
HALO = 2
EXT_ROWS = TILE_ROWS + 2 * HALO
EXT_COLS = TILE_COLS + 2 * HALO
HALF = EXT_COLS // 2
FRONT = HALO * HALF
FINE_ROWS = 2 * TILE_ROWS
FINE_COLS = 2 * TILE_COLS
FINE_PITCH = 48
KEY_TILE = 272
KEY_CHUNK = 1024
MAX_CHUNKS = 7
KEY_ROWS = MAX_CHUNKS * KEY_CHUNK + KEY_CHUNK
QUERY_BLOCK = 1056
HALF_ROWS = 208
STAT_ROW = EXT_ROWS * HALF - (HALF_ROWS - 16)
WIDE_ROWS = LAT_ROWS * HALF + 384
FINE_STEP = 13
TALL_TILE = 160
VMEM_BYTES = 60 * 1024 * 1024
NEAR = 48


def rms_scale(values_in, gain_vec):
    wide = values_in.astype(jnp.float32)
    return wide * lax.rsqrt(jnp.mean(wide * wide, axis=-1, keepdims=True) + epsilon) * gain_vec


def silu(v):
    return v / (1.0 + jnp.exp(-v))


def hop(value, axes, count, step):
    pairs = [(i, i + step) for i in range(count) if 0 <= i + step < count]
    return lax.ppermute(value, axes, pairs)


def far_hops(needed, ahead, back, axes, count):
    return lax.cond(
        needed,
        lambda a, b: [hop(a, axes, count, 2), hop(b, axes, count, -2)],
        lambda a, b: [a, b],
        ahead, back,
    )


def put_rows(ref, start, value):
    for g in range(ref.shape[0]):
        ref[g, pl.ds(start, value.shape[0]), :] = value[:, g * 128 : (g + 1) * 128].astype(ref.dtype)


def get_rows(ref, start, count, stride=None):
    return jnp.concatenate([ref[g, pl.ds(start, count, stride), :] for g in range(ref.shape[0])], axis=1)


def put_strided(ref, start, stride, value):
    for g in range(ref.shape[0]):
        ref[g, pl.ds(start, value.shape[0], stride), :] = value[:, g * 128 : (g + 1) * 128].astype(ref.dtype)


def before(size_ref, index):
    total = 0
    for t in range(size_ref.shape[0]):
        total = total + jnp.where(t < index, size_ref[t], 0)
    return total


def size_at(size_ref, index):
    count = size_ref.shape[0]
    inside = (index >= 0) & (index < count)
    return jnp.where(inside, size_ref[jnp.clip(index, 0, count - 1)], 0)


def keys_kernel(place_ref, row_ref, col_ref, token_ref, gain_ref, key_ref, pack_ref):
    wide = col_ref[place_ref[1]]
    pack_ref[...] = jnp.zeros_like(pack_ref)
    gain = gain_ref[...][None]
    for i in range(TILE_ROWS):
        put_rows(pack_ref, i * wide, rms_scale(token_ref[i].astype(jnp.float32), gain))
    key_ref[...] = get_rows(pack_ref, 0, KEY_TILE).astype(jnp.bfloat16)


def edges_kernel(
    place_ref, row_ref, col_ref, token_ref, one_ref, two_ref, right_ref, left_ref, right_far_ref, left_far_ref, coarse_ref, fine_ref
):
    wide = col_ref[place_ref[1]]
    for f in range(3):
        for i in range(TILE_ROWS):
            row = one_ref[f, i] if f < 2 else token_ref[i]
            put_rows(coarse_ref, (f * TILE_ROWS + i) * 24, row.astype(jnp.float32))
    for f in range(2):

        def copy_fine(i, carry):
            put_rows(fine_ref, pl.multiple_of((f * FINE_ROWS + i) * FINE_COLS, 8), two_ref[f, i].astype(jnp.float32))
            return carry

        lax.fori_loop(0, FINE_ROWS, copy_fine, 0)
    near = 3 * TILE_ROWS
    fine = 2 * FINE_ROWS
    for ref in (right_ref, left_ref, right_far_ref, left_far_ref):
        ref[...] = jnp.zeros_like(ref)
    last = get_rows(coarse_ref, wide - 1, near, 24).astype(jnp.bfloat16)
    first = get_rows(coarse_ref, 0, near, 24).astype(jnp.bfloat16)
    right_ref[0:near, :] = last
    right_ref[NEAR : NEAR + near, :] = get_rows(coarse_ref, jnp.maximum(wide - 2, 0), near, 24).astype(jnp.bfloat16)
    right_ref[2 * NEAR : 2 * NEAR + fine, :] = get_rows(fine_ref, 2 * wide - 1, fine, FINE_COLS).astype(jnp.bfloat16)
    left_ref[0:near, :] = first
    left_ref[NEAR : NEAR + near, :] = get_rows(coarse_ref, 1, near, 24).astype(jnp.bfloat16)
    left_ref[2 * NEAR : 2 * NEAR + fine, :] = get_rows(fine_ref, 0, fine, FINE_COLS).astype(jnp.bfloat16)
    right_far_ref[0:near, :] = last
    left_far_ref[0:near, :] = first


def columns_kernel(
    place_ref, row_ref, col_ref, token_ref, one_ref, two_ref, from_left_ref, from_right_ref, from_left_far_ref, from_right_far_ref,
    mine_ref, other_ref, prior_ref, fine_out_ref, down_ref, up_ref, down_far_ref, up_far_ref, coarse_ref, fine_ref, half_ref,
):
    core = place_ref[2]
    tall = row_ref[place_ref[0]]
    wide = col_ref[place_ref[1]]
    left_wide = size_at(col_ref, place_ref[1] - 1)
    right_wide = size_at(col_ref, place_ref[1] + 1)
    near = 3 * TILE_ROWS
    fine = 2 * FINE_ROWS
    blank = jnp.zeros((near, 384), jnp.float32)
    put_strided(coarse_ref, EXT_COLS - 2, EXT_COLS, blank)
    put_strided(coarse_ref, EXT_COLS - 1, EXT_COLS, blank)
    for f in range(3):
        for i in range(TILE_ROWS):
            row = one_ref[f, i] if f < 2 else token_ref[i]
            put_rows(coarse_ref, (f * TILE_ROWS + i) * EXT_COLS + HALO, row.astype(jnp.float32))
    left_two = jnp.where(left_wide == 1, from_left_far_ref[0:near, :], from_left_ref[NEAR : NEAR + near, :])
    right_two = jnp.where(right_wide == 1, from_right_far_ref[0:near, :], from_right_ref[NEAR : NEAR + near, :])
    put_strided(coarse_ref, 0, EXT_COLS, left_two.astype(jnp.float32))
    put_strided(coarse_ref, 1, EXT_COLS, from_left_ref[0:near, :].astype(jnp.float32))
    put_strided(coarse_ref, wide + 2, EXT_COLS, from_right_ref[0:near, :].astype(jnp.float32))
    put_strided(coarse_ref, wide + 3, EXT_COLS, right_two.astype(jnp.float32))
    for side, ref in ((core, mine_ref), (1 - core, other_ref)):
        for i in range(TILE_ROWS):
            put_rows(half_ref, i * HALF, get_rows(coarse_ref, (2 * TILE_ROWS + i) * EXT_COLS + side * HALF, HALF))
        half_ref[:, TILE_ROWS * HALF : TALL_TILE, :] = jnp.zeros((3, TALL_TILE - TILE_ROWS * HALF, 128), jnp.float32)
        ref[...] = get_rows(half_ref, 0, TALL_TILE).astype(jnp.bfloat16)
    for i in range(2 * TILE_ROWS):
        prior_ref[i] = get_rows(coarse_ref, i * EXT_COLS, EXT_COLS).astype(jnp.bfloat16)
    for c in range(FINE_COLS + 1, FINE_PITCH):
        put_strided(fine_ref, c, FINE_PITCH, jnp.zeros((fine, 384), jnp.float32))
    for f in range(2):

        def copy_fine(i, carry):
            put_rows(fine_ref, (f * FINE_ROWS + i) * FINE_PITCH + 1, two_ref[f, i].astype(jnp.float32))
            return carry

        lax.fori_loop(0, FINE_ROWS, copy_fine, 0)
    put_strided(fine_ref, 0, FINE_PITCH, from_left_ref[2 * NEAR : 2 * NEAR + fine, :].astype(jnp.float32))
    put_strided(fine_ref, 2 * wide + 1, FINE_PITCH, from_right_ref[2 * NEAR : 2 * NEAR + fine, :].astype(jnp.float32))

    def write_fine(i, carry):
        fine_out_ref[i] = get_rows(fine_ref, pl.multiple_of(i * FINE_PITCH, 8), FINE_PITCH).astype(jnp.bfloat16)
        return carry

    lax.fori_loop(0, fine, write_fine, 0)
    for f in range(2):
        base = f * TILE_ROWS
        last = prior_ref[base + tall - 1]
        down_ref[f] = last
        down_ref[2 + f] = prior_ref[base + jnp.maximum(tall - 2, 0)]
        down_far_ref[f] = last
        up_ref[f] = prior_ref[base]
        up_ref[2 + f] = prior_ref[base + 1]
        up_far_ref[f] = prior_ref[base]
        bottom = fine_out_ref[f * FINE_ROWS + 2 * tall - 1]
        top = fine_out_ref[f * FINE_ROWS]
        for h in range(2):
            down_ref[4 + 2 * f + h] = bottom[h * 24 : (h + 1) * 24]
            up_ref[4 + 2 * f + h] = top[h * 24 : (h + 1) * 24]


def prior_kernel(
    place_ref, row_ref, prior_ref, fine_ref, from_up_ref, from_down_ref, from_up_far_ref, from_down_far_ref, one_ref, two_ref,
    sum_one_ref, sum_two_ref, phase_ref, coarse_ref, wide_ref, part_ref, weight_one_ref, weight_two_ref, sem_ref,
):
    fetch_one = pltpu.make_async_copy(one_ref.at[pl.ds(0, 2)], weight_one_ref, sem_ref.at[0])
    fetch_two = pltpu.make_async_copy(two_ref, weight_two_ref, sem_ref.at[1])
    fetch_one.start()
    fetch_two.start()
    tall = row_ref[place_ref[0]]
    up_tall = size_at(row_ref, place_ref[0] - 1)
    down_tall = size_at(row_ref, place_ref[0] + 1)
    for f in range(2):
        coarse_ref[f, 0] = jnp.where(up_tall == 1, from_up_far_ref[f], from_up_ref[2 + f])
        coarse_ref[f, 1] = from_up_ref[f]
        for i in range(TILE_ROWS):
            coarse_ref[f, HALO + i] = prior_ref[f * TILE_ROWS + i]
        for i in (TILE_ROWS + 2, TILE_ROWS + 3):
            coarse_ref[f, i] = jnp.zeros((EXT_COLS, 384), jnp.bfloat16)
        coarse_ref[f, tall + 2] = from_down_ref[f]
        coarse_ref[f, tall + 3] = jnp.where(down_tall == 1, from_down_far_ref[f], from_down_ref[2 + f])
        wide_ref[f, 0] = jnp.concatenate([from_up_ref[4 + 2 * f], from_up_ref[5 + 2 * f]], axis=0)

        def copy_fine(i, carry):
            wide_ref[f, 1 + i] = fine_ref[f * FINE_ROWS + i]
            return carry

        lax.fori_loop(0, FINE_ROWS, copy_fine, 0)
        wide_ref[f, FINE_ROWS + 1] = jnp.zeros((FINE_PITCH, 384), jnp.bfloat16)
        wide_ref[f, 2 * tall + 1] = jnp.concatenate([from_down_ref[4 + 2 * f], from_down_ref[5 + 2 * f]], axis=0)
    fetch_one.wait()
    sum_one_ref[...] = coarse_conv(lambda f, a, n: coarse_ref[f, a : a + n], weight_one_ref, part_ref, 2)
    fetch_two.wait()
    for r in range(0, FINE_ROWS, FINE_STEP):
        sum_two_ref[r * FINE_PITCH : (r + FINE_STEP) * FINE_PITCH, :] = fine_conv(
            lambda f, a, n: wide_ref[f, r + a : r + a + n], weight_two_ref, part_ref, 2
        )
    taps = ((0,), (1, 2), (0, 1), (2,))
    for u in range(4):
        rows = []
        for b in range(3):
            tap = sum(weight_two_ref[2, a, b].astype(jnp.float32) for a in taps[u])
            rows.append(tap)
        for v in range(4):
            phase_ref[u, v] = sum(rows[b] for b in taps[v]).astype(jnp.bfloat16)


def coarse_conv(rows_of, weight_ref, part_ref, depth):
    rows = TILE_ROWS + 2
    taps = [(f, a) for f in range(depth) for a in range(3)]
    left = jnp.concatenate([rows_of(f, a, rows).reshape(rows * EXT_COLS, 384) for f, a in taps], axis=1)
    right = jnp.concatenate([jnp.concatenate([weight_ref[f, a, b] for b in range(3)], axis=1) for f, a in taps], axis=0)
    product = jnp.dot(left, right, preferred_element_type=jnp.float32)
    return shifted_sum([product[:, b * 384 : (b + 1) * 384] for b in range(3)], part_ref)


def fine_conv(rows_of, weight_ref, part_ref, depth):
    taps = [(f, a) for f in range(depth) for a in range(3)]
    left = jnp.concatenate([rows_of(f, a, FINE_STEP).reshape(FINE_STEP * FINE_PITCH, 384) for f, a in taps], axis=1)
    products = [
        lax.dot_general(
            left, jnp.concatenate([weight_ref[f, a, b] for f, a in taps], axis=1), (((1,), (1,)), ((), ())),
            preferred_element_type=jnp.float32,
        )
        for b in range(3)
    ]
    return shifted_sum(products, part_ref)


def shifted_sum(products, part_ref):
    total = products[0]
    count, width = total.shape
    groups = -(-width // 128)
    for b in (1, 2):
        for g in range(groups):
            hi = min((g + 1) * 128, width)
            part_ref[g, 0:count, 0 : hi - g * 128] = products[b][:, g * 128 : hi]
        moved = jnp.concatenate([part_ref[g, b : b + count, :] for g in range(groups)], axis=1)
        total = total + moved[:, 0:width]
    return total


def query_kernel(
    place_ref, row_ref, own_ref, one_ref, two_ref, three_ref, gain_ref, qw_ref, kw_ref, query_ref, frame_ref, frame_other_ref, wide_ref, *, scale
):
    y_at = place_ref[0] // 2
    wide_ref[...] = jnp.zeros_like(wide_ref)
    slot = lax.broadcasted_iota(jnp.int32, (TALL_TILE, 128), 0)
    for k, ref in enumerate((own_ref, one_ref, two_ref, three_ref)):
        source = jnp.bitwise_and(y_at - k, 3)
        for t in range(2):
            start = FRONT + before(row_ref, 2 * source + t) * HALF
            usable = slot < row_ref[2 * source + t] * HALF
            part = ref[t].astype(jnp.float32)
            for g in range(3):
                held = wide_ref[g, pl.ds(start, TALL_TILE), :]
                wide_ref[g, pl.ds(start, TALL_TILE), :] = jnp.where(usable, part[:, g * 128 : (g + 1) * 128], held)
    count = LAT_ROWS * HALF
    frame_ref[...] = get_rows(wide_ref, before(row_ref, place_ref[0]) * HALF, HALF_ROWS).astype(jnp.bfloat16)
    sibling = place_ref[0] + 1 - 2 * place_ref[2]
    frame_other_ref[...] = get_rows(wide_ref, before(row_ref, sibling) * HALF, HALF_ROWS).astype(jnp.bfloat16)
    step = count // 3
    for i in range(3):
        raw = get_rows(wide_ref, FRONT + i * step, step)
        normed = rms_scale(raw, gain_ref[...][None]).astype(jnp.bfloat16)
        query = jnp.dot(normed, qw_ref[...], preferred_element_type=jnp.float32).astype(jnp.bfloat16)
        turned = lax.dot_general(query, kw_ref[...], (((1,), (1,)), ((), ())), preferred_element_type=jnp.float32)
        query_ref[i * step : (i + 1) * step, :] = (turned * scale).astype(jnp.bfloat16)


def attention_kernel(
    place_ref, row_ref, col_ref, query_ref, tile_ref, out_ref,
    key_ref, bias_ref, score_ref, top_ref, sum_ref, acc_ref, wide_ref, stat_ref,
):
    tiles = tile_ref.shape[0]
    cols = col_ref.shape[0]
    y_at = place_ref[0] // 2
    spot = lax.broadcasted_iota(jnp.int32, (16, KEY_CHUNK), 0) * KEY_CHUNK + lax.broadcasted_iota(jnp.int32, (16, KEY_CHUNK), 1)

    def gather(t, carry):
        offset, bias = carry
        offset = pl.multiple_of(offset, 16)
        key_ref[pl.ds(offset, KEY_TILE), :] = tile_ref[t]
        count = row_ref[2 * y_at + t // cols] * col_ref[t % cols]
        bias = jnp.where((spot >= offset) & (spot < offset + count), 0.0, bias)
        return offset + (count + 15) // 16 * 16, bias

    tail, bias = lax.fori_loop(0, tiles, gather, (jnp.int32(0), jnp.full((16, KEY_CHUNK), masked_score, jnp.float32)))
    tail = pl.multiple_of(tail, 16)
    key_ref[pl.ds(tail, KEY_CHUNK), :] = jnp.zeros((KEY_CHUNK, key_ref.shape[1]), jnp.bfloat16)
    for j in range(MAX_CHUNKS):
        bias_ref[j] = bias[j : j + 1, :]
    chunk_count = (tail + KEY_CHUNK - 1) // KEY_CHUNK
    total = wide_ref.shape[1]
    count = query_ref.shape[0]
    wide_ref[:, 0:FRONT, :] = jnp.zeros((3, FRONT, 128), jnp.float32)
    wide_ref[:, FRONT + count : total, :] = jnp.zeros((3, total - FRONT - count, 128), jnp.float32)
    stat_ref[0:FRONT, :] = jnp.zeros((FRONT, 128), jnp.float32)
    stat_ref[FRONT + count : total, :] = jnp.zeros((total - FRONT - count, 128), jnp.float32)
    blocks = count // QUERY_BLOCK
    lane_groups = KEY_CHUNK // 128

    def keys_at(j):
        return key_ref[pl.ds(pl.multiple_of(j * KEY_CHUNK, KEY_CHUNK), KEY_CHUNK), :]

    def score_step(i, j):
        slot = 0
        query = query_ref[i * QUERY_BLOCK : (i + 1) * QUERY_BLOCK, :]
        s = lax.dot_general(query, keys_at(j), (((1,), (1,)), ((), ())), preferred_element_type=jnp.float32)
        s = s + bias_ref[j]
        score_ref[slot, j] = s
        best = s[:, 0:128]
        for g in range(1, lane_groups):
            best = jnp.maximum(best, s[:, g * 128 : (g + 1) * 128])
        top_ref[slot] = jnp.maximum(top_ref[slot], best)

    def value_step(i, j):
        slot = 0
        top = top_ref[slot]
        p = jnp.exp2(score_ref[slot, j] - jnp.concatenate([top] * lane_groups, axis=1))
        part = p[:, 0:128]
        for g in range(1, lane_groups):
            part = part + p[:, g * 128 : (g + 1) * 128]
        sum_ref[...] = sum_ref[...] + part
        acc_ref[...] = acc_ref[...] + jnp.dot(p.astype(jnp.bfloat16), keys_at(j), preferred_element_type=jnp.float32)

    for i in range(blocks + 1):
        if i < blocks:
            top_ref[0] = jnp.full((QUERY_BLOCK, 128), masked_score, jnp.float32)
        if i > 0:
            last = 0
            best = jnp.max(top_ref[last], axis=1, keepdims=True)
            top_ref[last] = jnp.broadcast_to(best, (QUERY_BLOCK, 128))
            sum_ref[...] = jnp.zeros_like(sum_ref)
            acc_ref[...] = jnp.zeros_like(acc_ref)

        def step(j, carry):
            if i < blocks:
                score_step(i, j)
            if i > 0:
                value_step(i - 1, j)
            return carry

        lax.fori_loop(0, chunk_count, step, 0)
        if i > 0:
            denominator = jnp.sum(sum_ref[...], axis=1, keepdims=True)
            lo = FRONT + (i - 1) * QUERY_BLOCK
            put_rows(wide_ref, lo, acc_ref[...] / denominator)
            level = top_ref[0] + jnp.log2(jnp.broadcast_to(denominator, (QUERY_BLOCK, 128)))
            high = level.astype(jnp.bfloat16).astype(jnp.float32)
            mid = (level - high).astype(jnp.bfloat16).astype(jnp.float32)
            low = level - high - mid
            lane = lax.broadcasted_iota(jnp.int32, (QUERY_BLOCK, 128), 1)
            packed = jnp.where(lane == 0, high, jnp.where(lane == 1, mid, jnp.where(lane == 2, low, 0.0)))
            stat_ref[lo : lo + QUERY_BLOCK, :] = packed
    body = HALF_ROWS - 16
    select = (
        lax.broadcasted_iota(jnp.int32, (16, 128), 0) - STAT_ROW == lax.broadcasted_iota(jnp.int32, (16, 128), 1)
    ).astype(jnp.bfloat16)
    is_stat = lax.broadcasted_iota(jnp.int32, (16, 384), 0) >= STAT_ROW
    for b in range(out_ref.shape[0]):
        offset = before(row_ref, b) * HALF
        out_ref[b, 0:body, :] = get_rows(wide_ref, offset, body).astype(jnp.bfloat16)
        levels = stat_ref[pl.ds(offset, 384), :].astype(jnp.bfloat16)
        levels = lax.dot_general(select, levels, (((1,), (1,)), ((), ())), preferred_element_type=jnp.float32)
        last = jnp.where(is_stat, levels, get_rows(wide_ref, offset + body, 16))
        out_ref[b, body:HALF_ROWS, :] = last.astype(jnp.bfloat16)


def finish_kernel(
    place_ref, row_ref, col_ref, part_ref, mine_ref, other_ref, vw_ref, ow_ref, gain_one_ref, sum_one_ref, sum_two_ref, one_ref, two_ref,
    gain_two_ref, out_ref, act_ref, first_ref, shift_ref, product_ref, fine_ref, weight_one_ref, phase_ref, sem_ref,
):
    fetch_one = pltpu.make_async_copy(one_ref.at[pl.ds(2, 1)], weight_one_ref, sem_ref.at[0])
    fetch_two = pltpu.make_async_copy(two_ref, phase_ref, sem_ref.at[1])
    fetch_one.start()
    fetch_two.start()
    core = place_ref[2]
    tall = row_ref[place_ref[0]]
    wide = col_ref[place_ref[1]]
    stat = lax.broadcasted_iota(jnp.int32, (16, 128), 0)
    ones = ((stat >= STAT_ROW) & (stat < STAT_ROW + 3)).astype(jnp.bfloat16)
    halves = []
    for side in range(2):
        sources = range(side, part_ref.shape[0], 2)
        levels = [
            lax.dot_general(
                part_ref[g, HALF_ROWS - 16 : HALF_ROWS, 0:256], ones, (((0,), (0,)), ((), ())), preferred_element_type=jnp.float32
            )[0:HALF_ROWS]
            for g in sources
        ]
        best = jnp.maximum(jnp.maximum(levels[0], levels[1]), jnp.maximum(levels[2], levels[3]))
        weights = [jnp.exp2(level - best) for level in levels]
        total = (weights[0] + weights[1]) + (weights[2] + weights[3])
        merged = None
        for weight, g in zip(weights, sources):
            share = weight / total
            term = part_ref[g, 0:HALF_ROWS, :].astype(jnp.float32) * jnp.concatenate([share] * 3, axis=1)
            merged = term if merged is None else merged + term
        halves.append(merged.astype(jnp.bfloat16))
    merged = jnp.concatenate(halves, axis=0)
    attention = jnp.dot(merged, vw_ref[...], preferred_element_type=jnp.float32).astype(jnp.bfloat16)
    projected = jnp.dot(attention, ow_ref[...], preferred_element_type=jnp.float32)
    mine = mine_ref[...].astype(jnp.float32)
    other = other_ref[...].astype(jnp.float32)
    frame = jnp.concatenate([jnp.where(core == 0, mine, other), jnp.where(core == 0, other, mine)], axis=0)
    mixed = (frame + projected).astype(jnp.bfloat16)
    put_rows(shift_ref, 0, silu(rms_scale(mixed, gain_one_ref[...][None])))
    row_start = before(row_ref, place_ref[0])
    col_start = before(col_ref, place_ref[1])
    for side in range(2):
        for i in range(EXT_ROWS):
            put_rows(act_ref, i * EXT_COLS + side * HALF, get_rows(shift_ref, side * HALF_ROWS + i * HALF, HALF))
    at_col = col_start - HALO + lax.broadcasted_iota(jnp.int32, (EXT_COLS, 384), 0)
    col_inside = (at_col >= 0) & (at_col < LAT_COLS)
    for i in range(EXT_ROWS):
        at_row = row_start - HALO + i
        inside = col_inside & (at_row >= 0) & (at_row < LAT_ROWS)
        first_ref[i] = jnp.where(inside, get_rows(act_ref, i * EXT_COLS, EXT_COLS), 0.0).astype(jnp.bfloat16)
    rows = TILE_ROWS + 2
    fetch_one.wait()
    total = coarse_conv(lambda f, a, n: first_ref[a : a + n], weight_one_ref, shift_ref, 1)
    y_one = (total + sum_one_ref[...]).astype(jnp.bfloat16)
    act = silu(rms_scale(y_one, gain_two_ref[...][None])).astype(jnp.bfloat16).astype(jnp.float32)
    put_rows(act_ref, 0, act)
    at_col = col_start - 1 + lax.broadcasted_iota(jnp.int32, (EXT_COLS, 384), 0)
    col_inside = (at_col >= 0) & (at_col < LAT_COLS)
    for i in range(rows):
        at_row = row_start - 1 + i
        inside = col_inside & (at_row >= 0) & (at_row < LAT_ROWS)
        first_ref[i] = jnp.where(inside, get_rows(act_ref, i * EXT_COLS, EXT_COLS), 0.0).astype(jnp.bfloat16)
    fetch_two.wait()
    count = TILE_ROWS * EXT_COLS
    for p in range(2):
        left = jnp.concatenate(
            [first_ref[p + u : p + u + TILE_ROWS].reshape(count, 384) for u in range(2)], axis=1
        )
        for q in range(2):
            for v in range(2):
                right = jnp.concatenate([phase_ref[2 * p + u, 2 * q + v] for u in range(2)], axis=1)
                product = lax.dot_general(left, right, (((1,), (1,)), ((), ())), preferred_element_type=jnp.float32)
                product_ref[2 * q + v, 0, 0:count, :] = product[:, 0:128]
                product_ref[2 * q + v, 1, 0:count, 0:64] = product[:, 128:192]
            for i in range(TILE_ROWS):
                for g in range(2):
                    near = product_ref[2 * q, g, pl.ds(i * EXT_COLS + q, EXT_COLS), :]
                    next_ = product_ref[2 * q + 1, g, pl.ds(i * EXT_COLS + q + 1, EXT_COLS), :]
                    fine_ref[g, pl.ds((2 * i + p) * FINE_PITCH + q, EXT_COLS, 2), :] = near + next_
    col = lax.broadcasted_iota(jnp.int32, (FINE_COLS, 192), 0)
    for r in range(FINE_ROWS):
        line = get_rows(fine_ref, r * FINE_PITCH, FINE_COLS)[:, 0:192] + sum_two_ref[r * FINE_PITCH : r * FINE_PITCH + FINE_COLS, :]
        usable = (col < 2 * wide) & (r < 2 * tall)
        out_ref[r] = jnp.where(usable, line, 0.0).astype(jnp.bfloat16)


def call(body, inputs, outs, scratch, smem_count, name, flops=0, far=()):
    smem = pl.BlockSpec(memory_space=pltpu.SMEM)
    vmem = pl.BlockSpec(memory_space=pltpu.VMEM)
    moved = sum(math.prod(v.shape) * v.dtype.itemsize for v in list(inputs) + list(outs))
    return pl.pallas_call(
        body,
        in_specs=[
            smem if i < smem_count else pl.BlockSpec(memory_space=pl.ANY) if i in far else vmem for i in range(len(inputs))
        ],
        out_specs=[vmem] * len(outs),
        out_shape=outs,
        scratch_shapes=scratch,
        compiler_params=pltpu.CompilerParams(vmem_limit_bytes=VMEM_BYTES),
        cost_estimate=pl.CostEstimate(flops=int(flops), transcendentals=0, bytes_accessed=int(moved)),
        name=name,
    )(*inputs)


def attend(place, row_sizes, col_sizes, queries, tiles):
    channels = queries.shape[1]
    scratch = lambda *dims: pltpu.VMEM(dims, jnp.float32)
    (parts,) = call(
        attention_kernel,
        [place, row_sizes, col_sizes, queries, tiles],
        [jax.ShapeDtypeStruct((8, HALF_ROWS, channels), jnp.bfloat16)],
        [
            pltpu.VMEM((KEY_ROWS, channels), jnp.bfloat16), scratch(MAX_CHUNKS, 1, KEY_CHUNK),
            scratch(1, MAX_CHUNKS, QUERY_BLOCK, KEY_CHUNK),
            scratch(1, QUERY_BLOCK, 128), scratch(QUERY_BLOCK, 128), scratch(QUERY_BLOCK, channels),
            scratch(3, WIDE_ROWS, 128), scratch(WIDE_ROWS, 128),
        ],
        3, "attention", 4 * LAT_ROWS * HALF * channels * KEY_ROWS,
    )
    return parts


def local(
    tokens, row_sizes, col_sizes, norm_gain, query_weight, key_weight, value_weight, out_weight,
    cache_one, gain_one, conv_one, cache_two, gain_two, conv_two,
):
    channels = tokens.shape[2]
    n_row = row_sizes.shape[0]
    n_col = col_sizes.shape[0]
    n_y = lax.axis_size("y")
    core = lax.axis_index("core")
    row_at = lax.axis_index("y") * lax.axis_size("core") + core
    col_at = lax.axis_index("x") * lax.axis_size("z") + lax.axis_index("z")
    place = jnp.stack([row_at, col_at, core]).astype(jnp.int32)
    shape = lambda *dims: jax.ShapeDtypeStruct(dims, jnp.bfloat16)
    wide_shape = lambda *dims: jax.ShapeDtypeStruct(dims, jnp.float32)
    scratch = lambda *dims: pltpu.VMEM(dims, jnp.float32)
    narrow = lambda *dims: pltpu.VMEM(dims, jnp.bfloat16)
    message = 160
    place_args = [place, row_sizes, col_sizes]
    (own_keys,) = call(
        keys_kernel, [*place_args, tokens, norm_gain], [shape(KEY_TILE, channels)], [scratch(3, 304, 128)], 3, "keys"
    )
    tiles = lax.all_gather(own_keys, ("core", "x", "z"), axis=0, tiled=False)
    to_right, to_left, to_right_far, to_left_far = call(
        edges_kernel,
        [*place_args, tokens, cache_one, cache_two],
        [shape(message, channels), shape(message, channels), shape(NEAR, channels), shape(NEAR, channels)],
        [scratch(3, 3 * TILE_ROWS * 24, 128), scratch(3, 2 * FINE_ROWS * FINE_COLS, 128)],
        3, "edges",
    )
    from_left = hop(to_right, COLS, n_col, 1)
    from_right = hop(to_left, COLS, n_col, -1)
    from_left_far, from_right_far = far_hops(jnp.any(col_sizes == 1), to_right_far, to_left_far, COLS, n_col)
    mine, other, prior, fine, down, up, down_far, up_far = call(
        columns_kernel,
        [*place_args, tokens, cache_one, cache_two, from_left, from_right, from_left_far, from_right_far],
        [
            shape(TALL_TILE, channels), shape(TALL_TILE, channels), shape(2 * TILE_ROWS, EXT_COLS, channels),
            shape(2 * FINE_ROWS, FINE_PITCH, channels), shape(8, EXT_COLS, channels), shape(8, EXT_COLS, channels),
            shape(2, EXT_COLS, channels), shape(2, EXT_COLS, channels),
        ],
        [scratch(3, 3 * TILE_ROWS * EXT_COLS, 128), scratch(3, 2 * FINE_ROWS * FINE_PITCH, 128), scratch(3, TALL_TILE, 128)],
        3, "columns",
    )
    swap = [(0, 1), (1, 0)]
    sibling = lax.ppermute(other, "core", swap)
    pair = jnp.where(core == 0, jnp.stack([mine, sibling]), jnp.stack([sibling, mine]))
    strips = [pair] + [lax.ppermute(pair, "y", [(i, (i + k) % n_y) for i in range(n_y)]) for k in range(1, n_y)]
    around = [hop(down, ROWS, n_row, 1), hop(up, ROWS, n_row, -1)]
    around += far_hops(jnp.any(row_sizes == 1), down_far, up_far, ROWS, n_row)
    strips, around = lax.optimization_barrier((strips, around))
    scale = math.log2(math.e) / math.sqrt(channels)

    def query_body(*refs):
        query_kernel(*refs, scale=scale)

    queries, frame, frame_other = call(
        query_body,
        [place, row_sizes, *strips, norm_gain, query_weight, key_weight],
        [shape(LAT_ROWS * HALF, channels), shape(HALF_ROWS, channels), shape(HALF_ROWS, channels)],
        [scratch(3, WIDE_ROWS, 128)],
        2, "queries", 4 * LAT_ROWS * HALF * channels * channels,
    )
    frame_other = lax.ppermute(frame_other, "core", swap)
    parts = attend(place, row_sizes, col_sizes, queries, tiles.reshape(2 * n_col, KEY_TILE, channels))
    parts = lax.all_to_all(parts, ROWS, 0, 0)
    conv_two = jnp.swapaxes(conv_two, 3, 4)
    channels_out = conv_two.shape[3]
    sum_one, sum_two, phases = call(
        prior_kernel,
        [place, row_sizes, prior, fine, *around, conv_one, conv_two],
        [
            wide_shape((TILE_ROWS + 2) * EXT_COLS, channels), wide_shape(FINE_ROWS * FINE_PITCH, channels_out),
            shape(4, 4, channels_out, channels),
        ],
        [
            narrow(2, EXT_ROWS, EXT_COLS, channels), narrow(2, FINE_ROWS + 2, FINE_PITCH, channels), scratch(3, 640, 128),
            narrow(2, 3, 3, channels, channels), narrow(3, 3, 3, channels_out, channels), pltpu.SemaphoreType.DMA((2,)),
        ],
        2, "prior", 2 * 18 * channels * (360 * 384 + 1248 * 192), (8, 9),
    )
    (decoded,) = call(
        finish_kernel,
        [
            *place_args, parts, frame, frame_other, value_weight, out_weight, gain_one, sum_one, sum_two, conv_one, phases, gain_two,
        ],
        [shape(FINE_ROWS, FINE_COLS, channels_out)],
        [
            scratch(3, EXT_ROWS * EXT_COLS, 128), narrow(EXT_ROWS, EXT_COLS, channels), scratch(3, 640, 128),
            scratch(4, 2, TILE_ROWS * EXT_COLS + 8, 128), scratch(2, FINE_ROWS * FINE_PITCH, 128),
            narrow(1, 3, 3, channels, channels), narrow(4, 4, channels_out, channels), pltpu.SemaphoreType.DMA((2,)),
        ],
        3, "finish", 0, (11, 12),
    )
    return decoded


def solution(mesh):
    grid = Mesh(mesh.devices.reshape(4, 2, 4, 4), ("y", "core", "x", "z"))
    placed = (
        P(ROWS, COLS, None), P(), P(), P(), P(), P(), P(), P(),
        P(None, ROWS, COLS, None), P(), P(), P(None, ROWS, COLS, None), P(), P(),
    )
    return jax.shard_map(local, mesh=grid, in_specs=placed, out_specs=P(ROWS, COLS, None), check_vma=False)
```

```python
import math

import jax
import jax.numpy as jnp
from jax import lax
from jax.experimental import pallas as pl
from jax.experimental.pallas import tpu as pltpu
from jax.sharding import Mesh
from jax.sharding import PartitionSpec as P

epsilon = 1e-06
masked_score = -1e30
ROWS = ("y", "core")
COLS = ("x", "z")
LAT_ROWS = 88
LAT_COLS = 256
TILE_ROWS = 13
TILE_COLS = 20
HALO = 2
EXT_ROWS = TILE_ROWS + 2 * HALO
EXT_COLS = TILE_COLS + 2 * HALO
HALF = EXT_COLS // 2
FRONT = HALO * HALF
FINE_ROWS = 2 * TILE_ROWS
FINE_COLS = 2 * TILE_COLS
FINE_PITCH = 48
KEY_TILE = 272
KEY_CHUNK = 1024
KEY_GROUPS = 4
MAX_CHUNKS = 7
KEY_ROWS = MAX_CHUNKS * KEY_CHUNK + KEY_CHUNK
QUERY_BLOCK = 1056
HALF_ROWS = 208
STAT_ROW = EXT_ROWS * HALF - (HALF_ROWS - 16)
WIDE_ROWS = LAT_ROWS * HALF + 384
FINE_STEP = 13
TALL_TILE = 160
VMEM_BYTES = 60 * 1024 * 1024
NEAR = 48


def rms_scale(values_in, gain_vec):
    wide = values_in.astype(jnp.float32)
    return wide * lax.rsqrt(jnp.mean(wide * wide, axis=-1, keepdims=True) + epsilon) * gain_vec


def silu(v):
    return v / (1.0 + jnp.exp(-v))


def hop(value, axes, count, step):
    pairs = [(i, i + step) for i in range(count) if 0 <= i + step < count]
    return lax.ppermute(value, axes, pairs)


def far_hops(needed, ahead, back, axes, count):
    return lax.cond(
        needed,
        lambda a, b: [hop(a, axes, count, 2), hop(b, axes, count, -2)],
        lambda a, b: [a, b],
        ahead, back,
    )


def put_rows(ref, start, value):
    for g in range(ref.shape[0]):
        ref[g, pl.ds(start, value.shape[0]), :] = value[:, g * 128 : (g + 1) * 128].astype(ref.dtype)


def get_rows(ref, start, count, stride=None):
    return jnp.concatenate([ref[g, pl.ds(start, count, stride), :] for g in range(ref.shape[0])], axis=1)


def put_strided(ref, start, stride, value):
    for g in range(ref.shape[0]):
        ref[g, pl.ds(start, value.shape[0], stride), :] = value[:, g * 128 : (g + 1) * 128].astype(ref.dtype)


def before(size_ref, index):
    total = 0
    for t in range(size_ref.shape[0]):
        total = total + jnp.where(t < index, size_ref[t], 0)
    return total


def size_at(size_ref, index):
    count = size_ref.shape[0]
    inside = (index >= 0) & (index < count)
    return jnp.where(inside, size_ref[jnp.clip(index, 0, count - 1)], 0)


def keys_kernel(col_ref, token_ref, gain_ref, key_ref, pack_ref):
    wide = col_ref[lax.axis_index("x") * lax.axis_size("z") + lax.axis_index("z")]
    pack_ref[...] = jnp.zeros_like(pack_ref)
    gain = gain_ref[...][None]
    for i in range(TILE_ROWS):
        put_rows(pack_ref, i * wide, rms_scale(token_ref[i].astype(jnp.float32), gain))
    key_ref[...] = get_rows(pack_ref, 0, KEY_TILE).astype(jnp.bfloat16)


def edges_kernel(
    place_ref, row_ref, col_ref, token_ref, one_ref, two_ref, right_ref, left_ref, right_far_ref, left_far_ref, coarse_ref, fine_ref
):
    wide = col_ref[place_ref[1]]
    for f in range(3):
        for i in range(TILE_ROWS):
            row = one_ref[f, i] if f < 2 else token_ref[i]
            put_rows(coarse_ref, (f * TILE_ROWS + i) * 24, row.astype(jnp.float32))
    for f in range(2):

        def copy_fine(i, carry):
            put_rows(fine_ref, pl.multiple_of((f * FINE_ROWS + i) * FINE_COLS, 8), two_ref[f, i].astype(jnp.float32))
            return carry

        lax.fori_loop(0, FINE_ROWS, copy_fine, 0)
    near = 3 * TILE_ROWS
    fine = 2 * FINE_ROWS
    for ref in (right_ref, left_ref, right_far_ref, left_far_ref):
        ref[...] = jnp.zeros_like(ref)
    last = get_rows(coarse_ref, wide - 1, near, 24).astype(jnp.bfloat16)
    first = get_rows(coarse_ref, 0, near, 24).astype(jnp.bfloat16)
    right_ref[0:near, :] = last
    right_ref[NEAR : NEAR + near, :] = get_rows(coarse_ref, jnp.maximum(wide - 2, 0), near, 24).astype(jnp.bfloat16)
    right_ref[2 * NEAR : 2 * NEAR + fine, :] = get_rows(fine_ref, 2 * wide - 1, fine, FINE_COLS).astype(jnp.bfloat16)
    left_ref[0:near, :] = first
    left_ref[NEAR : NEAR + near, :] = get_rows(coarse_ref, 1, near, 24).astype(jnp.bfloat16)
    left_ref[2 * NEAR : 2 * NEAR + fine, :] = get_rows(fine_ref, 0, fine, FINE_COLS).astype(jnp.bfloat16)
    right_far_ref[0:near, :] = last
    left_far_ref[0:near, :] = first


def columns_kernel(
    place_ref, row_ref, col_ref, token_ref, one_ref, two_ref, from_left_ref, from_right_ref, from_left_far_ref, from_right_far_ref,
    mine_ref, other_ref, prior_ref, fine_out_ref, down_ref, up_ref, down_far_ref, up_far_ref, coarse_ref, fine_ref, half_ref,
):
    core = place_ref[2]
    tall = row_ref[place_ref[0]]
    wide = col_ref[place_ref[1]]
    left_wide = size_at(col_ref, place_ref[1] - 1)
    right_wide = size_at(col_ref, place_ref[1] + 1)
    near = 3 * TILE_ROWS
    fine = 2 * FINE_ROWS
    blank = jnp.zeros((near, 384), jnp.float32)
    put_strided(coarse_ref, EXT_COLS - 2, EXT_COLS, blank)
    put_strided(coarse_ref, EXT_COLS - 1, EXT_COLS, blank)
    for f in range(3):
        for i in range(TILE_ROWS):
            row = one_ref[f, i] if f < 2 else token_ref[i]
            put_rows(coarse_ref, (f * TILE_ROWS + i) * EXT_COLS + HALO, row.astype(jnp.float32))
    left_two = jnp.where(left_wide == 1, from_left_far_ref[0:near, :], from_left_ref[NEAR : NEAR + near, :])
    right_two = jnp.where(right_wide == 1, from_right_far_ref[0:near, :], from_right_ref[NEAR : NEAR + near, :])
    put_strided(coarse_ref, 0, EXT_COLS, left_two.astype(jnp.float32))
    put_strided(coarse_ref, 1, EXT_COLS, from_left_ref[0:near, :].astype(jnp.float32))
    put_strided(coarse_ref, wide + 2, EXT_COLS, from_right_ref[0:near, :].astype(jnp.float32))
    put_strided(coarse_ref, wide + 3, EXT_COLS, right_two.astype(jnp.float32))
    for side, ref in ((core, mine_ref), (1 - core, other_ref)):
        for i in range(TILE_ROWS):
            put_rows(half_ref, i * HALF, get_rows(coarse_ref, (2 * TILE_ROWS + i) * EXT_COLS + side * HALF, HALF))
        half_ref[:, TILE_ROWS * HALF : TALL_TILE, :] = jnp.zeros((3, TALL_TILE - TILE_ROWS * HALF, 128), jnp.float32)
        ref[...] = get_rows(half_ref, 0, TALL_TILE).astype(jnp.bfloat16)
    for i in range(2 * TILE_ROWS):
        prior_ref[i] = get_rows(coarse_ref, i * EXT_COLS, EXT_COLS).astype(jnp.bfloat16)
    for c in range(FINE_COLS + 1, FINE_PITCH):
        put_strided(fine_ref, c, FINE_PITCH, jnp.zeros((fine, 384), jnp.float32))
    for f in range(2):

        def copy_fine(i, carry):
            put_rows(fine_ref, (f * FINE_ROWS + i) * FINE_PITCH + 1, two_ref[f, i].astype(jnp.float32))
            return carry

        lax.fori_loop(0, FINE_ROWS, copy_fine, 0)
    put_strided(fine_ref, 0, FINE_PITCH, from_left_ref[2 * NEAR : 2 * NEAR + fine, :].astype(jnp.float32))
    put_strided(fine_ref, 2 * wide + 1, FINE_PITCH, from_right_ref[2 * NEAR : 2 * NEAR + fine, :].astype(jnp.float32))

    def write_fine(i, carry):
        fine_out_ref[i] = get_rows(fine_ref, pl.multiple_of(i * FINE_PITCH, 8), FINE_PITCH).astype(jnp.bfloat16)
        return carry

    lax.fori_loop(0, fine, write_fine, 0)
    for f in range(2):
        base = f * TILE_ROWS
        last = prior_ref[base + tall - 1]
        down_ref[f] = last
        down_ref[2 + f] = prior_ref[base + jnp.maximum(tall - 2, 0)]
        down_far_ref[f] = last
        up_ref[f] = prior_ref[base]
        up_ref[2 + f] = prior_ref[base + 1]
        up_far_ref[f] = prior_ref[base]
        bottom = fine_out_ref[f * FINE_ROWS + 2 * tall - 1]
        top = fine_out_ref[f * FINE_ROWS]
        for h in range(2):
            down_ref[4 + 2 * f + h] = bottom[h * 24 : (h + 1) * 24]
            up_ref[4 + 2 * f + h] = top[h * 24 : (h + 1) * 24]


def prior_kernel(
    place_ref, row_ref, prior_ref, fine_ref, from_up_ref, from_down_ref, from_up_far_ref, from_down_far_ref, one_ref, two_ref,
    sum_one_ref, sum_two_ref, phase_ref, coarse_ref, wide_ref, part_ref, weight_one_ref, weight_two_ref, sem_ref,
):
    fetch_one = pltpu.make_async_copy(one_ref.at[pl.ds(0, 2)], weight_one_ref, sem_ref.at[0])
    fetch_two = pltpu.make_async_copy(two_ref, weight_two_ref, sem_ref.at[1])
    fetch_one.start()
    fetch_two.start()
    tall = row_ref[place_ref[0]]
    up_tall = size_at(row_ref, place_ref[0] - 1)
    down_tall = size_at(row_ref, place_ref[0] + 1)
    for f in range(2):
        coarse_ref[f, 0] = jnp.where(up_tall == 1, from_up_far_ref[f], from_up_ref[2 + f])
        coarse_ref[f, 1] = from_up_ref[f]
        for i in range(TILE_ROWS):
            coarse_ref[f, HALO + i] = prior_ref[f * TILE_ROWS + i]
        for i in (TILE_ROWS + 2, TILE_ROWS + 3):
            coarse_ref[f, i] = jnp.zeros((EXT_COLS, 384), jnp.bfloat16)
        coarse_ref[f, tall + 2] = from_down_ref[f]
        coarse_ref[f, tall + 3] = jnp.where(down_tall == 1, from_down_far_ref[f], from_down_ref[2 + f])
        wide_ref[f, 0] = jnp.concatenate([from_up_ref[4 + 2 * f], from_up_ref[5 + 2 * f]], axis=0)

        def copy_fine(i, carry):
            wide_ref[f, 1 + i] = fine_ref[f * FINE_ROWS + i]
            return carry

        lax.fori_loop(0, FINE_ROWS, copy_fine, 0)
        wide_ref[f, FINE_ROWS + 1] = jnp.zeros((FINE_PITCH, 384), jnp.bfloat16)
        wide_ref[f, 2 * tall + 1] = jnp.concatenate([from_down_ref[4 + 2 * f], from_down_ref[5 + 2 * f]], axis=0)
    fetch_one.wait()
    sum_one_ref[...] = coarse_conv(lambda f, a, n: coarse_ref[f, a : a + n], weight_one_ref, part_ref, 2)
    fetch_two.wait()
    for r in range(0, FINE_ROWS, FINE_STEP):
        sum_two_ref[r * FINE_PITCH : (r + FINE_STEP) * FINE_PITCH, :] = fine_conv(
            lambda f, a, n: wide_ref[f, r + a : r + a + n], weight_two_ref, part_ref, 2
        )
    taps = ((0,), (1, 2), (0, 1), (2,))
    for u in range(4):
        rows = []
        for b in range(3):
            tap = sum(weight_two_ref[2, a, b].astype(jnp.float32) for a in taps[u])
            rows.append(tap)
        for v in range(4):
            phase_ref[u, v] = sum(rows[b] for b in taps[v]).astype(jnp.bfloat16)


def coarse_conv(rows_of, weight_ref, part_ref, depth):
    rows = TILE_ROWS + 2
    taps = [(f, a) for f in range(depth) for a in range(3)]
    left = jnp.concatenate([rows_of(f, a, rows).reshape(rows * EXT_COLS, 384) for f, a in taps], axis=1)
    right = jnp.concatenate([jnp.concatenate([weight_ref[f, a, b] for b in range(3)], axis=1) for f, a in taps], axis=0)
    product = jnp.dot(left, right, preferred_element_type=jnp.float32)
    return shifted_sum([product[:, b * 384 : (b + 1) * 384] for b in range(3)], part_ref)


def fine_conv(rows_of, weight_ref, part_ref, depth):
    taps = [(f, a) for f in range(depth) for a in range(3)]
    left = jnp.concatenate([rows_of(f, a, FINE_STEP).reshape(FINE_STEP * FINE_PITCH, 384) for f, a in taps], axis=1)
    products = [
        lax.dot_general(
            left, jnp.concatenate([weight_ref[f, a, b] for f, a in taps], axis=1), (((1,), (1,)), ((), ())),
            preferred_element_type=jnp.float32,
        )
        for b in range(3)
    ]
    return shifted_sum(products, part_ref)


def shifted_sum(products, part_ref):
    total = products[0]
    count, width = total.shape
    groups = -(-width // 128)
    for b in (1, 2):
        for g in range(groups):
            hi = min((g + 1) * 128, width)
            part_ref[g, 0:count, 0 : hi - g * 128] = products[b][:, g * 128 : hi]
        moved = jnp.concatenate([part_ref[g, b : b + count, :] for g in range(groups)], axis=1)
        total = total + moved[:, 0:width]
    return total


def query_kernel(
    place_ref, row_ref, own_ref, one_ref, two_ref, three_ref, gain_ref, qw_ref, kw_ref, query_ref, frame_ref, frame_other_ref, wide_ref, *, scale
):
    y_at = place_ref[0] // 2
    wide_ref[...] = jnp.zeros_like(wide_ref)
    slot = lax.broadcasted_iota(jnp.int32, (TALL_TILE, 128), 0)
    for k, ref in enumerate((own_ref, one_ref, two_ref, three_ref)):
        source = jnp.bitwise_and(y_at - k, 3)
        for t in range(2):
            start = FRONT + before(row_ref, 2 * source + t) * HALF
            usable = slot < row_ref[2 * source + t] * HALF
            part = ref[t].astype(jnp.float32)
            for g in range(3):
                held = wide_ref[g, pl.ds(start, TALL_TILE), :]
                wide_ref[g, pl.ds(start, TALL_TILE), :] = jnp.where(usable, part[:, g * 128 : (g + 1) * 128], held)
    count = LAT_ROWS * HALF
    frame_ref[...] = get_rows(wide_ref, before(row_ref, place_ref[0]) * HALF, HALF_ROWS).astype(jnp.bfloat16)
    sibling = place_ref[0] + 1 - 2 * place_ref[2]
    frame_other_ref[...] = get_rows(wide_ref, before(row_ref, sibling) * HALF, HALF_ROWS).astype(jnp.bfloat16)
    step = count // 3
    for i in range(3):
        raw = get_rows(wide_ref, FRONT + i * step, step)
        normed = rms_scale(raw, gain_ref[...][None]).astype(jnp.bfloat16)
        query = jnp.dot(normed, qw_ref[...], preferred_element_type=jnp.float32).astype(jnp.bfloat16)
        turned = lax.dot_general(query, kw_ref[...], (((1,), (1,)), ((), ())), preferred_element_type=jnp.float32)
        query_ref[i * step : (i + 1) * step, :] = (turned * scale).astype(jnp.bfloat16)


def attention_kernel(
    place_ref, row_ref, col_ref, query_ref, tile_ref, out_ref,
    stage_ref, key_ref, bias_ref, score_ref, top_ref, sum_ref, acc_ref, wide_ref, stat_ref, offset_ref, sem_ref,
):
    tiles = tile_ref.shape[0]
    group = tiles // KEY_GROUPS
    fetches = [
        pltpu.make_async_copy(tile_ref.at[pl.ds(n * group, group)], stage_ref.at[pl.ds(n * group, group)], sem_ref.at[n])
        for n in range(KEY_GROUPS)
    ]
    fetches[0].start()
    cols = col_ref.shape[0]
    y_at = place_ref[0] // 2
    spot = lax.broadcasted_iota(jnp.int32, (8, KEY_CHUNK), 0) * KEY_CHUNK + lax.broadcasted_iota(jnp.int32, (8, KEY_CHUNK), 1)

    def locate(t, carry):
        offset, bias = carry
        offset_ref[t] = offset
        count = row_ref[2 * y_at + t // cols] * col_ref[t % cols]
        bias = jnp.where((spot >= offset) & (spot < offset + count), 0.0, bias)
        return offset + (count + 15) // 16 * 16, bias

    tail, bias = lax.fori_loop(0, tiles, locate, (jnp.int32(0), jnp.full((8, KEY_CHUNK), masked_score, jnp.float32)))
    offset_ref[tiles] = tail
    for j in range(MAX_CHUNKS):
        bias_ref[j] = bias[j : j + 1, :]
    chunk_count = (tail + KEY_CHUNK - 1) // KEY_CHUNK

    def gather(t, carry):
        key_ref[pl.ds(pl.multiple_of(offset_ref[t], 16), KEY_TILE), :] = stage_ref[t]
        return carry

    total = wide_ref.shape[1]
    count = query_ref.shape[0]
    wide_ref[:, 0:FRONT, :] = jnp.zeros((3, FRONT, 128), jnp.float32)
    wide_ref[:, FRONT + count : total, :] = jnp.zeros((3, total - FRONT - count, 128), jnp.float32)
    stat_ref[0:FRONT, :] = jnp.zeros((FRONT, 128), jnp.float32)
    stat_ref[FRONT + count : total, :] = jnp.zeros((total - FRONT - count, 128), jnp.float32)
    lane_groups = KEY_CHUNK // 128

    def keys_at(j):
        return key_ref[pl.ds(pl.multiple_of(j * KEY_CHUNK, KEY_CHUNK), KEY_CHUNK), :]

    def score_step(i, j):
        slot = 0
        query = query_ref[i * QUERY_BLOCK : (i + 1) * QUERY_BLOCK, :]
        s = lax.dot_general(query, keys_at(j), (((1,), (1,)), ((), ())), preferred_element_type=jnp.float32)
        s = s + bias_ref[j]
        score_ref[slot, j] = s
        best = s[:, 0:128]
        for g in range(1, lane_groups):
            best = jnp.maximum(best, s[:, g * 128 : (g + 1) * 128])
        top_ref[slot] = jnp.maximum(top_ref[slot], best)

    def value_step(i, j):
        slot = 0
        top = top_ref[slot]
        p = jnp.exp2(score_ref[slot, j] - jnp.concatenate([top] * lane_groups, axis=1))
        part = p[:, 0:128]
        for g in range(1, lane_groups):
            part = part + p[:, g * 128 : (g + 1) * 128]
        sum_ref[...] = sum_ref[...] + part
        acc_ref[...] = acc_ref[...] + jnp.dot(p.astype(jnp.bfloat16), keys_at(j), preferred_element_type=jnp.float32)

    top_ref[0] = jnp.full((QUERY_BLOCK, 128), masked_score, jnp.float32)
    done = jnp.int32(0)
    for n in range(KEY_GROUPS):
        fetches[n].wait()
        if n + 1 < KEY_GROUPS:
            fetches[n + 1].start()
        lax.fori_loop(n * group, (n + 1) * group, gather, 0)
        if n + 1 == KEY_GROUPS:
            key_ref[pl.ds(pl.multiple_of(tail, 16), KEY_CHUNK), :] = jnp.zeros((KEY_CHUNK, key_ref.shape[1]), jnp.bfloat16)
            ready = chunk_count
        else:
            ready = offset_ref[(n + 1) * group] // KEY_CHUNK

        def score_chunk(j, carry):
            score_step(0, j)
            return carry

        lax.fori_loop(done, ready, score_chunk, 0)
        done = ready
    best = jnp.max(top_ref[0], axis=1, keepdims=True)
    top_ref[0] = jnp.broadcast_to(best, (QUERY_BLOCK, 128))
    sum_ref[...] = jnp.zeros_like(sum_ref)
    acc_ref[...] = jnp.zeros_like(acc_ref)

    def value_chunk(j, carry):
        value_step(0, j)
        return carry

    def value_pair(j, carry):
        value_step(0, 2 * j)
        value_step(0, 2 * j + 1)
        return carry

    lax.fori_loop(0, chunk_count // 2, value_pair, 0)

    @pl.when(chunk_count % 2 == 1)
    def _():
        value_step(0, chunk_count - 1)

    denominator = jnp.sum(sum_ref[...], axis=1, keepdims=True)
    put_rows(wide_ref, FRONT, acc_ref[...] / denominator)
    level = top_ref[0] + jnp.log2(jnp.broadcast_to(denominator, (QUERY_BLOCK, 128)))
    high = level.astype(jnp.bfloat16).astype(jnp.float32)
    mid = (level - high).astype(jnp.bfloat16).astype(jnp.float32)
    low = level - high - mid
    lane = lax.broadcasted_iota(jnp.int32, (QUERY_BLOCK, 128), 1)
    packed = jnp.where(lane == 0, high, jnp.where(lane == 1, mid, jnp.where(lane == 2, low, 0.0)))
    stat_ref[FRONT : FRONT + QUERY_BLOCK, :] = packed
    body = HALF_ROWS - 16
    select = (
        lax.broadcasted_iota(jnp.int32, (16, 128), 0) - STAT_ROW == lax.broadcasted_iota(jnp.int32, (16, 128), 1)
    ).astype(jnp.bfloat16)
    is_stat = lax.broadcasted_iota(jnp.int32, (16, 384), 0) >= STAT_ROW
    for b in range(out_ref.shape[0]):
        offset = before(row_ref, b) * HALF
        out_ref[b, 0:body, :] = get_rows(wide_ref, offset, body).astype(jnp.bfloat16)
        levels = stat_ref[pl.ds(offset, 384), :].astype(jnp.bfloat16)
        levels = lax.dot_general(select, levels, (((1,), (1,)), ((), ())), preferred_element_type=jnp.float32)
        last = jnp.where(is_stat, levels, get_rows(wide_ref, offset + body, 16))
        out_ref[b, body:HALF_ROWS, :] = last.astype(jnp.bfloat16)


def finish_kernel(
    place_ref, row_ref, col_ref, parts_ref, mine_ref, other_ref, vw_ref, ow_ref, gain_one_ref, sum_one_ref, sum_two_ref, one_ref, two_ref,
    gain_two_ref, out_ref, part_ref, act_ref, first_ref, shift_ref, product_ref, fine_ref, weight_one_ref, phase_ref, sem_ref,
):
    fetch_part = pltpu.make_async_copy(parts_ref, part_ref, sem_ref.at[2])
    fetch_part.start()
    fetch_one = pltpu.make_async_copy(one_ref.at[pl.ds(2, 1)], weight_one_ref, sem_ref.at[0])
    fetch_two = pltpu.make_async_copy(two_ref, phase_ref, sem_ref.at[1])
    fetch_one.start()
    fetch_two.start()
    core = place_ref[2]
    tall = row_ref[place_ref[0]]
    wide = col_ref[place_ref[1]]
    groups = part_ref.shape[0]
    stat = lax.broadcasted_iota(jnp.int32, (16 * groups, 128 * groups), 0)
    owner = jnp.right_shift(lax.broadcasted_iota(jnp.int32, (16 * groups, 128 * groups), 1), 7)
    within = stat - owner * 16
    ones = ((within >= STAT_ROW) & (within < STAT_ROW + 3)).astype(jnp.bfloat16)
    fetch_part.wait()
    stacked = jnp.concatenate([part_ref[g, HALF_ROWS - 16 : HALF_ROWS, 0:256] for g in range(groups)], axis=0)
    spread = lax.dot_general(stacked, ones, (((0,), (0,)), ((), ())), preferred_element_type=jnp.float32)
    halves = []
    for side in range(2):
        sources = range(side, part_ref.shape[0], 2)
        levels = [spread[0:HALF_ROWS, g * 128 : (g + 1) * 128] for g in sources]
        best = jnp.maximum(jnp.maximum(levels[0], levels[1]), jnp.maximum(levels[2], levels[3]))
        weights = [jnp.exp2(level - best) for level in levels]
        total = (weights[0] + weights[1]) + (weights[2] + weights[3])
        merged = None
        for weight, g in zip(weights, sources):
            share = weight / total
            term = part_ref[g, 0:HALF_ROWS, :].astype(jnp.float32) * jnp.concatenate([share] * 3, axis=1)
            merged = term if merged is None else merged + term
        halves.append(merged.astype(jnp.bfloat16))
    merged = jnp.concatenate(halves, axis=0)
    attention = jnp.dot(merged, vw_ref[...], preferred_element_type=jnp.float32).astype(jnp.bfloat16)
    projected = jnp.dot(attention, ow_ref[...], preferred_element_type=jnp.float32)
    mine = mine_ref[...].astype(jnp.float32)
    other = other_ref[...].astype(jnp.float32)
    frame = jnp.concatenate([jnp.where(core == 0, mine, other), jnp.where(core == 0, other, mine)], axis=0)
    mixed = (frame + projected).astype(jnp.bfloat16)
    put_rows(shift_ref, 0, silu(rms_scale(mixed, gain_one_ref[...][None])))
    row_start = before(row_ref, place_ref[0])
    col_start = before(col_ref, place_ref[1])
    for side in range(2):
        for i in range(EXT_ROWS):
            put_rows(act_ref, i * EXT_COLS + side * HALF, get_rows(shift_ref, side * HALF_ROWS + i * HALF, HALF))
    at_col = col_start - HALO + lax.broadcasted_iota(jnp.int32, (EXT_COLS, 384), 0)
    col_inside = (at_col >= 0) & (at_col < LAT_COLS)
    for i in range(EXT_ROWS):
        at_row = row_start - HALO + i
        inside = col_inside & (at_row >= 0) & (at_row < LAT_ROWS)
        first_ref[i] = jnp.where(inside, get_rows(act_ref, i * EXT_COLS, EXT_COLS), 0.0).astype(jnp.bfloat16)
    rows = TILE_ROWS + 2
    fetch_one.wait()
    total = coarse_conv(lambda f, a, n: first_ref[a : a + n], weight_one_ref, shift_ref, 1)
    y_one = (total + sum_one_ref[...]).astype(jnp.bfloat16)
    act = silu(rms_scale(y_one, gain_two_ref[...][None])).astype(jnp.bfloat16).astype(jnp.float32)
    put_rows(act_ref, 0, act)
    at_col = col_start - 1 + lax.broadcasted_iota(jnp.int32, (EXT_COLS, 384), 0)
    col_inside = (at_col >= 0) & (at_col < LAT_COLS)
    for i in range(rows):
        at_row = row_start - 1 + i
        inside = col_inside & (at_row >= 0) & (at_row < LAT_ROWS)
        first_ref[i] = jnp.where(inside, get_rows(act_ref, i * EXT_COLS, EXT_COLS), 0.0).astype(jnp.bfloat16)
    fetch_two.wait()
    count = TILE_ROWS * EXT_COLS
    for p in range(2):
        left = jnp.concatenate(
            [first_ref[p + u : p + u + TILE_ROWS].reshape(count, 384) for u in range(2)], axis=1
        )
        for q in range(2):
            for v in range(2):
                right = jnp.concatenate([phase_ref[2 * p + u, 2 * q + v] for u in range(2)], axis=1)
                product = lax.dot_general(left, right, (((1,), (1,)), ((), ())), preferred_element_type=jnp.float32)
                product_ref[2 * q + v, 0, 0:count, :] = product[:, 0:128]
                product_ref[2 * q + v, 1, 0:count, 0:64] = product[:, 128:192]
            for i in range(TILE_ROWS):
                for g in range(2):
                    near = product_ref[2 * q, g, pl.ds(i * EXT_COLS + q, EXT_COLS), :]
                    next_ = product_ref[2 * q + 1, g, pl.ds(i * EXT_COLS + q + 1, EXT_COLS), :]
                    fine_ref[g, pl.ds((2 * i + p) * FINE_PITCH + q, EXT_COLS, 2), :] = near + next_
    col = lax.broadcasted_iota(jnp.int32, (FINE_COLS, 192), 0)
    for r in range(FINE_ROWS):
        line = get_rows(fine_ref, r * FINE_PITCH, FINE_COLS)[:, 0:192] + sum_two_ref[r * FINE_PITCH : r * FINE_PITCH + FINE_COLS, :]
        usable = (col < 2 * wide) & (r < 2 * tall)
        out_ref[r] = jnp.where(usable, line, 0.0).astype(jnp.bfloat16)


def call(body, inputs, outs, scratch, smem_count, name, flops=0, far=()):
    smem = pl.BlockSpec(memory_space=pltpu.SMEM)
    vmem = pl.BlockSpec(memory_space=pltpu.VMEM)
    moved = sum(math.prod(v.shape) * v.dtype.itemsize for v in list(inputs) + list(outs))
    return pl.pallas_call(
        body,
        in_specs=[
            smem if i < smem_count else pl.BlockSpec(memory_space=pl.ANY) if i in far else vmem for i in range(len(inputs))
        ],
        out_specs=[vmem] * len(outs),
        out_shape=outs,
        scratch_shapes=scratch,
        compiler_params=pltpu.CompilerParams(vmem_limit_bytes=VMEM_BYTES),
        cost_estimate=pl.CostEstimate(flops=int(flops), transcendentals=0, bytes_accessed=int(moved)),
        name=name,
    )(*inputs)


def attend(place, row_sizes, col_sizes, queries, tiles):
    channels = queries.shape[1]
    scratch = lambda *dims: pltpu.VMEM(dims, jnp.float32)
    (parts,) = call(
        attention_kernel,
        [place, row_sizes, col_sizes, queries, tiles],
        [jax.ShapeDtypeStruct((8, HALF_ROWS, channels), jnp.bfloat16)],
        [
            pltpu.VMEM(tiles.shape, jnp.bfloat16), pltpu.VMEM((KEY_ROWS, channels), jnp.bfloat16),
            scratch(MAX_CHUNKS, 1, KEY_CHUNK), scratch(1, MAX_CHUNKS, QUERY_BLOCK, KEY_CHUNK),
            scratch(1, QUERY_BLOCK, 128), scratch(QUERY_BLOCK, 128), scratch(QUERY_BLOCK, channels),
            scratch(3, WIDE_ROWS, 128), scratch(WIDE_ROWS, 128), pltpu.SMEM((tiles.shape[0] + 1,), jnp.int32),
            pltpu.SemaphoreType.DMA((KEY_GROUPS,)),
        ],
        3, "attention", 4 * LAT_ROWS * HALF * channels * KEY_ROWS, (4,),
    )
    return parts


def local(
    tokens, row_sizes, col_sizes, norm_gain, query_weight, key_weight, value_weight, out_weight,
    cache_one, gain_one, conv_one, cache_two, gain_two, conv_two,
):
    channels = tokens.shape[2]
    n_row = row_sizes.shape[0]
    n_col = col_sizes.shape[0]
    n_y = lax.axis_size("y")
    core = lax.axis_index("core")
    row_at = lax.axis_index("y") * lax.axis_size("core") + core
    col_at = lax.axis_index("x") * lax.axis_size("z") + lax.axis_index("z")
    place = jnp.stack([row_at, col_at, core]).astype(jnp.int32)
    shape = lambda *dims: jax.ShapeDtypeStruct(dims, jnp.bfloat16)
    wide_shape = lambda *dims: jax.ShapeDtypeStruct(dims, jnp.float32)
    scratch = lambda *dims: pltpu.VMEM(dims, jnp.float32)
    narrow = lambda *dims: pltpu.VMEM(dims, jnp.bfloat16)
    message = 160
    place_args = [place, row_sizes, col_sizes]
    (own_keys,) = call(
        keys_kernel, [col_sizes, tokens, norm_gain], [shape(KEY_TILE, channels)], [scratch(3, 304, 128)], 1, "keys"
    )
    tiles = lax.all_gather(own_keys, ("core", "x", "z"), axis=0, tiled=False)
    to_right, to_left, to_right_far, to_left_far = call(
        edges_kernel,
        [*place_args, tokens, cache_one, cache_two],
        [shape(message, channels), shape(message, channels), shape(NEAR, channels), shape(NEAR, channels)],
        [scratch(3, 3 * TILE_ROWS * 24, 128), scratch(3, 2 * FINE_ROWS * FINE_COLS, 128)],
        3, "edges",
    )
    from_left = hop(to_right, COLS, n_col, 1)
    from_right = hop(to_left, COLS, n_col, -1)
    from_left_far, from_right_far = far_hops(jnp.any(col_sizes == 1), to_right_far, to_left_far, COLS, n_col)
    mine, other, prior, fine, down, up, down_far, up_far = call(
        columns_kernel,
        [*place_args, tokens, cache_one, cache_two, from_left, from_right, from_left_far, from_right_far],
        [
            shape(TALL_TILE, channels), shape(TALL_TILE, channels), shape(2 * TILE_ROWS, EXT_COLS, channels),
            shape(2 * FINE_ROWS, FINE_PITCH, channels), shape(8, EXT_COLS, channels), shape(8, EXT_COLS, channels),
            shape(2, EXT_COLS, channels), shape(2, EXT_COLS, channels),
        ],
        [scratch(3, 3 * TILE_ROWS * EXT_COLS, 128), scratch(3, 2 * FINE_ROWS * FINE_PITCH, 128), scratch(3, TALL_TILE, 128)],
        3, "columns",
    )
    swap = [(0, 1), (1, 0)]
    sibling = lax.ppermute(other, "core", swap)
    pair = jnp.where(core == 0, jnp.stack([mine, sibling]), jnp.stack([sibling, mine]))
    strips = [pair] + [lax.ppermute(pair, "y", [(i, (i + k) % n_y) for i in range(n_y)]) for k in range(1, n_y)]
    around = [hop(down, ROWS, n_row, 1), hop(up, ROWS, n_row, -1)]
    around += far_hops(jnp.any(row_sizes == 1), down_far, up_far, ROWS, n_row)
    strips, around = lax.optimization_barrier((strips, around))
    scale = math.log2(math.e) / math.sqrt(channels)

    def query_body(*refs):
        query_kernel(*refs, scale=scale)

    queries, frame, frame_other = call(
        query_body,
        [place, row_sizes, *strips, norm_gain, query_weight, key_weight],
        [shape(LAT_ROWS * HALF, channels), shape(HALF_ROWS, channels), shape(HALF_ROWS, channels)],
        [scratch(3, WIDE_ROWS, 128)],
        2, "queries", 4 * LAT_ROWS * HALF * channels * channels,
    )
    frame_other = lax.ppermute(frame_other, "core", swap)
    parts = attend(place, row_sizes, col_sizes, queries, tiles.reshape(2 * n_col, KEY_TILE, channels))
    parts = lax.all_to_all(parts, ROWS, 0, 0)
    conv_two = jnp.swapaxes(conv_two, 3, 4)
    channels_out = conv_two.shape[3]
    sum_one, sum_two, phases = call(
        prior_kernel,
        [place, row_sizes, prior, fine, *around, conv_one, conv_two],
        [
            wide_shape((TILE_ROWS + 2) * EXT_COLS, channels), wide_shape(FINE_ROWS * FINE_PITCH, channels_out),
            shape(4, 4, channels_out, channels),
        ],
        [
            narrow(2, EXT_ROWS, EXT_COLS, channels), narrow(2, FINE_ROWS + 2, FINE_PITCH, channels), scratch(3, 640, 128),
            narrow(2, 3, 3, channels, channels), narrow(3, 3, 3, channels_out, channels), pltpu.SemaphoreType.DMA((2,)),
        ],
        2, "prior", 2 * 18 * channels * (360 * 384 + 1248 * 192), (8, 9),
    )
    (decoded,) = call(
        finish_kernel,
        [
            *place_args, parts, frame, frame_other, value_weight, out_weight, gain_one, sum_one, sum_two, conv_one, phases, gain_two,
        ],
        [shape(FINE_ROWS, FINE_COLS, channels_out)],
        [
            narrow(8, HALF_ROWS, channels), scratch(3, EXT_ROWS * EXT_COLS, 128), narrow(EXT_ROWS, EXT_COLS, channels),
            scratch(3, 640, 128),
            scratch(4, 2, TILE_ROWS * EXT_COLS + 8, 128), scratch(2, FINE_ROWS * FINE_PITCH, 128),
            narrow(1, 3, 3, channels, channels), narrow(4, 4, channels_out, channels), pltpu.SemaphoreType.DMA((3,)),
        ],
        3, "finish", 0, (3, 11, 12),
    )
    return decoded


def solution(mesh):
    grid = Mesh(mesh.devices.reshape(4, 2, 4, 4), ("y", "core", "x", "z"))
    placed = (
        P(ROWS, COLS, None), P(), P(), P(), P(), P(), P(), P(),
        P(None, ROWS, COLS, None), P(), P(), P(None, ROWS, COLS, None), P(), P(),
    )
    return jax.shard_map(local, mesh=grid, in_specs=placed, out_specs=P(ROWS, COLS, None), check_vma=False)
```

```python
import math

import jax
import jax.numpy as jnp
from jax import lax
from jax.experimental import pallas as pl
from jax.experimental.pallas import tpu as pltpu
from jax.sharding import Mesh
from jax.sharding import PartitionSpec as P

epsilon = 1e-06
masked_score = -1e30
ROWS = ("y", "core")
COLS = ("x", "z")
LAT_ROWS = 88
LAT_COLS = 256
TILE_ROWS = 13
TILE_COLS = 20
HALO = 2
EXT_ROWS = TILE_ROWS + 2 * HALO
EXT_COLS = TILE_COLS + 2 * HALO
HALF = EXT_COLS // 2
FRONT = HALO * HALF
FINE_ROWS = 2 * TILE_ROWS
FINE_COLS = 2 * TILE_COLS
FINE_PITCH = 48
KEY_TILE = 272
KEY_CHUNK = 1024
KEY_GROUPS = 4
MAX_CHUNKS = 7
KEY_ROWS = MAX_CHUNKS * KEY_CHUNK + KEY_CHUNK
QUERY_BLOCK = 1056
HALF_ROWS = 208
STAT_ROW = EXT_ROWS * HALF - (HALF_ROWS - 16)
WIDE_ROWS = LAT_ROWS * HALF + 384
FINE_STEP = 13
TALL_TILE = 160
VMEM_BYTES = 60 * 1024 * 1024
SMALL_BYTES = VMEM_BYTES
NEAR = 48


def rms_scale(values_in, gain_vec):
    wide = values_in.astype(jnp.float32)
    return wide * lax.rsqrt(jnp.mean(wide * wide, axis=-1, keepdims=True) + epsilon) * gain_vec


def silu(v):
    return v / (1.0 + jnp.exp(-v))


def hop(value, axes, count, step):
    pairs = [(i, i + step) for i in range(count) if 0 <= i + step < count]
    return lax.ppermute(value, axes, pairs)


def far_hops(needed, ahead, back, axes, count):
    return lax.cond(
        needed,
        lambda a, b: [hop(a, axes, count, 2), hop(b, axes, count, -2)],
        lambda a, b: [a, b],
        ahead, back,
    )


def put_rows(ref, start, value):
    for g in range(ref.shape[0]):
        ref[g, pl.ds(start, value.shape[0]), :] = value[:, g * 128 : (g + 1) * 128].astype(ref.dtype)


def get_rows(ref, start, count, stride=None):
    return jnp.concatenate([ref[g, pl.ds(start, count, stride), :] for g in range(ref.shape[0])], axis=1)


def put_strided(ref, start, stride, value):
    for g in range(ref.shape[0]):
        ref[g, pl.ds(start, value.shape[0], stride), :] = value[:, g * 128 : (g + 1) * 128].astype(ref.dtype)


def before(size_ref, index):
    total = 0
    for t in range(size_ref.shape[0]):
        total = total + jnp.where(t < index, size_ref[t], 0)
    return total


def size_at(size_ref, index):
    count = size_ref.shape[0]
    inside = (index >= 0) & (index < count)
    return jnp.where(inside, size_ref[jnp.clip(index, 0, count - 1)], 0)


def keys_kernel(col_ref, token_ref, gain_ref, key_ref, pack_ref):
    wide = col_ref[lax.axis_index("x") * lax.axis_size("z") + lax.axis_index("z")]
    pack_ref[...] = jnp.zeros_like(pack_ref)
    gain = gain_ref[...][None]
    for i in range(TILE_ROWS):
        put_rows(pack_ref, i * wide, rms_scale(token_ref[i].astype(jnp.float32), gain))
    key_ref[...] = get_rows(pack_ref, 0, KEY_TILE).astype(jnp.bfloat16)


def edges_kernel(
    place_ref, row_ref, col_ref, token_ref, one_ref, two_ref, right_ref, left_ref, right_far_ref, left_far_ref, coarse_ref, fine_ref
):
    wide = col_ref[place_ref[1]]
    for f in range(3):
        for i in range(TILE_ROWS):
            row = one_ref[f, i] if f < 2 else token_ref[i]
            put_rows(coarse_ref, (f * TILE_ROWS + i) * 24, row.astype(jnp.float32))
    for f in range(2):

        def copy_fine(i, carry):
            put_rows(fine_ref, pl.multiple_of((f * FINE_ROWS + i) * FINE_COLS, 8), two_ref[f, i].astype(jnp.float32))
            return carry

        lax.fori_loop(0, FINE_ROWS, copy_fine, 0)
    near = 3 * TILE_ROWS
    fine = 2 * FINE_ROWS
    for ref in (right_ref, left_ref, right_far_ref, left_far_ref):
        ref[...] = jnp.zeros_like(ref)
    last = get_rows(coarse_ref, wide - 1, near, 24).astype(jnp.bfloat16)
    first = get_rows(coarse_ref, 0, near, 24).astype(jnp.bfloat16)
    right_ref[0:near, :] = last
    right_ref[NEAR : NEAR + near, :] = get_rows(coarse_ref, jnp.maximum(wide - 2, 0), near, 24).astype(jnp.bfloat16)
    right_ref[2 * NEAR : 2 * NEAR + fine, :] = get_rows(fine_ref, 2 * wide - 1, fine, FINE_COLS).astype(jnp.bfloat16)
    left_ref[0:near, :] = first
    left_ref[NEAR : NEAR + near, :] = get_rows(coarse_ref, 1, near, 24).astype(jnp.bfloat16)
    left_ref[2 * NEAR : 2 * NEAR + fine, :] = get_rows(fine_ref, 0, fine, FINE_COLS).astype(jnp.bfloat16)
    right_far_ref[0:near, :] = last
    left_far_ref[0:near, :] = first


def columns_kernel(
    place_ref, row_ref, col_ref, token_ref, one_ref, two_ref, from_left_ref, from_right_ref, from_left_far_ref, from_right_far_ref,
    mine_ref, other_ref, prior_ref, fine_out_ref, down_ref, up_ref, down_far_ref, up_far_ref, coarse_ref, fine_ref, half_ref,
):
    core = place_ref[2]
    tall = row_ref[place_ref[0]]
    wide = col_ref[place_ref[1]]
    left_wide = size_at(col_ref, place_ref[1] - 1)
    right_wide = size_at(col_ref, place_ref[1] + 1)
    near = 3 * TILE_ROWS
    fine = 2 * FINE_ROWS
    blank = jnp.zeros((near, 384), jnp.float32)
    put_strided(coarse_ref, EXT_COLS - 2, EXT_COLS, blank)
    put_strided(coarse_ref, EXT_COLS - 1, EXT_COLS, blank)
    for f in range(3):
        for i in range(TILE_ROWS):
            row = one_ref[f, i] if f < 2 else token_ref[i]
            put_rows(coarse_ref, (f * TILE_ROWS + i) * EXT_COLS + HALO, row.astype(jnp.float32))
    left_two = jnp.where(left_wide == 1, from_left_far_ref[0:near, :], from_left_ref[NEAR : NEAR + near, :])
    right_two = jnp.where(right_wide == 1, from_right_far_ref[0:near, :], from_right_ref[NEAR : NEAR + near, :])
    put_strided(coarse_ref, 0, EXT_COLS, left_two.astype(jnp.float32))
    put_strided(coarse_ref, 1, EXT_COLS, from_left_ref[0:near, :].astype(jnp.float32))
    put_strided(coarse_ref, wide + 2, EXT_COLS, from_right_ref[0:near, :].astype(jnp.float32))
    put_strided(coarse_ref, wide + 3, EXT_COLS, right_two.astype(jnp.float32))
    for side, ref in ((core, mine_ref), (1 - core, other_ref)):
        for i in range(TILE_ROWS):
            put_rows(half_ref, i * HALF, get_rows(coarse_ref, (2 * TILE_ROWS + i) * EXT_COLS + side * HALF, HALF))
        half_ref[:, TILE_ROWS * HALF : TALL_TILE, :] = jnp.zeros((3, TALL_TILE - TILE_ROWS * HALF, 128), jnp.float32)
        ref[...] = get_rows(half_ref, 0, TALL_TILE).astype(jnp.bfloat16)
    for i in range(2 * TILE_ROWS):
        prior_ref[i] = get_rows(coarse_ref, i * EXT_COLS, EXT_COLS).astype(jnp.bfloat16)
    for c in range(FINE_COLS + 1, FINE_PITCH):
        put_strided(fine_ref, c, FINE_PITCH, jnp.zeros((fine, 384), jnp.float32))
    for f in range(2):

        def copy_fine(i, carry):
            put_rows(fine_ref, (f * FINE_ROWS + i) * FINE_PITCH + 1, two_ref[f, i].astype(jnp.float32))
            return carry

        lax.fori_loop(0, FINE_ROWS, copy_fine, 0)
    put_strided(fine_ref, 0, FINE_PITCH, from_left_ref[2 * NEAR : 2 * NEAR + fine, :].astype(jnp.float32))
    put_strided(fine_ref, 2 * wide + 1, FINE_PITCH, from_right_ref[2 * NEAR : 2 * NEAR + fine, :].astype(jnp.float32))

    def write_fine(i, carry):
        fine_out_ref[i] = get_rows(fine_ref, pl.multiple_of(i * FINE_PITCH, 8), FINE_PITCH).astype(jnp.bfloat16)
        return carry

    lax.fori_loop(0, fine, write_fine, 0)
    for f in range(2):
        base = f * TILE_ROWS
        last = prior_ref[base + tall - 1]
        down_ref[f] = last
        down_ref[2 + f] = prior_ref[base + jnp.maximum(tall - 2, 0)]
        down_far_ref[f] = last
        up_ref[f] = prior_ref[base]
        up_ref[2 + f] = prior_ref[base + 1]
        up_far_ref[f] = prior_ref[base]
        bottom = fine_out_ref[f * FINE_ROWS + 2 * tall - 1]
        top = fine_out_ref[f * FINE_ROWS]
        for h in range(2):
            down_ref[4 + 2 * f + h] = bottom[h * 24 : (h + 1) * 24]
            up_ref[4 + 2 * f + h] = top[h * 24 : (h + 1) * 24]


def prior_kernel(
    place_ref, row_ref, prior_ref, fine_ref, from_up_ref, from_down_ref, from_up_far_ref, from_down_far_ref, one_ref, two_ref,
    sum_one_ref, sum_two_ref, phase_ref, coarse_ref, wide_ref, part_ref, weight_one_ref, weight_two_ref, sem_ref,
):
    fetch_one = pltpu.make_async_copy(one_ref.at[pl.ds(0, 2)], weight_one_ref, sem_ref.at[0])
    fetch_two = pltpu.make_async_copy(two_ref, weight_two_ref, sem_ref.at[1])
    fetch_one.start()
    fetch_two.start()
    tall = row_ref[place_ref[0]]
    up_tall = size_at(row_ref, place_ref[0] - 1)
    down_tall = size_at(row_ref, place_ref[0] + 1)
    for f in range(2):
        coarse_ref[f, 0] = jnp.where(up_tall == 1, from_up_far_ref[f], from_up_ref[2 + f])
        coarse_ref[f, 1] = from_up_ref[f]
        for i in range(TILE_ROWS):
            coarse_ref[f, HALO + i] = prior_ref[f * TILE_ROWS + i]
        for i in (TILE_ROWS + 2, TILE_ROWS + 3):
            coarse_ref[f, i] = jnp.zeros((EXT_COLS, 384), jnp.bfloat16)
        coarse_ref[f, tall + 2] = from_down_ref[f]
        coarse_ref[f, tall + 3] = jnp.where(down_tall == 1, from_down_far_ref[f], from_down_ref[2 + f])
        wide_ref[f, 0] = jnp.concatenate([from_up_ref[4 + 2 * f], from_up_ref[5 + 2 * f]], axis=0)

        def copy_fine(i, carry):
            wide_ref[f, 1 + i] = fine_ref[f * FINE_ROWS + i]
            return carry

        lax.fori_loop(0, FINE_ROWS, copy_fine, 0)
        wide_ref[f, FINE_ROWS + 1] = jnp.zeros((FINE_PITCH, 384), jnp.bfloat16)
        wide_ref[f, 2 * tall + 1] = jnp.concatenate([from_down_ref[4 + 2 * f], from_down_ref[5 + 2 * f]], axis=0)
    fetch_one.wait()
    sum_one_ref[...] = coarse_conv(lambda f, a, n: coarse_ref[f, a : a + n], weight_one_ref, part_ref, 2)
    fetch_two.wait()
    for r in range(0, FINE_ROWS, FINE_STEP):
        sum_two_ref[r * FINE_PITCH : (r + FINE_STEP) * FINE_PITCH, :] = fine_conv(
            lambda f, a, n: wide_ref[f, r + a : r + a + n], weight_two_ref, part_ref, 2
        )
    taps = ((0,), (1, 2), (0, 1), (2,))
    for u in range(4):
        rows = []
        for b in range(3):
            tap = sum(weight_two_ref[2, a, b].astype(jnp.float32) for a in taps[u])
            rows.append(tap)
        for v in range(4):
            phase_ref[u, v] = sum(rows[b] for b in taps[v]).astype(jnp.bfloat16)


def coarse_conv(rows_of, weight_ref, part_ref, depth):
    rows = TILE_ROWS + 2
    taps = [(f, a) for f in range(depth) for a in range(3)]
    left = jnp.concatenate([rows_of(f, a, rows).reshape(rows * EXT_COLS, 384) for f, a in taps], axis=1)
    right = jnp.concatenate([jnp.concatenate([weight_ref[f, a, b] for b in range(3)], axis=1) for f, a in taps], axis=0)
    product = jnp.dot(left, right, preferred_element_type=jnp.float32)
    return shifted_sum([product[:, b * 384 : (b + 1) * 384] for b in range(3)], part_ref)


def fine_conv(rows_of, weight_ref, part_ref, depth):
    taps = [(f, a) for f in range(depth) for a in range(3)]
    left = jnp.concatenate([rows_of(f, a, FINE_STEP).reshape(FINE_STEP * FINE_PITCH, 384) for f, a in taps], axis=1)
    products = [
        lax.dot_general(
            left, jnp.concatenate([weight_ref[f, a, b] for f, a in taps], axis=1), (((1,), (1,)), ((), ())),
            preferred_element_type=jnp.float32,
        )
        for b in range(3)
    ]
    return shifted_sum(products, part_ref)


def shifted_sum(products, part_ref):
    total = products[0]
    count, width = total.shape
    groups = -(-width // 128)
    for b in (1, 2):
        for g in range(groups):
            hi = min((g + 1) * 128, width)
            part_ref[g, 0:count, 0 : hi - g * 128] = products[b][:, g * 128 : hi]
        moved = jnp.concatenate([part_ref[g, b : b + count, :] for g in range(groups)], axis=1)
        total = total + moved[:, 0:width]
    return total


def query_kernel(
    place_ref, row_ref, own_ref, one_ref, two_ref, three_ref, gain_ref, qw_ref, kw_ref, query_ref, frame_ref, frame_other_ref, wide_ref, *, scale
):
    y_at = place_ref[0] // 2
    wide_ref[...] = jnp.zeros_like(wide_ref)
    slot = lax.broadcasted_iota(jnp.int32, (TALL_TILE, 128), 0)
    for k, ref in enumerate((own_ref, one_ref, two_ref, three_ref)):
        source = jnp.bitwise_and(y_at - k, 3)
        for t in range(2):
            start = FRONT + before(row_ref, 2 * source + t) * HALF
            usable = slot < row_ref[2 * source + t] * HALF
            part = ref[t].astype(jnp.float32)
            for g in range(3):
                held = wide_ref[g, pl.ds(start, TALL_TILE), :]
                wide_ref[g, pl.ds(start, TALL_TILE), :] = jnp.where(usable, part[:, g * 128 : (g + 1) * 128], held)
    count = LAT_ROWS * HALF
    frame_ref[...] = get_rows(wide_ref, before(row_ref, place_ref[0]) * HALF, HALF_ROWS).astype(jnp.bfloat16)
    sibling = place_ref[0] + 1 - 2 * place_ref[2]
    frame_other_ref[...] = get_rows(wide_ref, before(row_ref, sibling) * HALF, HALF_ROWS).astype(jnp.bfloat16)
    step = count // 3
    for i in range(3):
        raw = get_rows(wide_ref, FRONT + i * step, step)
        normed = rms_scale(raw, gain_ref[...][None]).astype(jnp.bfloat16)
        query = jnp.dot(normed, qw_ref[...], preferred_element_type=jnp.float32).astype(jnp.bfloat16)
        turned = lax.dot_general(query, kw_ref[...], (((1,), (1,)), ((), ())), preferred_element_type=jnp.float32)
        query_ref[i * step : (i + 1) * step, :] = (turned * scale).astype(jnp.bfloat16)


def attention_kernel(
    place_ref, row_ref, col_ref, query_ref, tile_ref, out_ref,
    stage_ref, key_ref, bias_ref, score_ref, top_ref, sum_ref, acc_ref, wide_ref, stat_ref, offset_ref, sem_ref,
):
    tiles = tile_ref.shape[0]
    group = tiles // KEY_GROUPS
    fetches = [
        pltpu.make_async_copy(tile_ref.at[pl.ds(n * group, group)], stage_ref.at[pl.ds(n * group, group)], sem_ref.at[n])
        for n in range(KEY_GROUPS)
    ]
    fetches[0].start()
    cols = col_ref.shape[0]
    y_at = place_ref[0] // 2
    spot = lax.broadcasted_iota(jnp.int32, (8, KEY_CHUNK), 0) * KEY_CHUNK + lax.broadcasted_iota(jnp.int32, (8, KEY_CHUNK), 1)

    def locate(t, carry):
        offset, bias = carry
        offset_ref[t] = offset
        count = row_ref[2 * y_at + t // cols] * col_ref[t % cols]
        bias = jnp.where((spot >= offset) & (spot < offset + count), 0.0, bias)
        return offset + (count + 15) // 16 * 16, bias

    tail, bias = lax.fori_loop(0, tiles, locate, (jnp.int32(0), jnp.full((8, KEY_CHUNK), masked_score, jnp.float32)))
    offset_ref[tiles] = tail
    for j in range(MAX_CHUNKS):
        bias_ref[j] = bias[j : j + 1, :]
    chunk_count = (tail + KEY_CHUNK - 1) // KEY_CHUNK

    def gather(t, carry):
        key_ref[pl.ds(pl.multiple_of(offset_ref[t], 16), KEY_TILE), :] = stage_ref[t]
        return carry

    total = wide_ref.shape[1]
    count = query_ref.shape[0]
    wide_ref[:, 0:FRONT, :] = jnp.zeros((3, FRONT, 128), jnp.float32)
    wide_ref[:, FRONT + count : total, :] = jnp.zeros((3, total - FRONT - count, 128), jnp.float32)
    stat_ref[0:FRONT, :] = jnp.zeros((FRONT, 128), jnp.float32)
    stat_ref[FRONT + count : total, :] = jnp.zeros((total - FRONT - count, 128), jnp.float32)
    lane_groups = KEY_CHUNK // 128

    def keys_at(j):
        return key_ref[pl.ds(pl.multiple_of(j * KEY_CHUNK, KEY_CHUNK), KEY_CHUNK), :]

    def score_step(i, j):
        slot = 0
        query = query_ref[i * QUERY_BLOCK : (i + 1) * QUERY_BLOCK, :]
        s = lax.dot_general(query, keys_at(j), (((1,), (1,)), ((), ())), preferred_element_type=jnp.float32)
        s = s + bias_ref[j]
        score_ref[slot, j] = s
        best = s[:, 0:128]
        for g in range(1, lane_groups):
            best = jnp.maximum(best, s[:, g * 128 : (g + 1) * 128])
        top_ref[slot] = jnp.maximum(top_ref[slot], best)

    def value_step(i, j):
        slot = 0
        top = top_ref[slot]
        p = jnp.exp2(score_ref[slot, j] - jnp.concatenate([top] * lane_groups, axis=1))
        part = p[:, 0:128]
        for g in range(1, lane_groups):
            part = part + p[:, g * 128 : (g + 1) * 128]
        sum_ref[...] = sum_ref[...] + part
        acc_ref[...] = acc_ref[...] + jnp.dot(p.astype(jnp.bfloat16), keys_at(j), preferred_element_type=jnp.float32)

    top_ref[0] = jnp.full((QUERY_BLOCK, 128), masked_score, jnp.float32)
    done = jnp.int32(0)
    for n in range(KEY_GROUPS):
        fetches[n].wait()
        if n + 1 < KEY_GROUPS:
            fetches[n + 1].start()
        lax.fori_loop(n * group, (n + 1) * group, gather, 0)
        if n + 1 == KEY_GROUPS:
            key_ref[pl.ds(pl.multiple_of(tail, 16), KEY_CHUNK), :] = jnp.zeros((KEY_CHUNK, key_ref.shape[1]), jnp.bfloat16)
            ready = chunk_count
        else:
            ready = offset_ref[(n + 1) * group] // KEY_CHUNK

        def score_chunk(j, carry):
            score_step(0, j)
            return carry

        lax.fori_loop(done, ready, score_chunk, 0)
        done = ready
    best = jnp.max(top_ref[0], axis=1, keepdims=True)
    top_ref[0] = jnp.broadcast_to(best, (QUERY_BLOCK, 128))
    sum_ref[...] = jnp.zeros_like(sum_ref)
    acc_ref[...] = jnp.zeros_like(acc_ref)

    def value_chunk(j, carry):
        value_step(0, j)
        return carry

    def value_pair(j, carry):
        value_step(0, 2 * j)
        value_step(0, 2 * j + 1)
        return carry

    lax.fori_loop(0, chunk_count // 2, value_pair, 0)

    @pl.when(chunk_count % 2 == 1)
    def _():
        value_step(0, chunk_count - 1)

    denominator = jnp.sum(sum_ref[...], axis=1, keepdims=True)
    put_rows(wide_ref, FRONT, acc_ref[...] / denominator)
    level = top_ref[0] + jnp.log2(jnp.broadcast_to(denominator, (QUERY_BLOCK, 128)))
    high = level.astype(jnp.bfloat16).astype(jnp.float32)
    mid = (level - high).astype(jnp.bfloat16).astype(jnp.float32)
    low = level - high - mid
    lane = lax.broadcasted_iota(jnp.int32, (QUERY_BLOCK, 128), 1)
    packed = jnp.where(lane == 0, high, jnp.where(lane == 1, mid, jnp.where(lane == 2, low, 0.0)))
    stat_ref[FRONT : FRONT + QUERY_BLOCK, :] = packed
    body = HALF_ROWS - 16
    select = (
        lax.broadcasted_iota(jnp.int32, (16, 128), 0) - STAT_ROW == lax.broadcasted_iota(jnp.int32, (16, 128), 1)
    ).astype(jnp.bfloat16)
    is_stat = lax.broadcasted_iota(jnp.int32, (16, 384), 0) >= STAT_ROW
    for b in range(out_ref.shape[0]):
        offset = before(row_ref, b) * HALF
        out_ref[b, 0:body, :] = get_rows(wide_ref, offset, body).astype(jnp.bfloat16)
        levels = stat_ref[pl.ds(offset, 384), :].astype(jnp.bfloat16)
        levels = lax.dot_general(select, levels, (((1,), (1,)), ((), ())), preferred_element_type=jnp.float32)
        last = jnp.where(is_stat, levels, get_rows(wide_ref, offset + body, 16))
        out_ref[b, body:HALF_ROWS, :] = last.astype(jnp.bfloat16)


def finish_kernel(
    place_ref, row_ref, col_ref, part_ref, mine_ref, other_ref, vw_ref, ow_ref, gain_one_ref, far_one_ref, far_two_ref, one_ref, two_ref,
    gain_two_ref, out_ref, act_ref, first_ref, shift_ref, product_ref, fine_ref, weight_one_ref, phase_ref, sum_one_ref, sum_two_ref, sem_ref,
):
    fetch_one = pltpu.make_async_copy(one_ref.at[pl.ds(2, 1)], weight_one_ref, sem_ref.at[0])
    fetch_two = pltpu.make_async_copy(two_ref, phase_ref, sem_ref.at[1])
    fetch_sum_one = pltpu.make_async_copy(far_one_ref, sum_one_ref, sem_ref.at[2])
    fetch_sum_two = pltpu.make_async_copy(far_two_ref, sum_two_ref, sem_ref.at[3])
    fetch_one.start()
    fetch_sum_one.start()
    fetch_two.start()
    fetch_sum_two.start()
    core = place_ref[2]
    tall = row_ref[place_ref[0]]
    wide = col_ref[place_ref[1]]
    groups = part_ref.shape[0]
    stat = lax.broadcasted_iota(jnp.int32, (16 * groups, 128 * groups), 0)
    owner = jnp.right_shift(lax.broadcasted_iota(jnp.int32, (16 * groups, 128 * groups), 1), 7)
    within = stat - owner * 16
    ones = ((within >= STAT_ROW) & (within < STAT_ROW + 3)).astype(jnp.bfloat16)
    stacked = jnp.concatenate([part_ref[g, HALF_ROWS - 16 : HALF_ROWS, 0:256] for g in range(groups)], axis=0)
    spread = lax.dot_general(stacked, ones, (((0,), (0,)), ((), ())), preferred_element_type=jnp.float32)
    halves = []
    for side in range(2):
        sources = range(side, part_ref.shape[0], 2)
        levels = [spread[0:HALF_ROWS, g * 128 : (g + 1) * 128] for g in sources]
        best = jnp.maximum(jnp.maximum(levels[0], levels[1]), jnp.maximum(levels[2], levels[3]))
        weights = [jnp.exp2(level - best) for level in levels]
        total = (weights[0] + weights[1]) + (weights[2] + weights[3])
        merged = None
        for weight, g in zip(weights, sources):
            share = weight / total
            term = part_ref[g, 0:HALF_ROWS, :].astype(jnp.float32) * jnp.concatenate([share] * 3, axis=1)
            merged = term if merged is None else merged + term
        halves.append(merged.astype(jnp.bfloat16))
    merged = jnp.concatenate(halves, axis=0)
    attention = jnp.dot(merged, vw_ref[...], preferred_element_type=jnp.float32).astype(jnp.bfloat16)
    projected = jnp.dot(attention, ow_ref[...], preferred_element_type=jnp.float32)
    mine = mine_ref[...].astype(jnp.float32)
    other = other_ref[...].astype(jnp.float32)
    frame = jnp.concatenate([jnp.where(core == 0, mine, other), jnp.where(core == 0, other, mine)], axis=0)
    mixed = (frame + projected).astype(jnp.bfloat16)
    put_rows(shift_ref, 0, silu(rms_scale(mixed, gain_one_ref[...][None])))
    row_start = before(row_ref, place_ref[0])
    col_start = before(col_ref, place_ref[1])
    for side in range(2):
        for i in range(EXT_ROWS):
            put_rows(act_ref, i * EXT_COLS + side * HALF, get_rows(shift_ref, side * HALF_ROWS + i * HALF, HALF))
    at_col = col_start - HALO + lax.broadcasted_iota(jnp.int32, (EXT_COLS, 384), 0)
    col_inside = (at_col >= 0) & (at_col < LAT_COLS)
    for i in range(EXT_ROWS):
        at_row = row_start - HALO + i
        inside = col_inside & (at_row >= 0) & (at_row < LAT_ROWS)
        first_ref[i] = jnp.where(inside, get_rows(act_ref, i * EXT_COLS, EXT_COLS), 0.0).astype(jnp.bfloat16)
    rows = TILE_ROWS + 2
    fetch_one.wait()
    total = coarse_conv(lambda f, a, n: first_ref[a : a + n], weight_one_ref, shift_ref, 1)
    fetch_sum_one.wait()
    y_one = (total + sum_one_ref[...]).astype(jnp.bfloat16)
    act = silu(rms_scale(y_one, gain_two_ref[...][None])).astype(jnp.bfloat16).astype(jnp.float32)
    put_rows(act_ref, 0, act)
    at_col = col_start - 1 + lax.broadcasted_iota(jnp.int32, (EXT_COLS, 384), 0)
    col_inside = (at_col >= 0) & (at_col < LAT_COLS)
    for i in range(rows):
        at_row = row_start - 1 + i
        inside = col_inside & (at_row >= 0) & (at_row < LAT_ROWS)
        first_ref[i] = jnp.where(inside, get_rows(act_ref, i * EXT_COLS, EXT_COLS), 0.0).astype(jnp.bfloat16)
    fetch_two.wait()
    count = TILE_ROWS * EXT_COLS
    for p in range(2):
        left = jnp.concatenate(
            [first_ref[p + u : p + u + TILE_ROWS].reshape(count, 384) for u in range(2)], axis=1
        )
        for q in range(2):
            for v in range(2):
                right = jnp.concatenate([phase_ref[2 * p + u, 2 * q + v] for u in range(2)], axis=1)
                product = lax.dot_general(left, right, (((1,), (1,)), ((), ())), preferred_element_type=jnp.float32)
                product_ref[2 * q + v, 0, 0:count, :] = product[:, 0:128]
                product_ref[2 * q + v, 1, 0:count, 0:64] = product[:, 128:192]
            for i in range(TILE_ROWS):
                for g in range(2):
                    near = product_ref[2 * q, g, pl.ds(i * EXT_COLS + q, EXT_COLS), :]
                    next_ = product_ref[2 * q + 1, g, pl.ds(i * EXT_COLS + q + 1, EXT_COLS), :]
                    fine_ref[g, pl.ds((2 * i + p) * FINE_PITCH + q, EXT_COLS, 2), :] = near + next_
    col = lax.broadcasted_iota(jnp.int32, (FINE_COLS, 192), 0)
    fetch_sum_two.wait()
    for r in range(FINE_ROWS):
        line = get_rows(fine_ref, r * FINE_PITCH, FINE_COLS)[:, 0:192] + sum_two_ref[r * FINE_PITCH : r * FINE_PITCH + FINE_COLS, :]
        usable = (col < 2 * wide) & (r < 2 * tall)
        out_ref[r] = jnp.where(usable, line, 0.0).astype(jnp.bfloat16)


def call(body, inputs, outs, scratch, smem_count, name, flops=0, far=(), near=(), limit=SMALL_BYTES):
    smem = pl.BlockSpec(memory_space=pltpu.SMEM)
    vmem = pl.BlockSpec(memory_space=pltpu.VMEM)
    moved = sum(math.prod(v.shape) * v.dtype.itemsize for v in list(inputs) + list(outs))
    return pl.pallas_call(
        body,
        in_specs=[
            smem if i < smem_count else pl.BlockSpec(memory_space=pl.ANY) if i in far else vmem for i in range(len(inputs))
        ],
        out_specs=[vmem] * len(outs),
        out_shape=outs,
        scratch_shapes=scratch,
        compiler_params=pltpu.CompilerParams(vmem_limit_bytes=limit),
        cost_estimate=pl.CostEstimate(flops=int(flops), transcendentals=0, bytes_accessed=int(moved)),
        name=name,
    )(*[pltpu.with_memory_space_constraint(v, pltpu.VMEM) if i in near else v for i, v in enumerate(inputs)])


def attend(place, row_sizes, col_sizes, queries, tiles):
    channels = queries.shape[1]
    scratch = lambda *dims: pltpu.VMEM(dims, jnp.float32)
    (parts,) = call(
        attention_kernel,
        [place, row_sizes, col_sizes, queries, tiles],
        [jax.ShapeDtypeStruct((8, HALF_ROWS, channels), jnp.bfloat16)],
        [
            pltpu.VMEM(tiles.shape, jnp.bfloat16), pltpu.VMEM((KEY_ROWS, channels), jnp.bfloat16),
            scratch(MAX_CHUNKS, 1, KEY_CHUNK), scratch(1, MAX_CHUNKS, QUERY_BLOCK, KEY_CHUNK),
            scratch(1, QUERY_BLOCK, 128), scratch(QUERY_BLOCK, 128), scratch(QUERY_BLOCK, channels),
            scratch(3, WIDE_ROWS, 128), scratch(WIDE_ROWS, 128), pltpu.SMEM((tiles.shape[0] + 1,), jnp.int32),
            pltpu.SemaphoreType.DMA((KEY_GROUPS,)),
        ],
        3, "attention", 4 * LAT_ROWS * HALF * channels * KEY_ROWS, (4,), (), VMEM_BYTES,
    )
    return parts


def local(
    tokens, row_sizes, col_sizes, norm_gain, query_weight, key_weight, value_weight, out_weight,
    cache_one, gain_one, conv_one, cache_two, gain_two, conv_two,
):
    channels = tokens.shape[2]
    n_row = row_sizes.shape[0]
    n_col = col_sizes.shape[0]
    n_y = lax.axis_size("y")
    core = lax.axis_index("core")
    row_at = lax.axis_index("y") * lax.axis_size("core") + core
    col_at = lax.axis_index("x") * lax.axis_size("z") + lax.axis_index("z")
    place = jnp.stack([row_at, col_at, core]).astype(jnp.int32)
    shape = lambda *dims: jax.ShapeDtypeStruct(dims, jnp.bfloat16)
    wide_shape = lambda *dims: jax.ShapeDtypeStruct(dims, jnp.float32)
    scratch = lambda *dims: pltpu.VMEM(dims, jnp.float32)
    narrow = lambda *dims: pltpu.VMEM(dims, jnp.bfloat16)
    message = 160
    place_args = [place, row_sizes, col_sizes]
    (own_keys,) = call(
        keys_kernel, [col_sizes, tokens, norm_gain], [shape(KEY_TILE, channels)], [scratch(3, 304, 128)], 1, "keys"
    )
    tiles = lax.all_gather(own_keys, ("core", "x", "z"), axis=0, tiled=False)
    to_right, to_left, to_right_far, to_left_far = call(
        edges_kernel,
        [*place_args, tokens, cache_one, cache_two],
        [shape(message, channels), shape(message, channels), shape(NEAR, channels), shape(NEAR, channels)],
        [scratch(3, 3 * TILE_ROWS * 24, 128), scratch(3, 2 * FINE_ROWS * FINE_COLS, 128)],
        3, "edges",
    )
    from_left = hop(to_right, COLS, n_col, 1)
    from_right = hop(to_left, COLS, n_col, -1)
    from_left_far, from_right_far = far_hops(jnp.any(col_sizes == 1), to_right_far, to_left_far, COLS, n_col)
    mine, other, prior, fine, down, up, down_far, up_far = call(
        columns_kernel,
        [*place_args, tokens, cache_one, cache_two, from_left, from_right, from_left_far, from_right_far],
        [
            shape(TALL_TILE, channels), shape(TALL_TILE, channels), shape(2 * TILE_ROWS, EXT_COLS, channels),
            shape(2 * FINE_ROWS, FINE_PITCH, channels), shape(8, EXT_COLS, channels), shape(8, EXT_COLS, channels),
            shape(2, EXT_COLS, channels), shape(2, EXT_COLS, channels),
        ],
        [scratch(3, 3 * TILE_ROWS * EXT_COLS, 128), scratch(3, 2 * FINE_ROWS * FINE_PITCH, 128), scratch(3, TALL_TILE, 128)],
        3, "columns", 0, (), (6, 7),
    )
    swap = [(0, 1), (1, 0)]
    sibling = lax.ppermute(other, "core", swap)
    pair = jnp.where(core == 0, jnp.stack([mine, sibling]), jnp.stack([sibling, mine]))
    strips = [pair] + [lax.ppermute(pair, "y", [(i, (i + k) % n_y) for i in range(n_y)]) for k in range(1, n_y)]
    around = [hop(down, ROWS, n_row, 1), hop(up, ROWS, n_row, -1)]
    around += far_hops(jnp.any(row_sizes == 1), down_far, up_far, ROWS, n_row)
    strips, around = lax.optimization_barrier((strips, around))
    scale = math.log2(math.e) / math.sqrt(channels)

    def query_body(*refs):
        query_kernel(*refs, scale=scale)

    queries, frame, frame_other = call(
        query_body,
        [place, row_sizes, *strips, norm_gain, query_weight, key_weight],
        [shape(LAT_ROWS * HALF, channels), shape(HALF_ROWS, channels), shape(HALF_ROWS, channels)],
        [scratch(3, WIDE_ROWS, 128)],
        2, "queries", 4 * LAT_ROWS * HALF * channels * channels, (), (2, 3, 4, 5),
    )
    frame_other = lax.ppermute(frame_other, "core", swap)
    parts = attend(place, row_sizes, col_sizes, queries, tiles.reshape(2 * n_col, KEY_TILE, channels))
    parts = lax.all_to_all(parts, ROWS, 0, 0)
    conv_two = jnp.swapaxes(conv_two, 3, 4)
    channels_out = conv_two.shape[3]
    sum_one, sum_two, phases = call(
        prior_kernel,
        [place, row_sizes, prior, fine, *around, conv_one, conv_two],
        [
            wide_shape((TILE_ROWS + 2) * EXT_COLS, channels), wide_shape(FINE_ROWS * FINE_PITCH, channels_out),
            shape(4, 4, channels_out, channels),
        ],
        [
            narrow(2, EXT_ROWS, EXT_COLS, channels), narrow(2, FINE_ROWS + 2, FINE_PITCH, channels), scratch(3, 640, 128),
            narrow(2, 3, 3, channels, channels), narrow(3, 3, 3, channels_out, channels), pltpu.SemaphoreType.DMA((2,)),
        ],
        2, "prior", 2 * 18 * channels * (360 * 384 + 1248 * 192), (8, 9), (4, 5),
    )
    (decoded,) = call(
        finish_kernel,
        [
            *place_args, parts, frame, frame_other, value_weight, out_weight, gain_one, sum_one, sum_two, conv_one, phases, gain_two,
        ],
        [shape(FINE_ROWS, FINE_COLS, channels_out)],
        [
            scratch(3, EXT_ROWS * EXT_COLS, 128), narrow(EXT_ROWS, EXT_COLS, channels),
            scratch(3, 640, 128),
            scratch(4, 2, TILE_ROWS * EXT_COLS + 8, 128), scratch(2, FINE_ROWS * FINE_PITCH, 128),
            narrow(1, 3, 3, channels, channels), narrow(4, 4, channels_out, channels),
            scratch((TILE_ROWS + 2) * EXT_COLS, channels), scratch(FINE_ROWS * FINE_PITCH, channels_out), pltpu.SemaphoreType.DMA((4,)),
        ],
        3, "finish", 0, (9, 10, 11, 12), (3, 5),
    )
    return decoded


def solution(mesh):
    grid = Mesh(mesh.devices.reshape(4, 2, 4, 4), ("y", "core", "x", "z"))
    placed = (
        P(ROWS, COLS, None), P(), P(), P(), P(), P(), P(), P(),
        P(None, ROWS, COLS, None), P(), P(), P(None, ROWS, COLS, None), P(), P(),
    )
    return jax.shard_map(local, mesh=grid, in_specs=placed, out_specs=P(ROWS, COLS, None), check_vma=False)
```

```python
import math

import jax
import jax.numpy as jnp
from jax import lax
from jax.experimental import pallas as pl
from jax.experimental.pallas import tpu as pltpu
from jax.sharding import Mesh
from jax.sharding import PartitionSpec as P

epsilon = 1e-06
masked_score = -1e30
ROWS = ("y", "core")
COLS = ("x", "z")
LAT_ROWS = 88
LAT_COLS = 256
TILE_ROWS = 13
TILE_COLS = 20
HALO = 2
EXT_ROWS = TILE_ROWS + 2 * HALO
EXT_COLS = TILE_COLS + 2 * HALO
HALF = EXT_COLS // 2
FRONT = HALO * HALF
FINE_ROWS = 2 * TILE_ROWS
FINE_COLS = 2 * TILE_COLS
FINE_PITCH = 48
KEY_TILE = 272
KEY_CHUNK = 1024
KEY_GROUPS = 4
MAX_CHUNKS = 7
KEY_ROWS = MAX_CHUNKS * KEY_CHUNK + KEY_CHUNK
QUERY_BLOCK = 1056
HALF_ROWS = 208
STAT_ROW = EXT_ROWS * HALF - (HALF_ROWS - 16)
WIDE_ROWS = LAT_ROWS * HALF + 384
FINE_STEP = 13
TALL_TILE = 160
VMEM_BYTES = 60 * 1024 * 1024
SMALL_BYTES = VMEM_BYTES
NEAR = 48


def rms_scale(values_in, gain_vec):
    wide = values_in.astype(jnp.float32)
    return wide * lax.rsqrt(jnp.mean(wide * wide, axis=-1, keepdims=True) + epsilon) * gain_vec


def silu(v):
    return v / (1.0 + jnp.exp(-v))


def hop(value, axes, count, step):
    pairs = [(i, i + step) for i in range(count) if 0 <= i + step < count]
    return lax.ppermute(value, axes, pairs)


def far_hops(needed, ahead, back, axes, count):
    return lax.cond(
        needed,
        lambda a, b: [hop(a, axes, count, 2), hop(b, axes, count, -2)],
        lambda a, b: [a, b],
        ahead, back,
    )


def put_rows(ref, start, value):
    for g in range(ref.shape[0]):
        ref[g, pl.ds(start, value.shape[0]), :] = value[:, g * 128 : (g + 1) * 128].astype(ref.dtype)


def get_rows(ref, start, count, stride=None):
    return jnp.concatenate([ref[g, pl.ds(start, count, stride), :] for g in range(ref.shape[0])], axis=1)


def put_strided(ref, start, stride, value):
    for g in range(ref.shape[0]):
        ref[g, pl.ds(start, value.shape[0], stride), :] = value[:, g * 128 : (g + 1) * 128].astype(ref.dtype)


def before(size_ref, index):
    total = 0
    for t in range(size_ref.shape[0]):
        total = total + jnp.where(t < index, size_ref[t], 0)
    return total


def size_at(size_ref, index):
    count = size_ref.shape[0]
    inside = (index >= 0) & (index < count)
    return jnp.where(inside, size_ref[jnp.clip(index, 0, count - 1)], 0)


def keys_kernel(col_ref, token_ref, gain_ref, key_ref, pack_ref):
    wide = col_ref[lax.axis_index("x") * lax.axis_size("z") + lax.axis_index("z")]
    pack_ref[...] = jnp.zeros_like(pack_ref)
    gain = gain_ref[...][None]
    for i in range(TILE_ROWS):
        put_rows(pack_ref, i * wide, rms_scale(token_ref[i].astype(jnp.float32), gain))
    key_ref[...] = get_rows(pack_ref, 0, KEY_TILE).astype(jnp.bfloat16)


def edges_kernel(
    place_ref, row_ref, col_ref, token_ref, one_ref, two_ref, right_ref, left_ref, right_far_ref, left_far_ref, coarse_ref, fine_ref
):
    wide = col_ref[place_ref[1]]
    for f in range(3):
        for i in range(TILE_ROWS):
            row = one_ref[f, i] if f < 2 else token_ref[i]
            put_rows(coarse_ref, (f * TILE_ROWS + i) * 24, row.astype(jnp.float32))
    for f in range(2):

        def copy_fine(i, carry):
            put_rows(fine_ref, pl.multiple_of((f * FINE_ROWS + i) * FINE_COLS, 8), two_ref[f, i].astype(jnp.float32))
            return carry

        lax.fori_loop(0, FINE_ROWS, copy_fine, 0)
    near = 3 * TILE_ROWS
    fine = 2 * FINE_ROWS
    for ref in (right_ref, left_ref, right_far_ref, left_far_ref):
        ref[...] = jnp.zeros_like(ref)
    last = get_rows(coarse_ref, wide - 1, near, 24).astype(jnp.bfloat16)
    first = get_rows(coarse_ref, 0, near, 24).astype(jnp.bfloat16)
    right_ref[0:near, :] = last
    right_ref[NEAR : NEAR + near, :] = get_rows(coarse_ref, jnp.maximum(wide - 2, 0), near, 24).astype(jnp.bfloat16)
    right_ref[2 * NEAR : 2 * NEAR + fine, :] = get_rows(fine_ref, 2 * wide - 1, fine, FINE_COLS).astype(jnp.bfloat16)
    left_ref[0:near, :] = first
    left_ref[NEAR : NEAR + near, :] = get_rows(coarse_ref, 1, near, 24).astype(jnp.bfloat16)
    left_ref[2 * NEAR : 2 * NEAR + fine, :] = get_rows(fine_ref, 0, fine, FINE_COLS).astype(jnp.bfloat16)
    right_far_ref[0:near, :] = last
    left_far_ref[0:near, :] = first


def columns_kernel(
    place_ref, row_ref, col_ref, token_ref, one_ref, two_ref, from_left_ref, from_right_ref, from_left_far_ref, from_right_far_ref,
    mine_ref, other_ref, prior_ref, fine_out_ref, down_ref, up_ref, down_far_ref, up_far_ref, coarse_ref, fine_ref, half_ref,
):
    core = place_ref[2]
    tall = row_ref[place_ref[0]]
    wide = col_ref[place_ref[1]]
    left_wide = size_at(col_ref, place_ref[1] - 1)
    right_wide = size_at(col_ref, place_ref[1] + 1)
    near = 3 * TILE_ROWS
    fine = 2 * FINE_ROWS
    blank = jnp.zeros((near, 384), jnp.float32)
    put_strided(coarse_ref, EXT_COLS - 2, EXT_COLS, blank)
    put_strided(coarse_ref, EXT_COLS - 1, EXT_COLS, blank)
    for f in range(3):
        for i in range(TILE_ROWS):
            row = one_ref[f, i] if f < 2 else token_ref[i]
            put_rows(coarse_ref, (f * TILE_ROWS + i) * EXT_COLS + HALO, row.astype(jnp.float32))
    left_two = jnp.where(left_wide == 1, from_left_far_ref[0:near, :], from_left_ref[NEAR : NEAR + near, :])
    right_two = jnp.where(right_wide == 1, from_right_far_ref[0:near, :], from_right_ref[NEAR : NEAR + near, :])
    put_strided(coarse_ref, 0, EXT_COLS, left_two.astype(jnp.float32))
    put_strided(coarse_ref, 1, EXT_COLS, from_left_ref[0:near, :].astype(jnp.float32))
    put_strided(coarse_ref, wide + 2, EXT_COLS, from_right_ref[0:near, :].astype(jnp.float32))
    put_strided(coarse_ref, wide + 3, EXT_COLS, right_two.astype(jnp.float32))
    for side, ref in ((core, mine_ref), (1 - core, other_ref)):
        for i in range(TILE_ROWS):
            put_rows(half_ref, i * HALF, get_rows(coarse_ref, (2 * TILE_ROWS + i) * EXT_COLS + side * HALF, HALF))
        half_ref[:, TILE_ROWS * HALF : TALL_TILE, :] = jnp.zeros((3, TALL_TILE - TILE_ROWS * HALF, 128), jnp.float32)
        ref[...] = get_rows(half_ref, 0, TALL_TILE).astype(jnp.bfloat16)
    for i in range(2 * TILE_ROWS):
        prior_ref[i] = get_rows(coarse_ref, i * EXT_COLS, EXT_COLS).astype(jnp.bfloat16)
    for c in range(FINE_COLS + 1, FINE_PITCH):
        put_strided(fine_ref, c, FINE_PITCH, jnp.zeros((fine, 384), jnp.float32))
    for f in range(2):

        def copy_fine(i, carry):
            put_rows(fine_ref, (f * FINE_ROWS + i) * FINE_PITCH + 1, two_ref[f, i].astype(jnp.float32))
            return carry

        lax.fori_loop(0, FINE_ROWS, copy_fine, 0)
    put_strided(fine_ref, 0, FINE_PITCH, from_left_ref[2 * NEAR : 2 * NEAR + fine, :].astype(jnp.float32))
    put_strided(fine_ref, 2 * wide + 1, FINE_PITCH, from_right_ref[2 * NEAR : 2 * NEAR + fine, :].astype(jnp.float32))

    def write_fine(i, carry):
        fine_out_ref[i] = get_rows(fine_ref, pl.multiple_of(i * FINE_PITCH, 8), FINE_PITCH).astype(jnp.bfloat16)
        return carry

    lax.fori_loop(0, fine, write_fine, 0)
    for f in range(2):
        base = f * TILE_ROWS
        last = prior_ref[base + tall - 1]
        down_ref[f] = last
        down_ref[2 + f] = prior_ref[base + jnp.maximum(tall - 2, 0)]
        down_far_ref[f] = last
        up_ref[f] = prior_ref[base]
        up_ref[2 + f] = prior_ref[base + 1]
        up_far_ref[f] = prior_ref[base]
        bottom = fine_out_ref[f * FINE_ROWS + 2 * tall - 1]
        top = fine_out_ref[f * FINE_ROWS]
        for h in range(2):
            down_ref[4 + 2 * f + h] = bottom[h * 24 : (h + 1) * 24]
            up_ref[4 + 2 * f + h] = top[h * 24 : (h + 1) * 24]


def prior_coarse_kernel(
    place_ref, row_ref, prior_ref, from_up_ref, from_down_ref, from_up_far_ref, from_down_far_ref, one_ref, two_ref,
    sum_one_ref, phase_ref, coarse_ref, part_ref, weight_one_ref, weight_two_ref, sem_ref,
):
    fetch_one = pltpu.make_async_copy(one_ref.at[pl.ds(0, 2)], weight_one_ref, sem_ref.at[0])
    fetch_two = pltpu.make_async_copy(two_ref.at[pl.ds(2, 1)], weight_two_ref, sem_ref.at[1])
    fetch_two.start()
    fetch_one.start()
    tall = row_ref[place_ref[0]]
    up_tall = size_at(row_ref, place_ref[0] - 1)
    down_tall = size_at(row_ref, place_ref[0] + 1)
    for f in range(2):
        coarse_ref[f, 0] = jnp.where(up_tall == 1, from_up_far_ref[f], from_up_ref[2 + f])
        coarse_ref[f, 1] = from_up_ref[f]
        for i in range(TILE_ROWS):
            coarse_ref[f, HALO + i] = prior_ref[f * TILE_ROWS + i]
        for i in (TILE_ROWS + 2, TILE_ROWS + 3):
            coarse_ref[f, i] = jnp.zeros((EXT_COLS, 384), jnp.bfloat16)
        coarse_ref[f, tall + 2] = from_down_ref[f]
        coarse_ref[f, tall + 3] = jnp.where(down_tall == 1, from_down_far_ref[f], from_down_ref[2 + f])
    fetch_two.wait()
    taps = ((0,), (1, 2), (0, 1), (2,))
    for u in range(4):
        rows = [sum(weight_two_ref[0, a, b].astype(jnp.float32) for a in taps[u]) for b in range(3)]
        for v in range(4):
            phase_ref[u, v] = sum(rows[b] for b in taps[v]).astype(jnp.bfloat16)
    fetch_one.wait()
    sum_one_ref[...] = coarse_conv(lambda f, a, n: coarse_ref[f, a : a + n], weight_one_ref, part_ref, 2)


def prior_fine_kernel(
    place_ref, row_ref, fine_ref, from_up_ref, from_down_ref, two_ref, sum_two_ref, wide_ref, part_ref, weight_two_ref, sem_ref
):
    fetch_two = pltpu.make_async_copy(two_ref.at[pl.ds(0, 2)], weight_two_ref, sem_ref.at[0])
    fetch_two.start()
    tall = row_ref[place_ref[0]]
    for f in range(2):
        wide_ref[f, 0] = jnp.concatenate([from_up_ref[4 + 2 * f], from_up_ref[5 + 2 * f]], axis=0)

        def copy_fine(i, carry):
            wide_ref[f, 1 + i] = fine_ref[f * FINE_ROWS + i]
            return carry

        lax.fori_loop(0, FINE_ROWS, copy_fine, 0)
        wide_ref[f, FINE_ROWS + 1] = jnp.zeros((FINE_PITCH, 384), jnp.bfloat16)
        wide_ref[f, 2 * tall + 1] = jnp.concatenate([from_down_ref[4 + 2 * f], from_down_ref[5 + 2 * f]], axis=0)
    fetch_two.wait()
    for r in range(0, FINE_ROWS, FINE_STEP):
        sum_two_ref[r * FINE_PITCH : (r + FINE_STEP) * FINE_PITCH, :] = fine_conv(
            lambda f, a, n: wide_ref[f, r + a : r + a + n], weight_two_ref, part_ref, 2
        )


def coarse_conv(rows_of, weight_ref, part_ref, depth):
    rows = TILE_ROWS + 2
    taps = [(f, a) for f in range(depth) for a in range(3)]
    left = jnp.concatenate([rows_of(f, a, rows).reshape(rows * EXT_COLS, 384) for f, a in taps], axis=1)
    right = jnp.concatenate([jnp.concatenate([weight_ref[f, a, b] for b in range(3)], axis=1) for f, a in taps], axis=0)
    product = jnp.dot(left, right, preferred_element_type=jnp.float32)
    return shifted_sum([product[:, b * 384 : (b + 1) * 384] for b in range(3)], part_ref)


def fine_conv(rows_of, weight_ref, part_ref, depth):
    taps = [(f, a) for f in range(depth) for a in range(3)]
    left = jnp.concatenate([rows_of(f, a, FINE_STEP).reshape(FINE_STEP * FINE_PITCH, 384) for f, a in taps], axis=1)
    products = [
        lax.dot_general(
            left, jnp.concatenate([weight_ref[f, a, b] for f, a in taps], axis=1), (((1,), (1,)), ((), ())),
            preferred_element_type=jnp.float32,
        )
        for b in range(3)
    ]
    return shifted_sum(products, part_ref)


def shifted_sum(products, part_ref):
    total = products[0]
    count, width = total.shape
    groups = -(-width // 128)
    for b in (1, 2):
        for g in range(groups):
            hi = min((g + 1) * 128, width)
            part_ref[g, 0:count, 0 : hi - g * 128] = products[b][:, g * 128 : hi]
        moved = jnp.concatenate([part_ref[g, b : b + count, :] for g in range(groups)], axis=1)
        total = total + moved[:, 0:width]
    return total


def query_kernel(
    place_ref, row_ref, own_ref, one_ref, two_ref, three_ref, gain_ref, qw_ref, kw_ref, query_ref, frame_ref, frame_other_ref, wide_ref, *, scale
):
    y_at = place_ref[0] // 2
    wide_ref[...] = jnp.zeros_like(wide_ref)
    slot = lax.broadcasted_iota(jnp.int32, (TALL_TILE, 128), 0)
    for k, ref in enumerate((own_ref, one_ref, two_ref, three_ref)):
        source = jnp.bitwise_and(y_at - k, 3)
        for t in range(2):
            start = FRONT + before(row_ref, 2 * source + t) * HALF
            usable = slot < row_ref[2 * source + t] * HALF
            part = ref[t].astype(jnp.float32)
            for g in range(3):
                held = wide_ref[g, pl.ds(start, TALL_TILE), :]
                wide_ref[g, pl.ds(start, TALL_TILE), :] = jnp.where(usable, part[:, g * 128 : (g + 1) * 128], held)
    count = LAT_ROWS * HALF
    frame_ref[...] = get_rows(wide_ref, before(row_ref, place_ref[0]) * HALF, HALF_ROWS).astype(jnp.bfloat16)
    sibling = place_ref[0] + 1 - 2 * place_ref[2]
    frame_other_ref[...] = get_rows(wide_ref, before(row_ref, sibling) * HALF, HALF_ROWS).astype(jnp.bfloat16)
    step = count // 3
    for i in range(3):
        raw = get_rows(wide_ref, FRONT + i * step, step)
        normed = rms_scale(raw, gain_ref[...][None]).astype(jnp.bfloat16)
        query = jnp.dot(normed, qw_ref[...], preferred_element_type=jnp.float32).astype(jnp.bfloat16)
        turned = lax.dot_general(query, kw_ref[...], (((1,), (1,)), ((), ())), preferred_element_type=jnp.float32)
        query_ref[i * step : (i + 1) * step, :] = (turned * scale).astype(jnp.bfloat16)


def attention_kernel(
    place_ref, row_ref, col_ref, query_ref, tile_ref, out_ref,
    stage_ref, key_ref, bias_ref, score_ref, top_ref, sum_ref, acc_ref, wide_ref, stat_ref, offset_ref, sem_ref,
):
    tiles = tile_ref.shape[0]
    group = tiles // KEY_GROUPS
    fetches = [
        pltpu.make_async_copy(tile_ref.at[pl.ds(n * group, group)], stage_ref.at[pl.ds(n * group, group)], sem_ref.at[n])
        for n in range(KEY_GROUPS)
    ]
    fetches[0].start()
    cols = col_ref.shape[0]
    y_at = place_ref[0] // 2
    spot = lax.broadcasted_iota(jnp.int32, (8, KEY_CHUNK), 0) * KEY_CHUNK + lax.broadcasted_iota(jnp.int32, (8, KEY_CHUNK), 1)

    def locate(t, carry):
        offset, bias = carry
        offset_ref[t] = offset
        count = row_ref[2 * y_at + t // cols] * col_ref[t % cols]
        bias = jnp.where((spot >= offset) & (spot < offset + count), 0.0, bias)
        return offset + (count + 15) // 16 * 16, bias

    tail, bias = lax.fori_loop(0, tiles, locate, (jnp.int32(0), jnp.full((8, KEY_CHUNK), masked_score, jnp.float32)))
    offset_ref[tiles] = tail
    for j in range(MAX_CHUNKS):
        bias_ref[j] = bias[j : j + 1, :]
    chunk_count = (tail + KEY_CHUNK - 1) // KEY_CHUNK

    def gather(t, carry):
        key_ref[pl.ds(pl.multiple_of(offset_ref[t], 16), KEY_TILE), :] = stage_ref[t]
        return carry

    total = wide_ref.shape[1]
    count = query_ref.shape[0]
    wide_ref[:, 0:FRONT, :] = jnp.zeros((3, FRONT, 128), jnp.float32)
    wide_ref[:, FRONT + count : total, :] = jnp.zeros((3, total - FRONT - count, 128), jnp.float32)
    stat_ref[0:FRONT, :] = jnp.zeros((FRONT, 128), jnp.float32)
    stat_ref[FRONT + count : total, :] = jnp.zeros((total - FRONT - count, 128), jnp.float32)
    lane_groups = KEY_CHUNK // 128

    def keys_at(j):
        return key_ref[pl.ds(pl.multiple_of(j * KEY_CHUNK, KEY_CHUNK), KEY_CHUNK), :]

    def score_step(i, j):
        slot = 0
        query = query_ref[i * QUERY_BLOCK : (i + 1) * QUERY_BLOCK, :]
        s = lax.dot_general(query, keys_at(j), (((1,), (1,)), ((), ())), preferred_element_type=jnp.float32)
        s = s + bias_ref[j]
        score_ref[slot, j] = s
        best = s[:, 0:128]
        for g in range(1, lane_groups):
            best = jnp.maximum(best, s[:, g * 128 : (g + 1) * 128])
        top_ref[slot] = jnp.maximum(top_ref[slot], best)

    def value_step(i, j):
        slot = 0
        top = top_ref[slot]
        p = jnp.exp2(score_ref[slot, j] - jnp.concatenate([top] * lane_groups, axis=1))
        part = p[:, 0:128]
        for g in range(1, lane_groups):
            part = part + p[:, g * 128 : (g + 1) * 128]
        sum_ref[...] = sum_ref[...] + part
        acc_ref[...] = acc_ref[...] + jnp.dot(p.astype(jnp.bfloat16), keys_at(j), preferred_element_type=jnp.float32)

    top_ref[0] = jnp.full((QUERY_BLOCK, 128), masked_score, jnp.float32)
    done = jnp.int32(0)
    for n in range(KEY_GROUPS):
        fetches[n].wait()
        if n + 1 < KEY_GROUPS:
            fetches[n + 1].start()
        lax.fori_loop(n * group, (n + 1) * group, gather, 0)
        if n + 1 == KEY_GROUPS:
            key_ref[pl.ds(pl.multiple_of(tail, 16), KEY_CHUNK), :] = jnp.zeros((KEY_CHUNK, key_ref.shape[1]), jnp.bfloat16)
            ready = chunk_count
        else:
            ready = offset_ref[(n + 1) * group] // KEY_CHUNK

        def score_chunk(j, carry):
            score_step(0, j)
            return carry

        lax.fori_loop(done, ready, score_chunk, 0)
        done = ready
    best = jnp.max(top_ref[0], axis=1, keepdims=True)
    top_ref[0] = jnp.broadcast_to(best, (QUERY_BLOCK, 128))
    sum_ref[...] = jnp.zeros_like(sum_ref)
    acc_ref[...] = jnp.zeros_like(acc_ref)

    def value_chunk(j, carry):
        value_step(0, j)
        return carry

    def value_pair(j, carry):
        value_step(0, 2 * j)
        value_step(0, 2 * j + 1)
        return carry

    lax.fori_loop(0, chunk_count // 2, value_pair, 0)

    @pl.when(chunk_count % 2 == 1)
    def _():
        value_step(0, chunk_count - 1)

    denominator = jnp.sum(sum_ref[...], axis=1, keepdims=True)
    put_rows(wide_ref, FRONT, acc_ref[...] / denominator)
    level = top_ref[0] + jnp.log2(jnp.broadcast_to(denominator, (QUERY_BLOCK, 128)))
    high = level.astype(jnp.bfloat16).astype(jnp.float32)
    mid = (level - high).astype(jnp.bfloat16).astype(jnp.float32)
    low = level - high - mid
    lane = lax.broadcasted_iota(jnp.int32, (QUERY_BLOCK, 128), 1)
    packed = jnp.where(lane == 0, high, jnp.where(lane == 1, mid, jnp.where(lane == 2, low, 0.0)))
    stat_ref[FRONT : FRONT + QUERY_BLOCK, :] = packed
    body = HALF_ROWS - 16
    select = (
        lax.broadcasted_iota(jnp.int32, (16, 128), 0) - STAT_ROW == lax.broadcasted_iota(jnp.int32, (16, 128), 1)
    ).astype(jnp.bfloat16)
    is_stat = lax.broadcasted_iota(jnp.int32, (16, 384), 0) >= STAT_ROW
    for b in range(out_ref.shape[0]):
        offset = before(row_ref, b) * HALF
        out_ref[b, 0:body, :] = get_rows(wide_ref, offset, body).astype(jnp.bfloat16)
        levels = stat_ref[pl.ds(offset, 384), :].astype(jnp.bfloat16)
        levels = lax.dot_general(select, levels, (((1,), (1,)), ((), ())), preferred_element_type=jnp.float32)
        last = jnp.where(is_stat, levels, get_rows(wide_ref, offset + body, 16))
        out_ref[b, body:HALF_ROWS, :] = last.astype(jnp.bfloat16)


def finish_kernel(
    place_ref, row_ref, col_ref, part_ref, mine_ref, other_ref, vw_ref, ow_ref, gain_one_ref, far_one_ref, far_two_ref, one_ref, two_ref,
    gain_two_ref, out_ref, act_ref, first_ref, shift_ref, product_ref, fine_ref, weight_one_ref, phase_ref, sum_one_ref, sum_two_ref, sem_ref,
):
    fetch_one = pltpu.make_async_copy(one_ref.at[pl.ds(2, 1)], weight_one_ref, sem_ref.at[0])
    fetch_two = pltpu.make_async_copy(two_ref, phase_ref, sem_ref.at[1])
    fetch_sum_one = pltpu.make_async_copy(far_one_ref, sum_one_ref, sem_ref.at[2])
    fetch_sum_two = pltpu.make_async_copy(far_two_ref, sum_two_ref, sem_ref.at[3])
    fetch_one.start()
    fetch_sum_one.start()
    fetch_two.start()
    fetch_sum_two.start()
    core = place_ref[2]
    tall = row_ref[place_ref[0]]
    wide = col_ref[place_ref[1]]
    groups = part_ref.shape[0]
    stat = lax.broadcasted_iota(jnp.int32, (16 * groups, 128 * groups), 0)
    owner = jnp.right_shift(lax.broadcasted_iota(jnp.int32, (16 * groups, 128 * groups), 1), 7)
    within = stat - owner * 16
    ones = ((within >= STAT_ROW) & (within < STAT_ROW + 3)).astype(jnp.bfloat16)
    stacked = jnp.concatenate([part_ref[g, HALF_ROWS - 16 : HALF_ROWS, 0:256] for g in range(groups)], axis=0)
    spread = lax.dot_general(stacked, ones, (((0,), (0,)), ((), ())), preferred_element_type=jnp.float32)
    halves = []
    for side in range(2):
        sources = range(side, part_ref.shape[0], 2)
        levels = [spread[0:HALF_ROWS, g * 128 : (g + 1) * 128] for g in sources]
        best = jnp.maximum(jnp.maximum(levels[0], levels[1]), jnp.maximum(levels[2], levels[3]))
        weights = [jnp.exp2(level - best) for level in levels]
        total = (weights[0] + weights[1]) + (weights[2] + weights[3])
        merged = None
        for weight, g in zip(weights, sources):
            share = weight / total
            term = part_ref[g, 0:HALF_ROWS, :].astype(jnp.float32) * jnp.concatenate([share] * 3, axis=1)
            merged = term if merged is None else merged + term
        halves.append(merged.astype(jnp.bfloat16))
    merged = jnp.concatenate(halves, axis=0)
    attention = jnp.dot(merged, vw_ref[...], preferred_element_type=jnp.float32).astype(jnp.bfloat16)
    projected = jnp.dot(attention, ow_ref[...], preferred_element_type=jnp.float32)
    mine = mine_ref[...].astype(jnp.float32)
    other = other_ref[...].astype(jnp.float32)
    frame = jnp.concatenate([jnp.where(core == 0, mine, other), jnp.where(core == 0, other, mine)], axis=0)
    mixed = (frame + projected).astype(jnp.bfloat16)
    put_rows(shift_ref, 0, silu(rms_scale(mixed, gain_one_ref[...][None])))
    row_start = before(row_ref, place_ref[0])
    col_start = before(col_ref, place_ref[1])
    for side in range(2):
        for i in range(EXT_ROWS):
            put_rows(act_ref, i * EXT_COLS + side * HALF, get_rows(shift_ref, side * HALF_ROWS + i * HALF, HALF))
    at_col = col_start - HALO + lax.broadcasted_iota(jnp.int32, (EXT_COLS, 384), 0)
    col_inside = (at_col >= 0) & (at_col < LAT_COLS)
    for i in range(EXT_ROWS):
        at_row = row_start - HALO + i
        inside = col_inside & (at_row >= 0) & (at_row < LAT_ROWS)
        first_ref[i] = jnp.where(inside, get_rows(act_ref, i * EXT_COLS, EXT_COLS), 0.0).astype(jnp.bfloat16)
    rows = TILE_ROWS + 2
    fetch_one.wait()
    total = coarse_conv(lambda f, a, n: first_ref[a : a + n], weight_one_ref, shift_ref, 1)
    fetch_sum_one.wait()
    y_one = (total + sum_one_ref[...]).astype(jnp.bfloat16)
    act = silu(rms_scale(y_one, gain_two_ref[...][None])).astype(jnp.bfloat16).astype(jnp.float32)
    put_rows(act_ref, 0, act)
    at_col = col_start - 1 + lax.broadcasted_iota(jnp.int32, (EXT_COLS, 384), 0)
    col_inside = (at_col >= 0) & (at_col < LAT_COLS)
    for i in range(rows):
        at_row = row_start - 1 + i
        inside = col_inside & (at_row >= 0) & (at_row < LAT_ROWS)
        first_ref[i] = jnp.where(inside, get_rows(act_ref, i * EXT_COLS, EXT_COLS), 0.0).astype(jnp.bfloat16)
    fetch_two.wait()
    count = TILE_ROWS * EXT_COLS
    for p in range(2):
        left = jnp.concatenate(
            [first_ref[p + u : p + u + TILE_ROWS].reshape(count, 384) for u in range(2)], axis=1
        )
        for q in range(2):
            for v in range(2):
                right = jnp.concatenate([phase_ref[2 * p + u, 2 * q + v] for u in range(2)], axis=1)
                product = lax.dot_general(left, right, (((1,), (1,)), ((), ())), preferred_element_type=jnp.float32)
                product_ref[2 * q + v, 0, 0:count, :] = product[:, 0:128]
                product_ref[2 * q + v, 1, 0:count, 0:64] = product[:, 128:192]
            for i in range(TILE_ROWS):
                for g in range(2):
                    near = product_ref[2 * q, g, pl.ds(i * EXT_COLS + q, EXT_COLS), :]
                    next_ = product_ref[2 * q + 1, g, pl.ds(i * EXT_COLS + q + 1, EXT_COLS), :]
                    fine_ref[g, pl.ds((2 * i + p) * FINE_PITCH + q, EXT_COLS, 2), :] = near + next_
    col = lax.broadcasted_iota(jnp.int32, (FINE_COLS, 192), 0)
    fetch_sum_two.wait()
    for r in range(FINE_ROWS):
        line = get_rows(fine_ref, r * FINE_PITCH, FINE_COLS)[:, 0:192] + sum_two_ref[r * FINE_PITCH : r * FINE_PITCH + FINE_COLS, :]
        usable = (col < 2 * wide) & (r < 2 * tall)
        out_ref[r] = jnp.where(usable, line, 0.0).astype(jnp.bfloat16)


def call(body, inputs, outs, scratch, smem_count, name, flops=0, far=(), near=(), limit=SMALL_BYTES):
    smem = pl.BlockSpec(memory_space=pltpu.SMEM)
    vmem = pl.BlockSpec(memory_space=pltpu.VMEM)
    moved = sum(math.prod(v.shape) * v.dtype.itemsize for v in list(inputs) + list(outs))
    return pl.pallas_call(
        body,
        in_specs=[
            smem if i < smem_count else pl.BlockSpec(memory_space=pl.ANY) if i in far else vmem for i in range(len(inputs))
        ],
        out_specs=[vmem] * len(outs),
        out_shape=outs,
        scratch_shapes=scratch,
        compiler_params=pltpu.CompilerParams(vmem_limit_bytes=limit),
        cost_estimate=pl.CostEstimate(flops=int(flops), transcendentals=0, bytes_accessed=int(moved)),
        name=name,
    )(*[pltpu.with_memory_space_constraint(v, pltpu.VMEM) if i in near else v for i, v in enumerate(inputs)])


def attend(place, row_sizes, col_sizes, queries, tiles):
    channels = queries.shape[1]
    scratch = lambda *dims: pltpu.VMEM(dims, jnp.float32)
    (parts,) = call(
        attention_kernel,
        [place, row_sizes, col_sizes, queries, tiles],
        [jax.ShapeDtypeStruct((8, HALF_ROWS, channels), jnp.bfloat16)],
        [
            pltpu.VMEM(tiles.shape, jnp.bfloat16), pltpu.VMEM((KEY_ROWS, channels), jnp.bfloat16),
            scratch(MAX_CHUNKS, 1, KEY_CHUNK), scratch(1, MAX_CHUNKS, QUERY_BLOCK, KEY_CHUNK),
            scratch(1, QUERY_BLOCK, 128), scratch(QUERY_BLOCK, 128), scratch(QUERY_BLOCK, channels),
            scratch(3, WIDE_ROWS, 128), scratch(WIDE_ROWS, 128), pltpu.SMEM((tiles.shape[0] + 1,), jnp.int32),
            pltpu.SemaphoreType.DMA((KEY_GROUPS,)),
        ],
        3, "attention", 4 * LAT_ROWS * HALF * channels * KEY_ROWS, (4,), (), VMEM_BYTES,
    )
    return parts


def local(
    tokens, row_sizes, col_sizes, norm_gain, query_weight, key_weight, value_weight, out_weight,
    cache_one, gain_one, conv_one, cache_two, gain_two, conv_two,
):
    channels = tokens.shape[2]
    n_row = row_sizes.shape[0]
    n_col = col_sizes.shape[0]
    n_y = lax.axis_size("y")
    core = lax.axis_index("core")
    row_at = lax.axis_index("y") * lax.axis_size("core") + core
    col_at = lax.axis_index("x") * lax.axis_size("z") + lax.axis_index("z")
    place = jnp.stack([row_at, col_at, core]).astype(jnp.int32)
    shape = lambda *dims: jax.ShapeDtypeStruct(dims, jnp.bfloat16)
    wide_shape = lambda *dims: jax.ShapeDtypeStruct(dims, jnp.float32)
    scratch = lambda *dims: pltpu.VMEM(dims, jnp.float32)
    narrow = lambda *dims: pltpu.VMEM(dims, jnp.bfloat16)
    message = 160
    place_args = [place, row_sizes, col_sizes]
    (own_keys,) = call(
        keys_kernel, [col_sizes, tokens, norm_gain], [shape(KEY_TILE, channels)], [scratch(3, 304, 128)], 1, "keys"
    )
    tiles = lax.all_gather(own_keys, ("core", "x", "z"), axis=0, tiled=False)
    to_right, to_left, to_right_far, to_left_far = call(
        edges_kernel,
        [*place_args, tokens, cache_one, cache_two],
        [shape(message, channels), shape(message, channels), shape(NEAR, channels), shape(NEAR, channels)],
        [scratch(3, 3 * TILE_ROWS * 24, 128), scratch(3, 2 * FINE_ROWS * FINE_COLS, 128)],
        3, "edges",
    )
    from_left = hop(to_right, COLS, n_col, 1)
    from_right = hop(to_left, COLS, n_col, -1)
    from_left_far, from_right_far = far_hops(jnp.any(col_sizes == 1), to_right_far, to_left_far, COLS, n_col)
    mine, other, prior, fine, down, up, down_far, up_far = call(
        columns_kernel,
        [*place_args, tokens, cache_one, cache_two, from_left, from_right, from_left_far, from_right_far],
        [
            shape(TALL_TILE, channels), shape(TALL_TILE, channels), shape(2 * TILE_ROWS, EXT_COLS, channels),
            shape(2 * FINE_ROWS, FINE_PITCH, channels), shape(8, EXT_COLS, channels), shape(8, EXT_COLS, channels),
            shape(2, EXT_COLS, channels), shape(2, EXT_COLS, channels),
        ],
        [scratch(3, 3 * TILE_ROWS * EXT_COLS, 128), scratch(3, 2 * FINE_ROWS * FINE_PITCH, 128), scratch(3, TALL_TILE, 128)],
        3, "columns", 0, (), (6, 7),
    )
    swap = [(0, 1), (1, 0)]
    sibling = lax.ppermute(other, "core", swap)
    pair = jnp.where(core == 0, jnp.stack([mine, sibling]), jnp.stack([sibling, mine]))
    strips = [pair] + [lax.ppermute(pair, "y", [(i, (i + k) % n_y) for i in range(n_y)]) for k in range(1, n_y)]
    around = [hop(down, ROWS, n_row, 1), hop(up, ROWS, n_row, -1)]
    around += far_hops(jnp.any(row_sizes == 1), down_far, up_far, ROWS, n_row)
    strips, around = lax.optimization_barrier((strips, around))
    scale = math.log2(math.e) / math.sqrt(channels)

    def query_body(*refs):
        query_kernel(*refs, scale=scale)

    queries, frame, frame_other = call(
        query_body,
        [place, row_sizes, *strips, norm_gain, query_weight, key_weight],
        [shape(LAT_ROWS * HALF, channels), shape(HALF_ROWS, channels), shape(HALF_ROWS, channels)],
        [scratch(3, WIDE_ROWS, 128)],
        2, "queries", 4 * LAT_ROWS * HALF * channels * channels, (), (2, 3, 4, 5),
    )
    frame_other = lax.ppermute(frame_other, "core", swap)
    conv_two = jnp.swapaxes(conv_two, 3, 4)
    channels_out = conv_two.shape[3]
    from_up, from_down, from_up_far, from_down_far = around
    sum_one, phases = call(
        prior_coarse_kernel,
        [place, row_sizes, prior, from_up, from_down, from_up_far, from_down_far, conv_one, conv_two],
        [wide_shape((TILE_ROWS + 2) * EXT_COLS, channels), shape(4, 4, channels_out, channels)],
        [
            narrow(2, EXT_ROWS, EXT_COLS, channels), scratch(3, 640, 128), narrow(2, 3, 3, channels, channels),
            narrow(1, 3, 3, channels_out, channels), pltpu.SemaphoreType.DMA((2,)),
        ],
        2, "prior_coarse", 2 * 18 * channels * 360 * 384, (7, 8), (3, 4),
    )
    queries, sum_one, phases = lax.optimization_barrier((queries, sum_one, phases))
    parts = attend(place, row_sizes, col_sizes, queries, tiles.reshape(2 * n_col, KEY_TILE, channels))
    parts = lax.all_to_all(parts, ROWS, 0, 0)
    (sum_two,) = call(
        prior_fine_kernel,
        [place, row_sizes, fine, from_up, from_down, conv_two],
        [wide_shape(FINE_ROWS * FINE_PITCH, channels_out)],
        [
            narrow(2, FINE_ROWS + 2, FINE_PITCH, channels), scratch(3, 640, 128), narrow(2, 3, 3, channels_out, channels),
            pltpu.SemaphoreType.DMA((1,)),
        ],
        2, "prior_fine", 2 * 18 * channels * 1248 * 192, (5,), (3, 4),
    )
    (decoded,) = call(
        finish_kernel,
        [
            *place_args, parts, frame, frame_other, value_weight, out_weight, gain_one, sum_one, sum_two, conv_one, phases, gain_two,
        ],
        [shape(FINE_ROWS, FINE_COLS, channels_out)],
        [
            scratch(3, EXT_ROWS * EXT_COLS, 128), narrow(EXT_ROWS, EXT_COLS, channels),
            scratch(3, 640, 128),
            scratch(4, 2, TILE_ROWS * EXT_COLS + 8, 128), scratch(2, FINE_ROWS * FINE_PITCH, 128),
            narrow(1, 3, 3, channels, channels), narrow(4, 4, channels_out, channels),
            scratch((TILE_ROWS + 2) * EXT_COLS, channels), scratch(FINE_ROWS * FINE_PITCH, channels_out), pltpu.SemaphoreType.DMA((4,)),
        ],
        3, "finish", 0, (9, 10, 11, 12), (3, 5),
    )
    return decoded


def solution(mesh):
    grid = Mesh(mesh.devices.reshape(4, 2, 4, 4), ("y", "core", "x", "z"))
    placed = (
        P(ROWS, COLS, None), P(), P(), P(), P(), P(), P(), P(),
        P(None, ROWS, COLS, None), P(), P(), P(None, ROWS, COLS, None), P(), P(),
    )
    return jax.shard_map(local, mesh=grid, in_specs=placed, out_specs=P(ROWS, COLS, None), check_vma=False)
```

```python
import math

import jax
import jax.numpy as jnp
from jax import lax
from jax.experimental import pallas as pl
from jax.experimental.pallas import tpu as pltpu
from jax.sharding import Mesh
from jax.sharding import PartitionSpec as P

epsilon = 1e-06
masked_score = -1e30
ROWS = ("y", "core")
COLS = ("x", "z")
LAT_ROWS = 88
LAT_COLS = 256
TILE_ROWS = 13
TILE_COLS = 20
HALO = 2
EXT_ROWS = TILE_ROWS + 2 * HALO
EXT_COLS = TILE_COLS + 2 * HALO
HALF = EXT_COLS // 2
FRONT = HALO * HALF
FINE_ROWS = 2 * TILE_ROWS
FINE_COLS = 2 * TILE_COLS
FINE_PITCH = 48
KEY_TILE = 272
KEY_CHUNK = 1024
KEY_GROUPS = 4
MAX_CHUNKS = 7
KEY_ROWS = MAX_CHUNKS * KEY_CHUNK + KEY_CHUNK
QUERY_BLOCK = 1056
HALF_ROWS = 208
STAT_ROW = EXT_ROWS * HALF - (HALF_ROWS - 16)
WIDE_ROWS = LAT_ROWS * HALF + 384
FINE_STEP = 13
TALL_TILE = 160
VMEM_BYTES = 60 * 1024 * 1024
SMALL_BYTES = VMEM_BYTES
NEAR = 48


def rms_scale(values_in, gain_vec):
    wide = values_in.astype(jnp.float32)
    return wide * lax.rsqrt(jnp.mean(wide * wide, axis=-1, keepdims=True) + epsilon) * gain_vec


def silu(v):
    return v / (1.0 + jnp.exp(-v))


def hop(value, axes, count, step):
    pairs = [(i, i + step) for i in range(count) if 0 <= i + step < count]
    return lax.ppermute(value, axes, pairs)


def far_hops(needed, ahead, back, axes, count):
    return lax.cond(
        needed,
        lambda a, b: [hop(a, axes, count, 2), hop(b, axes, count, -2)],
        lambda a, b: [a, b],
        ahead, back,
    )


def put_rows(ref, start, value):
    for g in range(ref.shape[0]):
        ref[g, pl.ds(start, value.shape[0]), :] = value[:, g * 128 : (g + 1) * 128].astype(ref.dtype)


def get_rows(ref, start, count, stride=None):
    return jnp.concatenate([ref[g, pl.ds(start, count, stride), :] for g in range(ref.shape[0])], axis=1)


def put_strided(ref, start, stride, value):
    for g in range(ref.shape[0]):
        ref[g, pl.ds(start, value.shape[0], stride), :] = value[:, g * 128 : (g + 1) * 128].astype(ref.dtype)


def before(size_ref, index):
    total = 0
    for t in range(size_ref.shape[0]):
        total = total + jnp.where(t < index, size_ref[t], 0)
    return total


def size_at(size_ref, index):
    count = size_ref.shape[0]
    inside = (index >= 0) & (index < count)
    return jnp.where(inside, size_ref[jnp.clip(index, 0, count - 1)], 0)


def keys_kernel(col_ref, token_ref, gain_ref, key_ref, pack_ref):
    wide = col_ref[lax.axis_index("x") * lax.axis_size("z") + lax.axis_index("z")]
    pack_ref[...] = jnp.zeros_like(pack_ref)
    gain = gain_ref[...][None]
    for i in range(TILE_ROWS):
        put_rows(pack_ref, i * wide, rms_scale(token_ref[i].astype(jnp.float32), gain))
    key_ref[...] = get_rows(pack_ref, 0, KEY_TILE).astype(jnp.bfloat16)


def edges_kernel(
    place_ref, row_ref, col_ref, token_ref, one_ref, two_ref, right_ref, left_ref, right_far_ref, left_far_ref, coarse_ref, fine_ref
):
    wide = col_ref[place_ref[1]]
    for f in range(3):
        for i in range(TILE_ROWS):
            row = one_ref[f, i] if f < 2 else token_ref[i]
            put_rows(coarse_ref, (f * TILE_ROWS + i) * 24, row.astype(jnp.float32))
    for f in range(2):

        def copy_fine(i, carry):
            put_rows(fine_ref, pl.multiple_of((f * FINE_ROWS + i) * FINE_COLS, 8), two_ref[f, i].astype(jnp.float32))
            return carry

        lax.fori_loop(0, FINE_ROWS, copy_fine, 0)
    near = 3 * TILE_ROWS
    fine = 2 * FINE_ROWS
    for ref in (right_ref, left_ref, right_far_ref, left_far_ref):
        ref[...] = jnp.zeros_like(ref)
    last = get_rows(coarse_ref, wide - 1, near, 24).astype(jnp.bfloat16)
    first = get_rows(coarse_ref, 0, near, 24).astype(jnp.bfloat16)
    right_ref[0:near, :] = last
    right_ref[NEAR : NEAR + near, :] = get_rows(coarse_ref, jnp.maximum(wide - 2, 0), near, 24).astype(jnp.bfloat16)
    right_ref[2 * NEAR : 2 * NEAR + fine, :] = get_rows(fine_ref, 2 * wide - 1, fine, FINE_COLS).astype(jnp.bfloat16)
    left_ref[0:near, :] = first
    left_ref[NEAR : NEAR + near, :] = get_rows(coarse_ref, 1, near, 24).astype(jnp.bfloat16)
    left_ref[2 * NEAR : 2 * NEAR + fine, :] = get_rows(fine_ref, 0, fine, FINE_COLS).astype(jnp.bfloat16)
    right_far_ref[0:near, :] = last
    left_far_ref[0:near, :] = first


def columns_kernel(
    place_ref, row_ref, col_ref, token_ref, one_ref, two_ref, from_left_ref, from_right_ref, from_left_far_ref, from_right_far_ref,
    mine_ref, other_ref, prior_ref, fine_out_ref, down_ref, up_ref, down_far_ref, up_far_ref, coarse_ref, fine_ref, half_ref,
):
    core = place_ref[2]
    tall = row_ref[place_ref[0]]
    wide = col_ref[place_ref[1]]
    left_wide = size_at(col_ref, place_ref[1] - 1)
    right_wide = size_at(col_ref, place_ref[1] + 1)
    near = 3 * TILE_ROWS
    fine = 2 * FINE_ROWS
    blank = jnp.zeros((near, 384), jnp.float32)
    put_strided(coarse_ref, EXT_COLS - 2, EXT_COLS, blank)
    put_strided(coarse_ref, EXT_COLS - 1, EXT_COLS, blank)
    for f in range(3):
        for i in range(TILE_ROWS):
            row = one_ref[f, i] if f < 2 else token_ref[i]
            put_rows(coarse_ref, (f * TILE_ROWS + i) * EXT_COLS + HALO, row.astype(jnp.float32))
    left_two = jnp.where(left_wide == 1, from_left_far_ref[0:near, :], from_left_ref[NEAR : NEAR + near, :])
    right_two = jnp.where(right_wide == 1, from_right_far_ref[0:near, :], from_right_ref[NEAR : NEAR + near, :])
    put_strided(coarse_ref, 0, EXT_COLS, left_two.astype(jnp.float32))
    put_strided(coarse_ref, 1, EXT_COLS, from_left_ref[0:near, :].astype(jnp.float32))
    put_strided(coarse_ref, wide + 2, EXT_COLS, from_right_ref[0:near, :].astype(jnp.float32))
    put_strided(coarse_ref, wide + 3, EXT_COLS, right_two.astype(jnp.float32))
    for side, ref in ((core, mine_ref), (1 - core, other_ref)):
        for i in range(TILE_ROWS):
            put_rows(half_ref, i * HALF, get_rows(coarse_ref, (2 * TILE_ROWS + i) * EXT_COLS + side * HALF, HALF))
        half_ref[:, TILE_ROWS * HALF : TALL_TILE, :] = jnp.zeros((3, TALL_TILE - TILE_ROWS * HALF, 128), jnp.float32)
        ref[...] = get_rows(half_ref, 0, TALL_TILE).astype(jnp.bfloat16)
    for i in range(2 * TILE_ROWS):
        prior_ref[i] = get_rows(coarse_ref, i * EXT_COLS, EXT_COLS).astype(jnp.bfloat16)
    for c in range(FINE_COLS + 1, FINE_PITCH):
        put_strided(fine_ref, c, FINE_PITCH, jnp.zeros((fine, 384), jnp.float32))
    for f in range(2):

        def copy_fine(i, carry):
            put_rows(fine_ref, (f * FINE_ROWS + i) * FINE_PITCH + 1, two_ref[f, i].astype(jnp.float32))
            return carry

        lax.fori_loop(0, FINE_ROWS, copy_fine, 0)
    put_strided(fine_ref, 0, FINE_PITCH, from_left_ref[2 * NEAR : 2 * NEAR + fine, :].astype(jnp.float32))
    put_strided(fine_ref, 2 * wide + 1, FINE_PITCH, from_right_ref[2 * NEAR : 2 * NEAR + fine, :].astype(jnp.float32))

    def write_fine(i, carry):
        fine_out_ref[i] = get_rows(fine_ref, pl.multiple_of(i * FINE_PITCH, 8), FINE_PITCH).astype(jnp.bfloat16)
        return carry

    lax.fori_loop(0, fine, write_fine, 0)
    for f in range(2):
        base = f * TILE_ROWS
        last = prior_ref[base + tall - 1]
        down_ref[f] = last
        down_ref[2 + f] = prior_ref[base + jnp.maximum(tall - 2, 0)]
        down_far_ref[f] = last
        up_ref[f] = prior_ref[base]
        up_ref[2 + f] = prior_ref[base + 1]
        up_far_ref[f] = prior_ref[base]
        bottom = fine_out_ref[f * FINE_ROWS + 2 * tall - 1]
        top = fine_out_ref[f * FINE_ROWS]
        for h in range(2):
            down_ref[4 + 2 * f + h] = bottom[h * 24 : (h + 1) * 24]
            up_ref[4 + 2 * f + h] = top[h * 24 : (h + 1) * 24]


def prior_coarse_kernel(
    place_ref, row_ref, prior_ref, from_up_ref, from_down_ref, from_up_far_ref, from_down_far_ref, one_ref, two_ref,
    sum_one_ref, phase_ref, coarse_ref, part_ref, weight_one_ref, weight_two_ref, sem_ref,
):
    fetch_one = pltpu.make_async_copy(one_ref.at[pl.ds(0, 2)], weight_one_ref, sem_ref.at[0])
    fetch_two = pltpu.make_async_copy(two_ref.at[pl.ds(2, 1)], weight_two_ref, sem_ref.at[1])
    fetch_two.start()
    fetch_one.start()
    tall = row_ref[place_ref[0]]
    up_tall = size_at(row_ref, place_ref[0] - 1)
    down_tall = size_at(row_ref, place_ref[0] + 1)
    for f in range(2):
        coarse_ref[f, 0] = jnp.where(up_tall == 1, from_up_far_ref[f], from_up_ref[2 + f])
        coarse_ref[f, 1] = from_up_ref[f]
        for i in range(TILE_ROWS):
            coarse_ref[f, HALO + i] = prior_ref[f * TILE_ROWS + i]
        for i in (TILE_ROWS + 2, TILE_ROWS + 3):
            coarse_ref[f, i] = jnp.zeros((EXT_COLS, 384), jnp.bfloat16)
        coarse_ref[f, tall + 2] = from_down_ref[f]
        coarse_ref[f, tall + 3] = jnp.where(down_tall == 1, from_down_far_ref[f], from_down_ref[2 + f])
    fetch_two.wait()
    taps = ((0,), (1, 2), (0, 1), (2,))
    for u in range(4):
        rows = [sum(weight_two_ref[0, a, b].astype(jnp.float32) for a in taps[u]) for b in range(3)]
        for v in range(4):
            phase_ref[u, v] = sum(rows[b] for b in taps[v]).astype(jnp.bfloat16)
    fetch_one.wait()
    sum_one_ref[...] = coarse_conv(lambda f, a, n: coarse_ref[f, a : a + n], weight_one_ref, part_ref, 2)


def prior_fine_kernel(
    place_ref, row_ref, fine_ref, from_up_ref, from_down_ref, two_ref, sum_two_ref, wide_ref, part_ref, weight_two_ref, sem_ref
):
    fetch_two = pltpu.make_async_copy(two_ref.at[pl.ds(0, 2)], weight_two_ref, sem_ref.at[0])
    fetch_two.start()
    tall = row_ref[place_ref[0]]
    for f in range(2):
        wide_ref[f, 0] = jnp.concatenate([from_up_ref[4 + 2 * f], from_up_ref[5 + 2 * f]], axis=0)

        def copy_fine(i, carry):
            wide_ref[f, 1 + i] = fine_ref[f * FINE_ROWS + i]
            return carry

        lax.fori_loop(0, FINE_ROWS, copy_fine, 0)
        wide_ref[f, FINE_ROWS + 1] = jnp.zeros((FINE_PITCH, 384), jnp.bfloat16)
        wide_ref[f, 2 * tall + 1] = jnp.concatenate([from_down_ref[4 + 2 * f], from_down_ref[5 + 2 * f]], axis=0)
    fetch_two.wait()
    for r in range(0, FINE_ROWS, FINE_STEP):
        sum_two_ref[r * FINE_PITCH : (r + FINE_STEP) * FINE_PITCH, :] = fine_conv(
            lambda f, a, n: wide_ref[f, r + a : r + a + n], weight_two_ref, part_ref, 2
        )


def coarse_conv(rows_of, weight_ref, part_ref, depth):
    rows = TILE_ROWS + 2
    taps = [(f, a) for f in range(depth) for a in range(3)]
    left = jnp.concatenate([rows_of(f, a, rows).reshape(rows * EXT_COLS, 384) for f, a in taps], axis=1)
    right = jnp.concatenate([jnp.concatenate([weight_ref[f, a, b] for b in range(3)], axis=1) for f, a in taps], axis=0)
    product = jnp.dot(left, right, preferred_element_type=jnp.float32)
    return shifted_sum([product[:, b * 384 : (b + 1) * 384] for b in range(3)], part_ref)


def fine_conv(rows_of, weight_ref, part_ref, depth):
    taps = [(f, a) for f in range(depth) for a in range(3)]
    left = jnp.concatenate([rows_of(f, a, FINE_STEP).reshape(FINE_STEP * FINE_PITCH, 384) for f, a in taps], axis=1)
    products = [
        lax.dot_general(
            left, jnp.concatenate([weight_ref[f, a, b] for f, a in taps], axis=1), (((1,), (1,)), ((), ())),
            preferred_element_type=jnp.float32,
        )
        for b in range(3)
    ]
    return shifted_sum(products, part_ref)


def shifted_sum(products, part_ref):
    total = products[0]
    count, width = total.shape
    groups = -(-width // 128)
    for b in (1, 2):
        for g in range(groups):
            hi = min((g + 1) * 128, width)
            part_ref[g, 0:count, 0 : hi - g * 128] = products[b][:, g * 128 : hi]
        moved = jnp.concatenate([part_ref[g, b : b + count, :] for g in range(groups)], axis=1)
        total = total + moved[:, 0:width]
    return total


def query_kernel(
    place_ref, row_ref, own_ref, one_ref, two_ref, three_ref, gain_ref, qw_ref, kw_ref, query_ref, frame_ref, frame_other_ref, wide_ref, *, scale
):
    y_at = place_ref[0] // 2
    wide_ref[...] = jnp.zeros_like(wide_ref)
    slot = lax.broadcasted_iota(jnp.int32, (TALL_TILE, 128), 0)
    for k, ref in enumerate((own_ref, one_ref, two_ref, three_ref)):
        source = jnp.bitwise_and(y_at - k, 3)
        for t in range(2):
            start = FRONT + before(row_ref, 2 * source + t) * HALF
            usable = slot < row_ref[2 * source + t] * HALF
            part = ref[t].astype(jnp.float32)
            for g in range(3):
                held = wide_ref[g, pl.ds(start, TALL_TILE), :]
                wide_ref[g, pl.ds(start, TALL_TILE), :] = jnp.where(usable, part[:, g * 128 : (g + 1) * 128], held)
    count = LAT_ROWS * HALF
    frame_ref[...] = get_rows(wide_ref, before(row_ref, place_ref[0]) * HALF, HALF_ROWS).astype(jnp.bfloat16)
    sibling = place_ref[0] + 1 - 2 * place_ref[2]
    frame_other_ref[...] = get_rows(wide_ref, before(row_ref, sibling) * HALF, HALF_ROWS).astype(jnp.bfloat16)
    step = count // 3
    for i in range(3):
        raw = get_rows(wide_ref, FRONT + i * step, step)
        normed = rms_scale(raw, gain_ref[...][None]).astype(jnp.bfloat16)
        query = jnp.dot(normed, qw_ref[...], preferred_element_type=jnp.float32).astype(jnp.bfloat16)
        turned = lax.dot_general(query, kw_ref[...], (((1,), (1,)), ((), ())), preferred_element_type=jnp.float32)
        query_ref[i * step : (i + 1) * step, :] = (turned * scale).astype(jnp.bfloat16)


def attention_kernel(
    place_ref, row_ref, col_ref, query_ref, tile_ref, out_ref,
    stage_ref, key_ref, bias_ref, score_ref, top_ref, sum_ref, acc_ref, wide_ref, stat_ref, offset_ref, sem_ref,
):
    tiles = tile_ref.shape[0]
    group = tiles // KEY_GROUPS
    fetches = [
        pltpu.make_async_copy(tile_ref.at[pl.ds(n * group, group)], stage_ref.at[pl.ds(n * group, group)], sem_ref.at[n])
        for n in range(KEY_GROUPS)
    ]
    fetches[0].start()
    cols = col_ref.shape[0]
    y_at = place_ref[0] // 2
    spot = lax.broadcasted_iota(jnp.int32, (8, KEY_CHUNK), 0) * KEY_CHUNK + lax.broadcasted_iota(jnp.int32, (8, KEY_CHUNK), 1)

    def locate(t, carry):
        offset, bias = carry
        offset_ref[t] = offset
        count = row_ref[2 * y_at + t // cols] * col_ref[t % cols]
        bias = jnp.where((spot >= offset) & (spot < offset + count), 0.0, bias)
        return offset + (count + 15) // 16 * 16, bias

    tail, bias = lax.fori_loop(0, tiles, locate, (jnp.int32(0), jnp.full((8, KEY_CHUNK), masked_score, jnp.float32)))
    offset_ref[tiles] = tail
    for j in range(MAX_CHUNKS):
        bias_ref[j] = bias[j : j + 1, :]
    chunk_count = (tail + KEY_CHUNK - 1) // KEY_CHUNK

    def gather(t, carry):
        key_ref[pl.ds(pl.multiple_of(offset_ref[t], 16), KEY_TILE), :] = stage_ref[t]
        return carry

    total = wide_ref.shape[1]
    count = query_ref.shape[0]
    wide_ref[:, 0:FRONT, :] = jnp.zeros((3, FRONT, 128), jnp.float32)
    wide_ref[:, FRONT + count : total, :] = jnp.zeros((3, total - FRONT - count, 128), jnp.float32)
    stat_ref[0:FRONT, :] = jnp.zeros((FRONT, 128), jnp.float32)
    stat_ref[FRONT + count : total, :] = jnp.zeros((total - FRONT - count, 128), jnp.float32)
    lane_groups = KEY_CHUNK // 128

    def keys_at(j):
        return key_ref[pl.ds(pl.multiple_of(j * KEY_CHUNK, KEY_CHUNK), KEY_CHUNK), :]

    def score_step(i, j):
        slot = 0
        query = query_ref[i * QUERY_BLOCK : (i + 1) * QUERY_BLOCK, :]
        s = lax.dot_general(query, keys_at(j), (((1,), (1,)), ((), ())), preferred_element_type=jnp.float32)
        s = s + bias_ref[j]
        score_ref[slot, j] = s
        best = s[:, 0:128]
        for g in range(1, lane_groups):
            best = jnp.maximum(best, s[:, g * 128 : (g + 1) * 128])
        top_ref[slot] = jnp.maximum(top_ref[slot], best)

    def value_step(i, j):
        slot = 0
        top = top_ref[slot]
        p = jnp.exp2(score_ref[slot, j] - jnp.concatenate([top] * lane_groups, axis=1))
        part = p[:, 0:128]
        for g in range(1, lane_groups):
            part = part + p[:, g * 128 : (g + 1) * 128]
        sum_ref[...] = sum_ref[...] + part
        acc_ref[...] = acc_ref[...] + jnp.dot(p.astype(jnp.bfloat16), keys_at(j), preferred_element_type=jnp.float32)

    top_ref[0] = jnp.full((QUERY_BLOCK, 128), masked_score, jnp.float32)
    done = jnp.int32(0)
    for n in range(KEY_GROUPS):
        fetches[n].wait()
        if n + 1 < KEY_GROUPS:
            fetches[n + 1].start()
        lax.fori_loop(n * group, (n + 1) * group, gather, 0)
        if n + 1 == KEY_GROUPS:
            key_ref[pl.ds(pl.multiple_of(tail, 16), KEY_CHUNK), :] = jnp.zeros((KEY_CHUNK, key_ref.shape[1]), jnp.bfloat16)
            ready = chunk_count
        else:
            ready = offset_ref[(n + 1) * group] // KEY_CHUNK

        def score_chunk(j, carry):
            score_step(0, j)
            return carry

        lax.fori_loop(done, ready, score_chunk, 0)
        done = ready
    best = jnp.max(top_ref[0], axis=1, keepdims=True)
    top_ref[0] = jnp.broadcast_to(best, (QUERY_BLOCK, 128))
    sum_ref[...] = jnp.zeros_like(sum_ref)
    acc_ref[...] = jnp.zeros_like(acc_ref)

    def value_chunk(j, carry):
        value_step(0, j)
        return carry

    def value_pair(j, carry):
        value_step(0, 2 * j)
        value_step(0, 2 * j + 1)
        return carry

    lax.fori_loop(0, chunk_count // 2, value_pair, 0)

    @pl.when(chunk_count % 2 == 1)
    def _():
        value_step(0, chunk_count - 1)

    denominator = jnp.sum(sum_ref[...], axis=1, keepdims=True)
    put_rows(wide_ref, FRONT, acc_ref[...] / denominator)
    level = top_ref[0] + jnp.log2(jnp.broadcast_to(denominator, (QUERY_BLOCK, 128)))
    high = level.astype(jnp.bfloat16).astype(jnp.float32)
    mid = (level - high).astype(jnp.bfloat16).astype(jnp.float32)
    low = level - high - mid
    lane = lax.broadcasted_iota(jnp.int32, (QUERY_BLOCK, 128), 1)
    packed = jnp.where(lane == 0, high, jnp.where(lane == 1, mid, jnp.where(lane == 2, low, 0.0)))
    stat_ref[FRONT : FRONT + QUERY_BLOCK, :] = packed
    body = HALF_ROWS - 16
    select = (
        lax.broadcasted_iota(jnp.int32, (16, 128), 0) - STAT_ROW == lax.broadcasted_iota(jnp.int32, (16, 128), 1)
    ).astype(jnp.bfloat16)
    is_stat = lax.broadcasted_iota(jnp.int32, (16, 384), 0) >= STAT_ROW
    for b in range(out_ref.shape[0]):
        offset = before(row_ref, b) * HALF
        out_ref[b, 0:body, :] = get_rows(wide_ref, offset, body).astype(jnp.bfloat16)
        levels = stat_ref[pl.ds(offset, 384), :].astype(jnp.bfloat16)
        levels = lax.dot_general(select, levels, (((1,), (1,)), ((), ())), preferred_element_type=jnp.float32)
        last = jnp.where(is_stat, levels, get_rows(wide_ref, offset + body, 16))
        out_ref[b, body:HALF_ROWS, :] = last.astype(jnp.bfloat16)


def finish_kernel(
    place_ref, row_ref, col_ref, part_ref, mine_ref, other_ref, vw_ref, ow_ref, gain_one_ref, far_one_ref, far_two_ref, one_ref, two_ref,
    gain_two_ref, out_ref, act_ref, first_ref, shift_ref, product_ref, fine_ref, weight_one_ref, phase_ref, sum_one_ref, sum_two_ref, sem_ref,
):
    fetch_one = pltpu.make_async_copy(one_ref.at[pl.ds(2, 1)], weight_one_ref, sem_ref.at[0])
    fetch_two = pltpu.make_async_copy(two_ref, phase_ref, sem_ref.at[1])
    fetch_sum_one = pltpu.make_async_copy(far_one_ref, sum_one_ref, sem_ref.at[2])
    fetch_sum_two = pltpu.make_async_copy(far_two_ref, sum_two_ref, sem_ref.at[3])
    fetch_one.start()
    fetch_sum_one.start()
    fetch_two.start()
    fetch_sum_two.start()
    core = place_ref[2]
    tall = row_ref[place_ref[0]]
    wide = col_ref[place_ref[1]]
    groups = part_ref.shape[0]
    stat = lax.broadcasted_iota(jnp.int32, (16 * groups, 128 * groups), 0)
    owner = jnp.right_shift(lax.broadcasted_iota(jnp.int32, (16 * groups, 128 * groups), 1), 7)
    within = stat - owner * 16
    ones = ((within >= STAT_ROW) & (within < STAT_ROW + 3)).astype(jnp.bfloat16)
    stacked = jnp.concatenate([part_ref[g, HALF_ROWS - 16 : HALF_ROWS, 0:256] for g in range(groups)], axis=0)
    spread = lax.dot_general(stacked, ones, (((0,), (0,)), ((), ())), preferred_element_type=jnp.float32)
    halves = []
    for side in range(2):
        sources = range(side, part_ref.shape[0], 2)
        levels = [spread[0:HALF_ROWS, g * 128 : (g + 1) * 128] for g in sources]
        best = jnp.maximum(jnp.maximum(levels[0], levels[1]), jnp.maximum(levels[2], levels[3]))
        weights = [jnp.exp2(level - best) for level in levels]
        total = (weights[0] + weights[1]) + (weights[2] + weights[3])
        merged = None
        for weight, g in zip(weights, sources):
            share = weight / total
            term = part_ref[g, 0:HALF_ROWS, :].astype(jnp.float32) * jnp.concatenate([share] * 3, axis=1)
            merged = term if merged is None else merged + term
        halves.append(merged.astype(jnp.bfloat16))
    merged = jnp.concatenate(halves, axis=0)
    attention = jnp.dot(merged, vw_ref[...], preferred_element_type=jnp.float32).astype(jnp.bfloat16)
    projected = jnp.dot(attention, ow_ref[...], preferred_element_type=jnp.float32)
    mine = mine_ref[...].astype(jnp.float32)
    other = other_ref[...].astype(jnp.float32)
    frame = jnp.concatenate([jnp.where(core == 0, mine, other), jnp.where(core == 0, other, mine)], axis=0)
    mixed = (frame + projected).astype(jnp.bfloat16)
    put_rows(shift_ref, 0, silu(rms_scale(mixed, gain_one_ref[...][None])))
    row_start = before(row_ref, place_ref[0])
    col_start = before(col_ref, place_ref[1])
    for side in range(2):
        for i in range(EXT_ROWS):
            put_rows(act_ref, i * EXT_COLS + side * HALF, get_rows(shift_ref, side * HALF_ROWS + i * HALF, HALF))
    at_col = col_start - HALO + lax.broadcasted_iota(jnp.int32, (EXT_COLS, 384), 0)
    col_inside = (at_col >= 0) & (at_col < LAT_COLS)
    for i in range(EXT_ROWS):
        at_row = row_start - HALO + i
        inside = col_inside & (at_row >= 0) & (at_row < LAT_ROWS)
        first_ref[i] = jnp.where(inside, get_rows(act_ref, i * EXT_COLS, EXT_COLS), 0.0).astype(jnp.bfloat16)
    rows = TILE_ROWS + 2
    fetch_one.wait()
    total = coarse_conv(lambda f, a, n: first_ref[a : a + n], weight_one_ref, shift_ref, 1)
    fetch_sum_one.wait()
    y_one = (total + sum_one_ref[...]).astype(jnp.bfloat16)
    act = silu(rms_scale(y_one, gain_two_ref[...][None])).astype(jnp.bfloat16).astype(jnp.float32)
    put_rows(act_ref, 0, act)
    at_col = col_start - 1 + lax.broadcasted_iota(jnp.int32, (EXT_COLS, 384), 0)
    col_inside = (at_col >= 0) & (at_col < LAT_COLS)
    for i in range(rows):
        at_row = row_start - 1 + i
        inside = col_inside & (at_row >= 0) & (at_row < LAT_ROWS)
        first_ref[i] = jnp.where(inside, get_rows(act_ref, i * EXT_COLS, EXT_COLS), 0.0).astype(jnp.bfloat16)
    fetch_two.wait()
    count = TILE_ROWS * EXT_COLS
    for p in range(2):
        left = jnp.concatenate(
            [first_ref[p + u : p + u + TILE_ROWS].reshape(count, 384) for u in range(2)], axis=1
        )
        for q in range(2):
            for v in range(2):
                right = jnp.concatenate([phase_ref[2 * p + u, 2 * q + v] for u in range(2)], axis=1)
                product = lax.dot_general(left, right, (((1,), (1,)), ((), ())), preferred_element_type=jnp.float32)
                product_ref[2 * q + v, 0, 0:count, :] = product[:, 0:128]
                product_ref[2 * q + v, 1, 0:count, 0:64] = product[:, 128:192]
            for i in range(TILE_ROWS):
                for g in range(2):
                    near = product_ref[2 * q, g, pl.ds(i * EXT_COLS + q, EXT_COLS), :]
                    next_ = product_ref[2 * q + 1, g, pl.ds(i * EXT_COLS + q + 1, EXT_COLS), :]
                    fine_ref[g, pl.ds((2 * i + p) * FINE_PITCH + q, EXT_COLS, 2), :] = near + next_
    col = lax.broadcasted_iota(jnp.int32, (FINE_COLS, 192), 0)
    fetch_sum_two.wait()
    for r in range(FINE_ROWS):
        line = get_rows(fine_ref, r * FINE_PITCH, FINE_COLS)[:, 0:192] + sum_two_ref[r * FINE_PITCH : r * FINE_PITCH + FINE_COLS, :]
        usable = (col < 2 * wide) & (r < 2 * tall)
        out_ref[r] = jnp.where(usable, line, 0.0).astype(jnp.bfloat16)


def call(body, inputs, outs, scratch, smem_count, name, flops=0, far=(), near=(), limit=SMALL_BYTES):
    smem = pl.BlockSpec(memory_space=pltpu.SMEM)
    vmem = pl.BlockSpec(memory_space=pltpu.VMEM)
    moved = sum(math.prod(v.shape) * v.dtype.itemsize for v in list(inputs) + list(outs))
    return pl.pallas_call(
        body,
        in_specs=[
            smem if i < smem_count else pl.BlockSpec(memory_space=pl.ANY) if i in far else vmem for i in range(len(inputs))
        ],
        out_specs=[vmem] * len(outs),
        out_shape=outs,
        scratch_shapes=scratch,
        compiler_params=pltpu.CompilerParams(vmem_limit_bytes=limit),
        cost_estimate=pl.CostEstimate(flops=int(flops), transcendentals=0, bytes_accessed=int(moved)),
        name=name,
    )(*[pltpu.with_memory_space_constraint(v, pltpu.VMEM) if i in near else v for i, v in enumerate(inputs)])


def attend(place, row_sizes, col_sizes, queries, tiles):
    channels = queries.shape[1]
    scratch = lambda *dims: pltpu.VMEM(dims, jnp.float32)
    (parts,) = call(
        attention_kernel,
        [place, row_sizes, col_sizes, queries, tiles],
        [jax.ShapeDtypeStruct((8, HALF_ROWS, channels), jnp.bfloat16)],
        [
            pltpu.VMEM(tiles.shape, jnp.bfloat16), pltpu.VMEM((KEY_ROWS, channels), jnp.bfloat16),
            scratch(MAX_CHUNKS, 1, KEY_CHUNK), scratch(1, MAX_CHUNKS, QUERY_BLOCK, KEY_CHUNK),
            scratch(1, QUERY_BLOCK, 128), scratch(QUERY_BLOCK, 128), scratch(QUERY_BLOCK, channels),
            scratch(3, WIDE_ROWS, 128), scratch(WIDE_ROWS, 128), pltpu.SMEM((tiles.shape[0] + 1,), jnp.int32),
            pltpu.SemaphoreType.DMA((KEY_GROUPS,)),
        ],
        3, "attention", 4 * LAT_ROWS * HALF * channels * KEY_ROWS, (4,), (), VMEM_BYTES,
    )
    return parts


def local(
    tokens, row_sizes, col_sizes, norm_gain, query_weight, key_weight, value_weight, out_weight,
    cache_one, gain_one, conv_one, cache_two, gain_two, conv_two,
):
    channels = tokens.shape[2]
    n_row = row_sizes.shape[0]
    n_col = col_sizes.shape[0]
    n_y = lax.axis_size("y")
    core = lax.axis_index("core")
    row_at = lax.axis_index("y") * lax.axis_size("core") + core
    col_at = lax.axis_index("x") * lax.axis_size("z") + lax.axis_index("z")
    place = jnp.stack([row_at, col_at, core]).astype(jnp.int32)
    shape = lambda *dims: jax.ShapeDtypeStruct(dims, jnp.bfloat16)
    wide_shape = lambda *dims: jax.ShapeDtypeStruct(dims, jnp.float32)
    scratch = lambda *dims: pltpu.VMEM(dims, jnp.float32)
    narrow = lambda *dims: pltpu.VMEM(dims, jnp.bfloat16)
    message = 160
    place_args = [place, row_sizes, col_sizes]
    (own_keys,) = call(
        keys_kernel, [col_sizes, tokens, norm_gain], [shape(KEY_TILE, channels)], [scratch(3, 304, 128)], 1, "keys"
    )
    tiles = lax.all_gather(own_keys, ("core", "x", "z"), axis=0, tiled=False)
    to_right, to_left, to_right_far, to_left_far = call(
        edges_kernel,
        [*place_args, tokens, cache_one, cache_two],
        [shape(message, channels), shape(message, channels), shape(NEAR, channels), shape(NEAR, channels)],
        [scratch(3, (3 * TILE_ROWS + 1) * 24, 128), scratch(3, (2 * FINE_ROWS + 1) * FINE_COLS, 128)],
        3, "edges",
    )
    from_left = hop(to_right, COLS, n_col, 1)
    from_right = hop(to_left, COLS, n_col, -1)
    from_left_far, from_right_far = far_hops(jnp.any(col_sizes == 1), to_right_far, to_left_far, COLS, n_col)
    mine, other, prior, fine, down, up, down_far, up_far = call(
        columns_kernel,
        [*place_args, tokens, cache_one, cache_two, from_left, from_right, from_left_far, from_right_far],
        [
            shape(TALL_TILE, channels), shape(TALL_TILE, channels), shape(2 * TILE_ROWS, EXT_COLS, channels),
            shape(2 * FINE_ROWS, FINE_PITCH, channels), shape(8, EXT_COLS, channels), shape(8, EXT_COLS, channels),
            shape(2, EXT_COLS, channels), shape(2, EXT_COLS, channels),
        ],
        [
            scratch(3, (3 * TILE_ROWS + 1) * EXT_COLS, 128), scratch(3, (2 * FINE_ROWS + 1) * FINE_PITCH, 128),
            scratch(3, TALL_TILE, 128),
        ],
        3, "columns", 0, (), (6, 7),
    )
    swap = [(0, 1), (1, 0)]
    sibling = lax.ppermute(other, "core", swap)
    pair = jnp.where(core == 0, jnp.stack([mine, sibling]), jnp.stack([sibling, mine]))
    strips = [pair] + [lax.ppermute(pair, "y", [(i, (i + k) % n_y) for i in range(n_y)]) for k in range(1, n_y)]
    around = [hop(down, ROWS, n_row, 1), hop(up, ROWS, n_row, -1)]
    around += far_hops(jnp.any(row_sizes == 1), down_far, up_far, ROWS, n_row)
    strips, around = lax.optimization_barrier((strips, around))
    scale = math.log2(math.e) / math.sqrt(channels)

    def query_body(*refs):
        query_kernel(*refs, scale=scale)

    queries, frame, frame_other = call(
        query_body,
        [place, row_sizes, *strips, norm_gain, query_weight, key_weight],
        [shape(LAT_ROWS * HALF, channels), shape(HALF_ROWS, channels), shape(HALF_ROWS, channels)],
        [scratch(3, WIDE_ROWS, 128)],
        2, "queries", 4 * LAT_ROWS * HALF * channels * channels, (), (2, 3, 4, 5),
    )
    frame_other = lax.ppermute(frame_other, "core", swap)
    conv_two = jnp.swapaxes(conv_two, 3, 4)
    channels_out = conv_two.shape[3]
    from_up, from_down, from_up_far, from_down_far = around
    sum_one, phases = call(
        prior_coarse_kernel,
        [place, row_sizes, prior, from_up, from_down, from_up_far, from_down_far, conv_one, conv_two],
        [wide_shape((TILE_ROWS + 2) * EXT_COLS, channels), shape(4, 4, channels_out, channels)],
        [
            narrow(2, EXT_ROWS, EXT_COLS, channels), scratch(3, 640, 128), narrow(2, 3, 3, channels, channels),
            narrow(1, 3, 3, channels_out, channels), pltpu.SemaphoreType.DMA((2,)),
        ],
        2, "prior_coarse", 2 * 18 * channels * 360 * 384, (7, 8), (3, 4),
    )
    queries, sum_one, phases = lax.optimization_barrier((queries, sum_one, phases))
    parts = attend(place, row_sizes, col_sizes, queries, tiles.reshape(2 * n_col, KEY_TILE, channels))
    parts = lax.all_to_all(parts, ROWS, 0, 0)
    (sum_two,) = call(
        prior_fine_kernel,
        [place, row_sizes, fine, from_up, from_down, conv_two],
        [wide_shape(FINE_ROWS * FINE_PITCH, channels_out)],
        [
            narrow(2, FINE_ROWS + 2, FINE_PITCH, channels), scratch(3, 640, 128), narrow(2, 3, 3, channels_out, channels),
            pltpu.SemaphoreType.DMA((1,)),
        ],
        2, "prior_fine", 2 * 18 * channels * 1248 * 192, (5,), (3, 4),
    )
    (decoded,) = call(
        finish_kernel,
        [
            *place_args, parts, frame, frame_other, value_weight, out_weight, gain_one, sum_one, sum_two, conv_one, phases, gain_two,
        ],
        [shape(FINE_ROWS, FINE_COLS, channels_out)],
        [
            scratch(3, EXT_ROWS * EXT_COLS, 128), narrow(EXT_ROWS, EXT_COLS, channels),
            scratch(3, 640, 128),
            scratch(4, 2, TILE_ROWS * EXT_COLS + 8, 128), scratch(2, (FINE_ROWS + 1) * FINE_PITCH, 128),
            narrow(1, 3, 3, channels, channels), narrow(4, 4, channels_out, channels),
            scratch((TILE_ROWS + 2) * EXT_COLS, channels), scratch(FINE_ROWS * FINE_PITCH, channels_out), pltpu.SemaphoreType.DMA((4,)),
        ],
        3, "finish", 0, (9, 10, 11, 12), (3, 5),
    )
    return decoded


def solution(mesh):
    grid = Mesh(mesh.devices.reshape(4, 2, 4, 4), ("y", "core", "x", "z"))
    placed = (
        P(ROWS, COLS, None), P(), P(), P(), P(), P(), P(), P(),
        P(None, ROWS, COLS, None), P(), P(), P(None, ROWS, COLS, None), P(), P(),
    )
    return jax.shard_map(local, mesh=grid, in_specs=placed, out_specs=P(ROWS, COLS, None), check_vma=False)
```

```python
import math

import jax
import jax.numpy as jnp
from jax import lax
from jax.experimental import pallas as pl
from jax.experimental.pallas import tpu as pltpu
from jax.sharding import Mesh
from jax.sharding import PartitionSpec as P

epsilon = 1e-06
masked_score = -1e30
ROWS = ("y", "core")
COLS = ("x", "z")
LAT_ROWS = 88
LAT_COLS = 256
TILE_ROWS = 13
TILE_COLS = 20
HALO = 2
EXT_ROWS = TILE_ROWS + 2 * HALO
EXT_COLS = TILE_COLS + 2 * HALO
HALF = EXT_COLS // 2
FRONT = HALO * HALF
FINE_ROWS = 2 * TILE_ROWS
FINE_COLS = 2 * TILE_COLS
FINE_PITCH = 48
KEY_TILE = 272
KEY_CHUNK = 1024
KEY_GROUPS = 4
MAX_CHUNKS = 7
KEY_ROWS = MAX_CHUNKS * KEY_CHUNK + KEY_CHUNK
QUERY_BLOCK = 1056
HALF_ROWS = 208
STAT_ROW = EXT_ROWS * HALF - (HALF_ROWS - 16)
WIDE_ROWS = LAT_ROWS * HALF + 384
FINE_STEP = 13
TALL_TILE = 160
VMEM_BYTES = 60 * 1024 * 1024
SMALL_BYTES = VMEM_BYTES
NEAR = 48


def rms_scale(values_in, gain_vec):
    wide = values_in.astype(jnp.float32)
    return wide * lax.rsqrt(jnp.mean(wide * wide, axis=-1, keepdims=True) + epsilon) * gain_vec


def silu(v):
    return v / (1.0 + jnp.exp(-v))


def hop(value, axes, count, step):
    pairs = [(i, i + step) for i in range(count) if 0 <= i + step < count]
    return lax.ppermute(value, axes, pairs)


def far_hops(needed, ahead, back, axes, count):
    return lax.cond(
        needed,
        lambda a, b: [hop(a, axes, count, 2), hop(b, axes, count, -2)],
        lambda a, b: [a, b],
        ahead, back,
    )


def put_rows(ref, start, value):
    for g in range(ref.shape[0]):
        ref[g, pl.ds(start, value.shape[0]), :] = value[:, g * 128 : (g + 1) * 128].astype(ref.dtype)


def get_rows(ref, start, count, stride=None):
    return jnp.concatenate([ref[g, pl.ds(start, count, stride), :] for g in range(ref.shape[0])], axis=1)


def put_strided(ref, start, stride, value):
    for g in range(ref.shape[0]):
        ref[g, pl.ds(start, value.shape[0], stride), :] = value[:, g * 128 : (g + 1) * 128].astype(ref.dtype)


def before(size_ref, index):
    total = 0
    for t in range(size_ref.shape[0]):
        total = total + jnp.where(t < index, size_ref[t], 0)
    return total


def size_at(size_ref, index):
    count = size_ref.shape[0]
    inside = (index >= 0) & (index < count)
    return jnp.where(inside, size_ref[jnp.clip(index, 0, count - 1)], 0)


def keys_kernel(col_ref, token_ref, gain_ref, key_ref, pack_ref):
    wide = col_ref[lax.axis_index("x") * lax.axis_size("z") + lax.axis_index("z")]
    pack_ref[...] = jnp.zeros_like(pack_ref)
    gain = gain_ref[...][None]
    for i in range(TILE_ROWS):
        put_rows(pack_ref, i * wide, rms_scale(token_ref[i].astype(jnp.float32), gain))
    key_ref[...] = get_rows(pack_ref, 0, KEY_TILE).astype(jnp.bfloat16)


def edges_kernel(
    place_ref, row_ref, col_ref, token_ref, one_ref, two_ref, right_ref, left_ref, right_far_ref, left_far_ref, coarse_ref, fine_ref
):
    wide = col_ref[place_ref[1]]
    for f in range(3):
        for i in range(TILE_ROWS):
            row = one_ref[f, i] if f < 2 else token_ref[i]
            put_rows(coarse_ref, (f * TILE_ROWS + i) * 24, row.astype(jnp.float32))
    for f in range(2):

        def copy_fine(i, carry):
            put_rows(fine_ref, pl.multiple_of((f * FINE_ROWS + i) * FINE_COLS, 8), two_ref[f, i].astype(jnp.float32))
            return carry

        lax.fori_loop(0, FINE_ROWS, copy_fine, 0)
    near = 3 * TILE_ROWS
    fine = 2 * FINE_ROWS
    for ref in (right_ref, left_ref, right_far_ref, left_far_ref):
        ref[...] = jnp.zeros_like(ref)
    last = get_rows(coarse_ref, wide - 1, near, 24).astype(jnp.bfloat16)
    first = get_rows(coarse_ref, 0, near, 24).astype(jnp.bfloat16)
    right_ref[0:near, :] = last
    right_ref[NEAR : NEAR + near, :] = get_rows(coarse_ref, jnp.maximum(wide - 2, 0), near, 24).astype(jnp.bfloat16)
    right_ref[2 * NEAR : 2 * NEAR + fine, :] = get_rows(fine_ref, 2 * wide - 1, fine, FINE_COLS).astype(jnp.bfloat16)
    left_ref[0:near, :] = first
    left_ref[NEAR : NEAR + near, :] = get_rows(coarse_ref, 1, near, 24).astype(jnp.bfloat16)
    left_ref[2 * NEAR : 2 * NEAR + fine, :] = get_rows(fine_ref, 0, fine, FINE_COLS).astype(jnp.bfloat16)
    right_far_ref[0:near, :] = last
    left_far_ref[0:near, :] = first


def columns_kernel(
    place_ref, row_ref, col_ref, token_ref, one_ref, two_ref, from_left_ref, from_right_ref, from_left_far_ref, from_right_far_ref,
    mine_ref, other_ref, prior_ref, fine_out_ref, down_ref, up_ref, down_far_ref, up_far_ref, coarse_ref, fine_ref, half_ref,
):
    core = place_ref[2]
    tall = row_ref[place_ref[0]]
    wide = col_ref[place_ref[1]]
    left_wide = size_at(col_ref, place_ref[1] - 1)
    right_wide = size_at(col_ref, place_ref[1] + 1)
    near = 3 * TILE_ROWS
    fine = 2 * FINE_ROWS
    blank = jnp.zeros((near, 384), jnp.float32)
    put_strided(coarse_ref, EXT_COLS - 2, EXT_COLS, blank)
    put_strided(coarse_ref, EXT_COLS - 1, EXT_COLS, blank)
    for f in range(3):
        for i in range(TILE_ROWS):
            row = one_ref[f, i] if f < 2 else token_ref[i]
            put_rows(coarse_ref, (f * TILE_ROWS + i) * EXT_COLS + HALO, row.astype(jnp.float32))
    left_two = jnp.where(left_wide == 1, from_left_far_ref[0:near, :], from_left_ref[NEAR : NEAR + near, :])
    right_two = jnp.where(right_wide == 1, from_right_far_ref[0:near, :], from_right_ref[NEAR : NEAR + near, :])
    put_strided(coarse_ref, 0, EXT_COLS, left_two.astype(jnp.float32))
    put_strided(coarse_ref, 1, EXT_COLS, from_left_ref[0:near, :].astype(jnp.float32))
    put_strided(coarse_ref, wide + 2, EXT_COLS, from_right_ref[0:near, :].astype(jnp.float32))
    put_strided(coarse_ref, wide + 3, EXT_COLS, right_two.astype(jnp.float32))
    for side, ref in ((core, mine_ref), (1 - core, other_ref)):
        for i in range(TILE_ROWS):
            put_rows(half_ref, i * HALF, get_rows(coarse_ref, (2 * TILE_ROWS + i) * EXT_COLS + side * HALF, HALF))
        half_ref[:, TILE_ROWS * HALF : TALL_TILE, :] = jnp.zeros((3, TALL_TILE - TILE_ROWS * HALF, 128), jnp.float32)
        ref[...] = get_rows(half_ref, 0, TALL_TILE).astype(jnp.bfloat16)
    for i in range(2 * TILE_ROWS):
        prior_ref[i] = get_rows(coarse_ref, i * EXT_COLS, EXT_COLS).astype(jnp.bfloat16)
    for c in range(FINE_COLS + 1, FINE_PITCH):
        put_strided(fine_ref, c, FINE_PITCH, jnp.zeros((fine, 384), jnp.float32))
    for f in range(2):

        def copy_fine(i, carry):
            put_rows(fine_ref, (f * FINE_ROWS + i) * FINE_PITCH + 1, two_ref[f, i].astype(jnp.float32))
            return carry

        lax.fori_loop(0, FINE_ROWS, copy_fine, 0)
    put_strided(fine_ref, 0, FINE_PITCH, from_left_ref[2 * NEAR : 2 * NEAR + fine, :].astype(jnp.float32))
    put_strided(fine_ref, 2 * wide + 1, FINE_PITCH, from_right_ref[2 * NEAR : 2 * NEAR + fine, :].astype(jnp.float32))

    def write_fine(i, carry):
        fine_out_ref[i] = get_rows(fine_ref, pl.multiple_of(i * FINE_PITCH, 8), FINE_PITCH).astype(jnp.bfloat16)
        return carry

    lax.fori_loop(0, fine, write_fine, 0)
    for f in range(2):
        base = f * TILE_ROWS
        last = prior_ref[base + tall - 1]
        down_ref[f] = last
        down_ref[2 + f] = prior_ref[base + jnp.maximum(tall - 2, 0)]
        down_far_ref[f] = last
        up_ref[f] = prior_ref[base]
        up_ref[2 + f] = prior_ref[base + 1]
        up_far_ref[f] = prior_ref[base]
        bottom = fine_out_ref[f * FINE_ROWS + 2 * tall - 1]
        top = fine_out_ref[f * FINE_ROWS]
        for h in range(2):
            down_ref[4 + 2 * f + h] = bottom[h * 24 : (h + 1) * 24]
            up_ref[4 + 2 * f + h] = top[h * 24 : (h + 1) * 24]


def prior_coarse_kernel(
    place_ref, row_ref, prior_ref, from_up_ref, from_down_ref, from_up_far_ref, from_down_far_ref, one_ref, two_ref,
    sum_one_ref, phase_ref, coarse_ref, part_ref, weight_one_ref, weight_two_ref, sem_ref,
):
    fetch_one = pltpu.make_async_copy(one_ref.at[pl.ds(0, 2)], weight_one_ref, sem_ref.at[0])
    fetch_two = pltpu.make_async_copy(two_ref.at[pl.ds(2, 1)], weight_two_ref, sem_ref.at[1])
    fetch_two.start()
    fetch_one.start()
    tall = row_ref[place_ref[0]]
    up_tall = size_at(row_ref, place_ref[0] - 1)
    down_tall = size_at(row_ref, place_ref[0] + 1)
    for f in range(2):
        coarse_ref[f, 0] = jnp.where(up_tall == 1, from_up_far_ref[f], from_up_ref[2 + f])
        coarse_ref[f, 1] = from_up_ref[f]
        for i in range(TILE_ROWS):
            coarse_ref[f, HALO + i] = prior_ref[f * TILE_ROWS + i]
        for i in (TILE_ROWS + 2, TILE_ROWS + 3):
            coarse_ref[f, i] = jnp.zeros((EXT_COLS, 384), jnp.bfloat16)
        coarse_ref[f, tall + 2] = from_down_ref[f]
        coarse_ref[f, tall + 3] = jnp.where(down_tall == 1, from_down_far_ref[f], from_down_ref[2 + f])
    fetch_two.wait()
    taps = ((0,), (1, 2), (0, 1), (2,))
    for u in range(4):
        rows = [sum(weight_two_ref[0, a, b].astype(jnp.float32) for a in taps[u]) for b in range(3)]
        for v in range(4):
            phase_ref[u, v] = sum(rows[b] for b in taps[v]).astype(jnp.bfloat16)
    fetch_one.wait()
    sum_one_ref[...] = coarse_conv(lambda f, a, n: coarse_ref[f, a : a + n], weight_one_ref, part_ref, 2)


def prior_fine_kernel(
    place_ref, row_ref, fine_ref, from_up_ref, from_down_ref, two_ref, sum_two_ref, wide_ref, part_ref, weight_two_ref, sem_ref
):
    fetch_two = pltpu.make_async_copy(two_ref.at[pl.ds(0, 2)], weight_two_ref, sem_ref.at[0])
    fetch_two.start()
    tall = row_ref[place_ref[0]]
    for f in range(2):
        wide_ref[f, 0] = jnp.concatenate([from_up_ref[4 + 2 * f], from_up_ref[5 + 2 * f]], axis=0)

        def copy_fine(i, carry):
            wide_ref[f, 1 + i] = fine_ref[f * FINE_ROWS + i]
            return carry

        lax.fori_loop(0, FINE_ROWS, copy_fine, 0)
        wide_ref[f, FINE_ROWS + 1] = jnp.zeros((FINE_PITCH, 384), jnp.bfloat16)
        wide_ref[f, 2 * tall + 1] = jnp.concatenate([from_down_ref[4 + 2 * f], from_down_ref[5 + 2 * f]], axis=0)
    fetch_two.wait()
    for r in range(0, FINE_ROWS, FINE_STEP):
        sum_two_ref[r * FINE_PITCH : (r + FINE_STEP) * FINE_PITCH, :] = fine_conv(
            lambda f, a, n: wide_ref[f, r + a : r + a + n], weight_two_ref, part_ref, 2
        )


def coarse_conv(rows_of, weight_ref, part_ref, depth):
    rows = TILE_ROWS + 2
    taps = [(f, a) for f in range(depth) for a in range(3)]
    left = jnp.concatenate([rows_of(f, a, rows).reshape(rows * EXT_COLS, 384) for f, a in taps], axis=1)
    right = jnp.concatenate([jnp.concatenate([weight_ref[f, a, b] for b in range(3)], axis=1) for f, a in taps], axis=0)
    product = jnp.dot(left, right, preferred_element_type=jnp.float32)
    return shifted_sum([product[:, b * 384 : (b + 1) * 384] for b in range(3)], part_ref)


def fine_conv(rows_of, weight_ref, part_ref, depth):
    taps = [(f, a) for f in range(depth) for a in range(3)]
    left = jnp.concatenate([rows_of(f, a, FINE_STEP).reshape(FINE_STEP * FINE_PITCH, 384) for f, a in taps], axis=1)
    products = [
        lax.dot_general(
            left, jnp.concatenate([weight_ref[f, a, b] for f, a in taps], axis=1), (((1,), (1,)), ((), ())),
            preferred_element_type=jnp.float32,
        )
        for b in range(3)
    ]
    return shifted_sum(products, part_ref)


def shifted_sum(products, part_ref):
    total = products[0]
    count, width = total.shape
    groups = -(-width // 128)
    for b in (1, 2):
        for g in range(groups):
            hi = min((g + 1) * 128, width)
            part_ref[g, 0:count, 0 : hi - g * 128] = products[b][:, g * 128 : hi]
        moved = jnp.concatenate([part_ref[g, b : b + count, :] for g in range(groups)], axis=1)
        total = total + moved[:, 0:width]
    return total


def query_kernel(
    place_ref, row_ref, own_ref, one_ref, two_ref, three_ref, gain_ref, qw_ref, kw_ref, query_ref, frame_ref, frame_other_ref, wide_ref, *, scale
):
    y_at = place_ref[0] // 2
    wide_ref[...] = jnp.zeros_like(wide_ref)
    slot = lax.broadcasted_iota(jnp.int32, (TALL_TILE, 128), 0)
    for k, ref in enumerate((own_ref, one_ref, two_ref, three_ref)):
        source = jnp.bitwise_and(y_at - k, 3)
        for t in range(2):
            start = FRONT + before(row_ref, 2 * source + t) * HALF
            usable = slot < row_ref[2 * source + t] * HALF
            part = ref[t].astype(jnp.float32)
            for g in range(3):
                held = wide_ref[g, pl.ds(start, TALL_TILE), :]
                wide_ref[g, pl.ds(start, TALL_TILE), :] = jnp.where(usable, part[:, g * 128 : (g + 1) * 128], held)
    count = LAT_ROWS * HALF
    frame_ref[...] = get_rows(wide_ref, before(row_ref, place_ref[0]) * HALF, HALF_ROWS).astype(jnp.bfloat16)
    sibling = place_ref[0] + 1 - 2 * place_ref[2]
    frame_other_ref[...] = get_rows(wide_ref, before(row_ref, sibling) * HALF, HALF_ROWS).astype(jnp.bfloat16)
    step = count // 3
    for i in range(3):
        raw = get_rows(wide_ref, FRONT + i * step, step)
        normed = rms_scale(raw, gain_ref[...][None]).astype(jnp.bfloat16)
        query = jnp.dot(normed, qw_ref[...], preferred_element_type=jnp.float32).astype(jnp.bfloat16)
        turned = lax.dot_general(query, kw_ref[...], (((1,), (1,)), ((), ())), preferred_element_type=jnp.float32)
        query_ref[i * step : (i + 1) * step, :] = (turned * scale).astype(jnp.bfloat16)


def attention_kernel(
    place_ref, row_ref, col_ref, query_ref, tile_ref, out_ref,
    stage_ref, key_ref, bias_ref, score_ref, top_ref, sum_ref, acc_ref, wide_ref, stat_ref, offset_ref, sem_ref,
):
    tiles = tile_ref.shape[0]
    group = tiles // KEY_GROUPS
    fetches = [
        pltpu.make_async_copy(tile_ref.at[pl.ds(n * group, group)], stage_ref.at[pl.ds(n * group, group)], sem_ref.at[n])
        for n in range(KEY_GROUPS)
    ]
    fetches[0].start()
    cols = col_ref.shape[0]
    y_at = place_ref[0] // 2
    spot = lax.broadcasted_iota(jnp.int32, (8, KEY_CHUNK), 0) * KEY_CHUNK + lax.broadcasted_iota(jnp.int32, (8, KEY_CHUNK), 1)

    def locate(t, carry):
        offset, bias = carry
        offset_ref[t] = offset
        count = row_ref[2 * y_at + t // cols] * col_ref[t % cols]
        bias = jnp.where((spot >= offset) & (spot < offset + count), 0.0, bias)
        return offset + (count + 15) // 16 * 16, bias

    tail, bias = lax.fori_loop(0, tiles, locate, (jnp.int32(0), jnp.full((8, KEY_CHUNK), masked_score, jnp.float32)))
    offset_ref[tiles] = tail
    for j in range(MAX_CHUNKS):
        bias_ref[j] = bias[j : j + 1, :]
    chunk_count = (tail + KEY_CHUNK - 1) // KEY_CHUNK

    def gather(t, carry):
        key_ref[pl.ds(pl.multiple_of(offset_ref[t], 16), KEY_TILE), :] = stage_ref[t]
        return carry

    total = wide_ref.shape[1]
    count = query_ref.shape[0]
    wide_ref[:, 0:FRONT, :] = jnp.zeros((3, FRONT, 128), jnp.float32)
    wide_ref[:, FRONT + count : total, :] = jnp.zeros((3, total - FRONT - count, 128), jnp.float32)
    stat_ref[0:FRONT, :] = jnp.zeros((FRONT, 128), jnp.float32)
    stat_ref[FRONT + count : total, :] = jnp.zeros((total - FRONT - count, 128), jnp.float32)
    lane_groups = KEY_CHUNK // 128

    def keys_at(j):
        return key_ref[pl.ds(pl.multiple_of(j * KEY_CHUNK, KEY_CHUNK), KEY_CHUNK), :]

    def score_step(i, j):
        slot = 0
        query = query_ref[i * QUERY_BLOCK : (i + 1) * QUERY_BLOCK, :]
        s = lax.dot_general(query, keys_at(j), (((1,), (1,)), ((), ())), preferred_element_type=jnp.float32)
        s = s + bias_ref[j]
        score_ref[slot, j] = s
        best = s[:, 0:128]
        for g in range(1, lane_groups):
            best = jnp.maximum(best, s[:, g * 128 : (g + 1) * 128])
        top_ref[slot] = jnp.maximum(top_ref[slot], best)

    def value_step(i, j):
        slot = 0
        top = top_ref[slot]
        p = jnp.exp2(score_ref[slot, j] - jnp.concatenate([top] * lane_groups, axis=1))
        part = p[:, 0:128]
        for g in range(1, lane_groups):
            part = part + p[:, g * 128 : (g + 1) * 128]
        sum_ref[...] = sum_ref[...] + part
        acc_ref[...] = acc_ref[...] + jnp.dot(p.astype(jnp.bfloat16), keys_at(j), preferred_element_type=jnp.float32)

    top_ref[0] = jnp.full((QUERY_BLOCK, 128), masked_score, jnp.float32)
    done = jnp.int32(0)
    for n in range(KEY_GROUPS):
        fetches[n].wait()
        if n + 1 < KEY_GROUPS:
            fetches[n + 1].start()
        lax.fori_loop(n * group, (n + 1) * group, gather, 0)
        if n + 1 == KEY_GROUPS:
            key_ref[pl.ds(pl.multiple_of(tail, 16), KEY_CHUNK), :] = jnp.zeros((KEY_CHUNK, key_ref.shape[1]), jnp.bfloat16)
            ready = chunk_count
        else:
            ready = offset_ref[(n + 1) * group] // KEY_CHUNK

        def score_chunk(j, carry):
            score_step(0, j)
            return carry

        lax.fori_loop(done, ready, score_chunk, 0)
        done = ready
    best = jnp.max(top_ref[0], axis=1, keepdims=True)
    top_ref[0] = jnp.broadcast_to(best, (QUERY_BLOCK, 128))
    sum_ref[...] = jnp.zeros_like(sum_ref)
    acc_ref[...] = jnp.zeros_like(acc_ref)

    def value_chunk(j, carry):
        value_step(0, j)
        return carry

    def value_pair(j, carry):
        value_step(0, 2 * j)
        value_step(0, 2 * j + 1)
        return carry

    lax.fori_loop(0, chunk_count // 2, value_pair, 0)

    @pl.when(chunk_count % 2 == 1)
    def _():
        value_step(0, chunk_count - 1)

    denominator = jnp.sum(sum_ref[...], axis=1, keepdims=True)
    put_rows(wide_ref, FRONT, acc_ref[...] / denominator)
    level = top_ref[0] + jnp.log2(jnp.broadcast_to(denominator, (QUERY_BLOCK, 128)))
    high = level.astype(jnp.bfloat16).astype(jnp.float32)
    mid = (level - high).astype(jnp.bfloat16).astype(jnp.float32)
    low = level - high - mid
    lane = lax.broadcasted_iota(jnp.int32, (QUERY_BLOCK, 128), 1)
    packed = jnp.where(lane == 0, high, jnp.where(lane == 1, mid, jnp.where(lane == 2, low, 0.0)))
    stat_ref[FRONT : FRONT + QUERY_BLOCK, :] = packed
    body = HALF_ROWS - 16
    select = (
        lax.broadcasted_iota(jnp.int32, (16, 128), 0) - STAT_ROW == lax.broadcasted_iota(jnp.int32, (16, 128), 1)
    ).astype(jnp.bfloat16)
    is_stat = lax.broadcasted_iota(jnp.int32, (16, 384), 0) >= STAT_ROW
    for b in range(out_ref.shape[0]):
        offset = before(row_ref, b) * HALF
        out_ref[b, 0:body, :] = get_rows(wide_ref, offset, body).astype(jnp.bfloat16)
        levels = stat_ref[pl.ds(offset, 384), :].astype(jnp.bfloat16)
        levels = lax.dot_general(select, levels, (((1,), (1,)), ((), ())), preferred_element_type=jnp.float32)
        last = jnp.where(is_stat, levels, get_rows(wide_ref, offset + body, 16))
        out_ref[b, body:HALF_ROWS, :] = last.astype(jnp.bfloat16)


def finish_kernel(
    place_ref, row_ref, col_ref, part_ref, mine_ref, other_ref, vw_ref, ow_ref, gain_one_ref, far_one_ref, sum_two_ref, one_ref, two_ref,
    gain_two_ref, out_ref, act_ref, first_ref, shift_ref, product_ref, fine_ref, weight_one_ref, phase_ref, sum_one_ref, sem_ref,
):
    fetch_one = pltpu.make_async_copy(one_ref.at[pl.ds(2, 1)], weight_one_ref, sem_ref.at[0])
    fetch_two = pltpu.make_async_copy(two_ref, phase_ref, sem_ref.at[1])
    fetch_sum_one = pltpu.make_async_copy(far_one_ref, sum_one_ref, sem_ref.at[2])
    fetch_one.start()
    fetch_sum_one.start()
    fetch_two.start()
    core = place_ref[2]
    tall = row_ref[place_ref[0]]
    wide = col_ref[place_ref[1]]
    groups = part_ref.shape[0]
    stat = lax.broadcasted_iota(jnp.int32, (16 * groups, 128 * groups), 0)
    owner = jnp.right_shift(lax.broadcasted_iota(jnp.int32, (16 * groups, 128 * groups), 1), 7)
    within = stat - owner * 16
    ones = ((within >= STAT_ROW) & (within < STAT_ROW + 3)).astype(jnp.bfloat16)
    stacked = jnp.concatenate([part_ref[g, HALF_ROWS - 16 : HALF_ROWS, 0:256] for g in range(groups)], axis=0)
    spread = lax.dot_general(stacked, ones, (((0,), (0,)), ((), ())), preferred_element_type=jnp.float32)
    halves = []
    for side in range(2):
        sources = range(side, part_ref.shape[0], 2)
        levels = [spread[0:HALF_ROWS, g * 128 : (g + 1) * 128] for g in sources]
        best = jnp.maximum(jnp.maximum(levels[0], levels[1]), jnp.maximum(levels[2], levels[3]))
        weights = [jnp.exp2(level - best) for level in levels]
        total = (weights[0] + weights[1]) + (weights[2] + weights[3])
        merged = None
        for weight, g in zip(weights, sources):
            share = weight / total
            term = part_ref[g, 0:HALF_ROWS, :].astype(jnp.float32) * jnp.concatenate([share] * 3, axis=1)
            merged = term if merged is None else merged + term
        halves.append(merged.astype(jnp.bfloat16))
    merged = jnp.concatenate(halves, axis=0)
    attention = jnp.dot(merged, vw_ref[...], preferred_element_type=jnp.float32).astype(jnp.bfloat16)
    projected = jnp.dot(attention, ow_ref[...], preferred_element_type=jnp.float32)
    mine = mine_ref[...].astype(jnp.float32)
    other = other_ref[...].astype(jnp.float32)
    frame = jnp.concatenate([jnp.where(core == 0, mine, other), jnp.where(core == 0, other, mine)], axis=0)
    mixed = (frame + projected).astype(jnp.bfloat16)
    put_rows(shift_ref, 0, silu(rms_scale(mixed, gain_one_ref[...][None])))
    row_start = before(row_ref, place_ref[0])
    col_start = before(col_ref, place_ref[1])
    for side in range(2):
        for i in range(EXT_ROWS):
            put_rows(act_ref, i * EXT_COLS + side * HALF, get_rows(shift_ref, side * HALF_ROWS + i * HALF, HALF))
    at_col = col_start - HALO + lax.broadcasted_iota(jnp.int32, (EXT_COLS, 384), 0)
    col_inside = (at_col >= 0) & (at_col < LAT_COLS)
    for i in range(EXT_ROWS):
        at_row = row_start - HALO + i
        inside = col_inside & (at_row >= 0) & (at_row < LAT_ROWS)
        first_ref[i] = jnp.where(inside, get_rows(act_ref, i * EXT_COLS, EXT_COLS), 0.0).astype(jnp.bfloat16)
    rows = TILE_ROWS + 2
    fetch_one.wait()
    total = coarse_conv(lambda f, a, n: first_ref[a : a + n], weight_one_ref, shift_ref, 1)
    fetch_sum_one.wait()
    y_one = (total + sum_one_ref[...]).astype(jnp.bfloat16)
    act = silu(rms_scale(y_one, gain_two_ref[...][None])).astype(jnp.bfloat16).astype(jnp.float32)
    put_rows(act_ref, 0, act)
    at_col = col_start - 1 + lax.broadcasted_iota(jnp.int32, (EXT_COLS, 384), 0)
    col_inside = (at_col >= 0) & (at_col < LAT_COLS)
    for i in range(rows):
        at_row = row_start - 1 + i
        inside = col_inside & (at_row >= 0) & (at_row < LAT_ROWS)
        first_ref[i] = jnp.where(inside, get_rows(act_ref, i * EXT_COLS, EXT_COLS), 0.0).astype(jnp.bfloat16)
    fetch_two.wait()
    count = TILE_ROWS * EXT_COLS
    for p in range(2):
        left = jnp.concatenate(
            [first_ref[p + u : p + u + TILE_ROWS].reshape(count, 384) for u in range(2)], axis=1
        )
        for q in range(2):
            for v in range(2):
                right = jnp.concatenate([phase_ref[2 * p + u, 2 * q + v] for u in range(2)], axis=1)
                product = lax.dot_general(left, right, (((1,), (1,)), ((), ())), preferred_element_type=jnp.float32)
                product_ref[2 * q + v, 0, 0:count, :] = product[:, 0:128]
                product_ref[2 * q + v, 1, 0:count, 0:64] = product[:, 128:192]
            for i in range(TILE_ROWS):
                for g in range(2):
                    near = product_ref[2 * q, g, pl.ds(i * EXT_COLS + q, EXT_COLS), :]
                    next_ = product_ref[2 * q + 1, g, pl.ds(i * EXT_COLS + q + 1, EXT_COLS), :]
                    fine_ref[g, pl.ds((2 * i + p) * FINE_PITCH + q, EXT_COLS, 2), :] = near + next_
    col = lax.broadcasted_iota(jnp.int32, (FINE_COLS, 192), 0)
    for r in range(FINE_ROWS):
        line = get_rows(fine_ref, r * FINE_PITCH, FINE_COLS)[:, 0:192] + sum_two_ref[r * FINE_PITCH : r * FINE_PITCH + FINE_COLS, :]
        usable = (col < 2 * wide) & (r < 2 * tall)
        out_ref[r] = jnp.where(usable, line, 0.0).astype(jnp.bfloat16)


def call(body, inputs, outs, scratch, smem_count, name, flops=0, far=(), near=(), limit=SMALL_BYTES):
    smem = pl.BlockSpec(memory_space=pltpu.SMEM)
    vmem = pl.BlockSpec(memory_space=pltpu.VMEM)
    moved = sum(math.prod(v.shape) * v.dtype.itemsize for v in list(inputs) + list(outs))
    return pl.pallas_call(
        body,
        in_specs=[
            smem if i < smem_count else pl.BlockSpec(memory_space=pl.ANY) if i in far else vmem for i in range(len(inputs))
        ],
        out_specs=[vmem] * len(outs),
        out_shape=outs,
        scratch_shapes=scratch,
        compiler_params=pltpu.CompilerParams(vmem_limit_bytes=limit),
        cost_estimate=pl.CostEstimate(flops=int(flops), transcendentals=0, bytes_accessed=int(moved)),
        name=name,
    )(*[pltpu.with_memory_space_constraint(v, pltpu.VMEM) if i in near else v for i, v in enumerate(inputs)])


def attend(place, row_sizes, col_sizes, queries, tiles):
    channels = queries.shape[1]
    scratch = lambda *dims: pltpu.VMEM(dims, jnp.float32)
    (parts,) = call(
        attention_kernel,
        [place, row_sizes, col_sizes, queries, tiles],
        [jax.ShapeDtypeStruct((8, HALF_ROWS, channels), jnp.bfloat16)],
        [
            pltpu.VMEM(tiles.shape, jnp.bfloat16), pltpu.VMEM((KEY_ROWS, channels), jnp.bfloat16),
            scratch(MAX_CHUNKS, 1, KEY_CHUNK), scratch(1, MAX_CHUNKS, QUERY_BLOCK, KEY_CHUNK),
            scratch(1, QUERY_BLOCK, 128), scratch(QUERY_BLOCK, 128), scratch(QUERY_BLOCK, channels),
            scratch(3, WIDE_ROWS, 128), scratch(WIDE_ROWS, 128), pltpu.SMEM((tiles.shape[0] + 1,), jnp.int32),
            pltpu.SemaphoreType.DMA((KEY_GROUPS,)),
        ],
        3, "attention", 4 * LAT_ROWS * HALF * channels * KEY_ROWS, (4,), (), VMEM_BYTES,
    )
    return parts


def local(
    tokens, row_sizes, col_sizes, norm_gain, query_weight, key_weight, value_weight, out_weight,
    cache_one, gain_one, conv_one, cache_two, gain_two, conv_two,
):
    channels = tokens.shape[2]
    n_row = row_sizes.shape[0]
    n_col = col_sizes.shape[0]
    n_y = lax.axis_size("y")
    core = lax.axis_index("core")
    row_at = lax.axis_index("y") * lax.axis_size("core") + core
    col_at = lax.axis_index("x") * lax.axis_size("z") + lax.axis_index("z")
    place = jnp.stack([row_at, col_at, core]).astype(jnp.int32)
    shape = lambda *dims: jax.ShapeDtypeStruct(dims, jnp.bfloat16)
    wide_shape = lambda *dims: jax.ShapeDtypeStruct(dims, jnp.float32)
    scratch = lambda *dims: pltpu.VMEM(dims, jnp.float32)
    narrow = lambda *dims: pltpu.VMEM(dims, jnp.bfloat16)
    message = 160
    place_args = [place, row_sizes, col_sizes]
    (own_keys,) = call(
        keys_kernel, [col_sizes, tokens, norm_gain], [shape(KEY_TILE, channels)], [scratch(3, 304, 128)], 1, "keys"
    )
    tiles = lax.all_gather(own_keys, ("core", "x", "z"), axis=0, tiled=False)
    to_right, to_left, to_right_far, to_left_far = call(
        edges_kernel,
        [*place_args, tokens, cache_one, cache_two],
        [shape(message, channels), shape(message, channels), shape(NEAR, channels), shape(NEAR, channels)],
        [scratch(3, (3 * TILE_ROWS + 1) * 24, 128), scratch(3, (2 * FINE_ROWS + 1) * FINE_COLS, 128)],
        3, "edges",
    )
    from_left = hop(to_right, COLS, n_col, 1)
    from_right = hop(to_left, COLS, n_col, -1)
    from_left_far, from_right_far = far_hops(jnp.any(col_sizes == 1), to_right_far, to_left_far, COLS, n_col)
    mine, other, prior, fine, down, up, down_far, up_far = call(
        columns_kernel,
        [*place_args, tokens, cache_one, cache_two, from_left, from_right, from_left_far, from_right_far],
        [
            shape(TALL_TILE, channels), shape(TALL_TILE, channels), shape(2 * TILE_ROWS, EXT_COLS, channels),
            shape(2 * FINE_ROWS, FINE_PITCH, channels), shape(8, EXT_COLS, channels), shape(8, EXT_COLS, channels),
            shape(2, EXT_COLS, channels), shape(2, EXT_COLS, channels),
        ],
        [
            scratch(3, (3 * TILE_ROWS + 1) * EXT_COLS, 128), scratch(3, (2 * FINE_ROWS + 1) * FINE_PITCH, 128),
            scratch(3, TALL_TILE, 128),
        ],
        3, "columns", 0, (), (6, 7),
    )
    swap = [(0, 1), (1, 0)]
    sibling = lax.ppermute(other, "core", swap)
    pair = jnp.where(core == 0, jnp.stack([mine, sibling]), jnp.stack([sibling, mine]))
    strips = [pair] + [lax.ppermute(pair, "y", [(i, (i + k) % n_y) for i in range(n_y)]) for k in range(1, n_y)]
    around = [hop(down, ROWS, n_row, 1), hop(up, ROWS, n_row, -1)]
    around += far_hops(jnp.any(row_sizes == 1), down_far, up_far, ROWS, n_row)
    strips, around = lax.optimization_barrier((strips, around))
    scale = math.log2(math.e) / math.sqrt(channels)

    def query_body(*refs):
        query_kernel(*refs, scale=scale)

    queries, frame, frame_other = call(
        query_body,
        [place, row_sizes, *strips, norm_gain, query_weight, key_weight],
        [shape(LAT_ROWS * HALF, channels), shape(HALF_ROWS, channels), shape(HALF_ROWS, channels)],
        [scratch(3, WIDE_ROWS, 128)],
        2, "queries", 4 * LAT_ROWS * HALF * channels * channels, (), (2, 3, 4, 5),
    )
    frame_other = lax.ppermute(frame_other, "core", swap)
    conv_two = jnp.swapaxes(conv_two, 3, 4)
    channels_out = conv_two.shape[3]
    from_up, from_down, from_up_far, from_down_far = around
    sum_one, phases = call(
        prior_coarse_kernel,
        [place, row_sizes, prior, from_up, from_down, from_up_far, from_down_far, conv_one, conv_two],
        [wide_shape((TILE_ROWS + 2) * EXT_COLS, channels), shape(4, 4, channels_out, channels)],
        [
            narrow(2, EXT_ROWS, EXT_COLS, channels), scratch(3, 640, 128), narrow(2, 3, 3, channels, channels),
            narrow(1, 3, 3, channels_out, channels), pltpu.SemaphoreType.DMA((2,)),
        ],
        2, "prior_coarse", 2 * 18 * channels * 360 * 384, (7, 8), (3, 4),
    )
    queries, sum_one, phases = lax.optimization_barrier((queries, sum_one, phases))
    parts = attend(place, row_sizes, col_sizes, queries, tiles.reshape(2 * n_col, KEY_TILE, channels))
    parts = lax.all_to_all(parts, ROWS, 0, 0)
    (sum_two,) = call(
        prior_fine_kernel,
        [place, row_sizes, fine, from_up, from_down, conv_two],
        [wide_shape(FINE_ROWS * FINE_PITCH, channels_out)],
        [
            narrow(2, FINE_ROWS + 2, FINE_PITCH, channels), scratch(3, 640, 128), narrow(2, 3, 3, channels_out, channels),
            pltpu.SemaphoreType.DMA((1,)),
        ],
        2, "prior_fine", 2 * 18 * channels * 1248 * 192, (5,), (3, 4),
    )
    (decoded,) = call(
        finish_kernel,
        [
            *place_args, parts, frame, frame_other, value_weight, out_weight, gain_one, sum_one, sum_two, conv_one, phases, gain_two,
        ],
        [shape(FINE_ROWS, FINE_COLS, channels_out)],
        [
            scratch(3, EXT_ROWS * EXT_COLS, 128), narrow(EXT_ROWS, EXT_COLS, channels),
            scratch(3, 640, 128),
            scratch(4, 2, TILE_ROWS * EXT_COLS + 8, 128), scratch(2, (FINE_ROWS + 1) * FINE_PITCH, 128),
            narrow(1, 3, 3, channels, channels), narrow(4, 4, channels_out, channels),
            scratch((TILE_ROWS + 2) * EXT_COLS, channels), pltpu.SemaphoreType.DMA((3,)),
        ],
        3, "finish", 0, (9, 11, 12), (3, 5, 10),
    )
    return decoded


def solution(mesh):
    grid = Mesh(mesh.devices.reshape(4, 2, 4, 4), ("y", "core", "x", "z"))
    placed = (
        P(ROWS, COLS, None), P(), P(), P(), P(), P(), P(), P(),
        P(None, ROWS, COLS, None), P(), P(), P(None, ROWS, COLS, None), P(), P(),
    )
    return jax.shard_map(local, mesh=grid, in_specs=placed, out_specs=P(ROWS, COLS, None), check_vma=False)
```
